32 devices in a mesh: dp: 16 (over z, x, core), fsdp: 2 (over y).
Axes of the slice: x: 2, y: 2, z: 4, core: 2. Of those that a mesh axis runs over, the one named last changes fastest.
Arguments:
- grads: bfloat16 [16, 2, 8192, 1024], P('dp', None, 'fsdp'), may hold values from -1.1953125 to 1.1953125
- raw_proj: float32 [2, 1024, 512], P(None, 'fsdp'), may hold values from -6 to 6
- bucket_owner: int32 [2, 512], P(None, 'fsdp'), may hold values from 0 to 15, as said below
- first_moment: float32 [2, 2, 512, 16, 512], P(None, 'fsdp', 'dp'), may hold values from -0.6 to 0.6
- second_moment: float32 [2, 2, 512, 16, 512], P(None, 'fsdp', 'dp'), may hold values from 0.01 to 0.05
Outputs:
- weight_delta: bfloat16 [2, 8192, 1024], P(None, 'fsdp')
- first_out: float32 [2, 2, 512, 16, 512], P(None, 'fsdp', 'dp')
- second_out: float32 [2, 2, 512, 16, 512], P(None, 'fsdp', 'dp')
The draws below stay inside these ranges and needn't reach their ends.
Inputs may be any that keep to these rules, and one draw needn't show every extreme that they name: `bucket_owner`: within each matrix and each block of 256 buckets of one fsdp index, no owner holds more than 32 buckets, and one owner holds exactly 32.
All inputs are finite; a program needn't handle non-finite values.
Results may differ from the reference program's by a relative error of at most 0.0062.
Values may be sent and summed in bfloat16 or wider, within the bound.
No kernel may reach another device: no remote copies, remote signals or barrier semaphores. Data moves between devices by JAX's collectives and lax.ppermute only.
A program may use at most 128 MiB of HBM per device.

```python
import math
import jax
import jax.numpy as jnp
from jax import lax

D = 8192
KV = 1024
R = 512
MATS = 2
BROWS = 16
NB = 256
CAP = 32
SLOTS = 512
N_DP = 16
N_FSDP = 2


def owners_of_block(key):
    key_full, key_scores, key_order = jax.random.split(key, 3)
    owner_count = SLOTS // CAP
    full_owner = jax.random.randint(key_full, (), 0, owner_count)
    scores = jax.random.permutation(key_scores, SLOTS).astype(jnp.int32)
    slot_ids = jnp.arange(SLOTS, dtype=jnp.int32)
    slot_owner = slot_ids // CAP
    scores = jnp.where(slot_owner == full_owner, slot_ids % CAP - CAP, scores)
    ordered = jnp.argsort(scores, stable=True)
    chosen = ordered[:NB] // CAP
    shuffle = jax.random.permutation(key_order, NB)
    return chosen[shuffle].astype(jnp.int32)


def draw_bucket_owner(key, part):
    blocks = D // BROWS // NB
    keys = jax.random.split(jax.random.fold_in(key, 17), MATS * blocks)
    table = jax.vmap(owners_of_block)(keys)
    return table.reshape(MATS, blocks * NB).astype(jnp.int32)


def level_of(stream_key, dims, pieces, smallest, high):
    factor_of = 1.0
    for position, shards_of in pieces:
        steps = jax.random.uniform(jax.random.fold_in(jax.random.fold_in(stream_key, 6), position), (shards_of,), jnp.float32, smallest / len(pieces), high / len(pieces))
        factor_of = factor_of * jnp.repeat(jnp.exp(steps), dims[position] // shards_of).reshape((-1,) + (1,) * (len(dims) - 1 - position))
    return factor_of


def scatter_about(own_key, dims, deviation, limit, pieces=(), kind=jnp.bfloat16):
    entries = jax.random.normal(own_key, dims, jnp.float32) * deviation
    if len(pieces) > 0:
        entries = level_of(own_key, dims, pieces, -0.22, 0.18) * entries
    return jnp.clip(entries, min=-limit, max=limit).astype(kind)


def setup_inputs(seed: int = 0) -> dict:
    seeds = jax.random.split(jax.random.key(seed), 6)
    return {
        "grads": scatter_about(seeds[0], (N_DP, MATS, D, KV), 0.2, 1.1953125, ((0, 16), (2, 2))),
        "raw_proj": scatter_about(seeds[1], (MATS, KV, R), 1.0, 6.0, ((1, 2),), jnp.float32),
        "bucket_owner": draw_bucket_owner(jax.random.fold_in(seeds[5], 71), 0),
        "first_moment": scatter_about(seeds[3], (MATS, N_FSDP, SLOTS, BROWS, R), 0.1, 0.6, ((1, 2), (2, 16)), jnp.float32),
        "second_moment": jnp.clip(jnp.exp(math.log(0.05) - 1.609438 * jax.random.uniform(seeds[4], (MATS, N_FSDP, SLOTS, BROWS, R), jnp.float32) ** level_of(seeds[4], (MATS, N_FSDP, SLOTS, BROWS, R), ((1, 2), (2, 16)), -0.2, 0.2)), 0.01, 0.05),
    }


def cholesky_basis(raw_rows):
    gram = jnp.einsum('mkr,mks->mrs', raw_rows, raw_rows, precision=lax.Precision.HIGHEST)
    factor = jnp.linalg.cholesky(gram)
    basis = lax.linalg.triangular_solve(factor, raw_rows, left_side=False, lower=True, transpose_a=True)
    return basis.astype(jnp.bfloat16)

def bucket_slots(owners):
    same = owners[..., :, None] == owners[..., None, :]
    count = owners.shape[-1]
    earlier = jnp.arange(count)[None, :] < jnp.arange(count)[:, None]
    ranks = lax.optimization_barrier(jnp.sum(jnp.logical_and(same, earlier).astype(jnp.int32), axis=-1)).astype(jnp.int32)
    return (owners * CAP + ranks).astype(jnp.int32)

def adam_update(first, second, grad_rows):
    new_first = 0.9 * first + 0.1 * grad_rows
    new_second = 0.999 * second + 0.001 * grad_rows * grad_rows
    scaled = 6.0 * (new_first / (1.0 - 0.9 ** 10)) / (jnp.sqrt(new_second / (1.0 - 0.999 ** 10)) + 1e-08)
    return (new_first, new_second, scaled.astype(jnp.bfloat16))

def reference(grads, raw_proj, bucket_owner, first_moment, second_moment):
    basis = cholesky_basis(raw_proj)
    blocks = D // BROWS // NB

    def accumulate(total, replica):
        return (total + replica.astype(jnp.float32), None)
    summed, _ = lax.scan(accumulate, jnp.zeros(grads.shape[1:], jnp.float32), grads)
    projected = jnp.einsum('mdk,mkr->mdr', summed, basis.astype(jnp.float32), precision=lax.Precision.HIGHEST)
    grad_rows = projected.reshape(MATS, blocks, NB, BROWS, R)
    slots = bucket_slots(bucket_owner.reshape(MATS, blocks, NB))
    mat_index = jnp.arange(MATS)[:, None, None]
    block_index = jnp.arange(blocks)[None, :, None]
    first = first_moment[mat_index, block_index, slots]
    second = second_moment[mat_index, block_index, slots]
    new_first, new_second, update = adam_update(first, second, grad_rows)
    delta = jnp.einsum('mcnbr,mkr->mcnbk', update.astype(jnp.float32), basis.astype(jnp.float32), precision=lax.Precision.HIGHEST)
    weight_delta = delta.astype(jnp.bfloat16).reshape(MATS, D, KV)
    first_out = first_moment.at[mat_index, block_index, slots].set(new_first)
    second_out = second_moment.at[mat_index, block_index, slots].set(new_second)
    return (weight_delta, first_out, second_out)
```

```python
import functools

import jax
import jax.numpy as jnp
from jax import lax
from jax.experimental import pallas as pl
from jax.experimental.pallas import tpu as pltpu
from jax.sharding import PartitionSpec as P


PANEL = 8
BLOCK = 128
QUAD = 4
F32 = jnp.float32
BF16 = jnp.bfloat16


def dot_f32(a, b, dims):
    return lax.dot_general(
        a, b, (dims, ((), ())), precision=lax.Precision.HIGHEST, preferred_element_type=F32
    )


def dot_bf16(a, b, dims):
    return lax.dot_general(a, b, (dims, ((), ())), preferred_element_type=F32)


def eliminate_panel(block_ref, inverse_ref, scale_ref, m, start, size):
    rows = block_ref[m, pl.ds(start, PANEL), :]
    inv_rows = inverse_ref[m, pl.ds(start, PANEL), :]
    sub = lax.broadcasted_iota(jnp.int32, rows.shape, 0)
    turned = pltpu.roll(rows, size - start, 1)
    cols = [jnp.broadcast_to(turned[:, j : j + 1], rows.shape) for j in range(PANEL)]
    recip = jnp.zeros_like(rows)
    for j in range(PANEL):
        r = 1.0 / jnp.broadcast_to(cols[j][j : j + 1, :], rows.shape)
        recip = jnp.where(sub == j, r, recip)
        if j + 1 < PANEL:
            mult = jnp.where(sub > j, cols[j] * r, 0.0)
            for k in range(j + 1, PANEL):
                cols[k] = cols[k] - mult * jnp.broadcast_to(cols[k][j : j + 1, :], rows.shape)
            rows = rows - mult * jnp.broadcast_to(rows[j : j + 1, :], rows.shape)
            inv_rows = inv_rows - mult * jnp.broadcast_to(inv_rows[j : j + 1, :], rows.shape)
    inverse_ref[m, pl.ds(start, PANEL), :] = inv_rows
    scale_ref[m, pl.ds(start, PANEL), :] = recip
    return rows, inv_rows, recip


def eliminate_block(block_ref, inverse_ref, scale_ref, mats, size):
    row_id = lax.broadcasted_iota(jnp.int32, (size, size), 0)
    lane_id = lax.broadcasted_iota(jnp.int32, (size, size), 1)
    for m in range(mats):
        inverse_ref[m] = jnp.where(row_id == lane_id, 1.0, 0.0)

    def panel(p, _):
        start = pl.multiple_of(p * PANEL, PANEL)
        done = [
            eliminate_panel(block_ref, inverse_ref, scale_ref, m, start, size) for m in range(mats)
        ]
        below = row_id >= start + PANEL
        for m in range(mats):
            rows, inv_rows, recip = done[m]
            both = jnp.concatenate([rows, inv_rows], axis=1)
            change = dot_f32(rows * recip, both, ((0,), (0,)))
            block_ref[m] = block_ref[m] - jnp.where(below, change[:, :size], 0.0)
            inverse_ref[m] = inverse_ref[m] - jnp.where(below, change[:, size:], 0.0)
        return 0

    lax.fori_loop(0, size // PANEL, panel, 0)


def basis_kernel(offsets, *refs, pieces):
    own_ref = refs[0]
    piece_refs = refs[1 : 1 + pieces]
    basis_ref = refs[1 + pieces]
    raw, gram, low, inv, block, binv, scale = refs[2 + pieces :]
    mats, feats, rank = raw.shape
    n = rank // BLOCK

    def sl(i):
        return slice(i * BLOCK, (i + 1) * BLOCK)

    for i, ref in enumerate((own_ref, *piece_refs)):
        at = pl.multiple_of(offsets[i], 8)
        raw[:, pl.ds(at, ref.shape[1]), :] = ref[...]

    def grams(m, _):
        for j in range(n):
            gram[m, j * BLOCK :, sl(j)] = dot_f32(
                raw[m, :, j * BLOCK :], raw[m, :, sl(j)], ((0,), (0,))
            )
        return 0

    lax.fori_loop(0, mats, grams, 0)
    for b in range(n):
        below = (b + 1) * BLOCK
        for m in range(mats):
            block[m] = gram[m, sl(b), sl(b)]
        eliminate_block(block, binv, scale, mats, BLOCK)
        for m in range(mats):
            d_inv = binv[m] * jnp.sqrt(scale[m])
            inv[m, sl(b), sl(b)] = d_inv
            if b > 0:
                acc = dot_f32(
                    low[m, sl(b), : b * BLOCK], inv[m, : b * BLOCK, : b * BLOCK], ((1,), (0,))
                )
                inv[m, sl(b), : b * BLOCK] = -dot_f32(d_inv, acc, ((1,), (0,)))
            if b + 1 < n:
                low[m, below:, sl(b)] = dot_f32(gram[m, below:, sl(b)], d_inv, ((1,), (1,)))
                inv[m, sl(b), below:] = jnp.zeros((BLOCK, rank - below), F32)
                for j in range(b + 1, n):
                    gram[m, j * BLOCK :, sl(j)] = gram[m, j * BLOCK :, sl(j)] - dot_f32(
                        low[m, j * BLOCK :, sl(b)], low[m, sl(j), sl(b)], ((1,), (1,))
                    )

    def bases(m, _):
        for j in range(n):
            depth = (j + 1) * BLOCK
            basis_ref[m, :, sl(j)] = dot_f32(
                raw[m, :, :depth], inv[m, sl(j), :depth], ((1,), (1,))
            ).astype(BF16)
        return 0

    lax.fori_loop(0, mats, bases, 0)


def orthonormal_basis(own, pieces, offsets, feats):
    mats, _, rank = own.shape
    vmem = pl.BlockSpec(memory_space=pltpu.VMEM)
    smem = pl.BlockSpec(memory_space=pltpu.SMEM)
    return pl.pallas_call(
        functools.partial(basis_kernel, pieces=len(pieces)),
        out_shape=jax.ShapeDtypeStruct((mats, feats, rank), BF16),
        in_specs=[smem] + [vmem] * (1 + len(pieces)),
        out_specs=vmem,
        scratch_shapes=[pltpu.VMEM((mats, feats, rank), F32)]
        + [pltpu.VMEM((mats, rank, rank), F32)] * 3
        + [pltpu.VMEM((mats, BLOCK, BLOCK), F32)] * 3,
        cost_estimate=pl.CostEstimate(
            flops=90_000_000_000, bytes_accessed=6 * mats * feats * rank, transcendentals=0
        ),
        name="basis",
    )(offsets, own, *pieces)


def spread_kernel(bucket_of, first_ref, second_ref, out_ref):
    m = pl.program_id(0)
    capacity = first_ref.shape[2]

    for which, ref in enumerate((first_ref, second_ref)):
        out_ref[which] = jnp.zeros(out_ref.shape[1:], BF16)

        def place(s, _):
            bucket = bucket_of[m, s]

            @pl.when(bucket >= 0)
            def _():
                out_ref[which, 0, jnp.maximum(bucket, 0)] = ref[0, 0, s].astype(BF16)

            return 0

        lax.fori_loop(0, capacity, place, 0)


def spread_moments(first, second, bucket_of, buckets):
    mats, _, capacity, rows, rank = first.shape
    spec = pl.BlockSpec((1, 1, capacity, rows, rank), lambda m, t: (m, 0, 0, 0, 0))
    return pl.pallas_call(
        spread_kernel,
        out_shape=jax.ShapeDtypeStruct((2, mats, buckets, rows, rank), BF16),
        grid_spec=pltpu.PrefetchScalarGridSpec(
            num_scalar_prefetch=1,
            grid=(mats,),
            in_specs=[spec, spec],
            out_specs=pl.BlockSpec((2, 1, buckets, rows, rank), lambda m, t: (0, m, 0, 0, 0)),
        ),
        cost_estimate=pl.CostEstimate(
            flops=0, bytes_accessed=4 * mats * buckets * rows * rank, transcendentals=0
        ),
        name="spread",
    )(bucket_of, first, second)


def project_kernel(units, grads_ref, basis_ref, other_ref, own_ref):
    j = pl.program_id(1)
    result = dot_bf16(grads_ref[0, 0], basis_ref[0], ((1,), (0,))).astype(BF16)

    @pl.when(j < 2)
    def _():
        other_ref[0, 0] = result

    @pl.when(j >= 2)
    def _():
        own_ref[0, 0] = result


def project(grads, basis, units, unit_rows):
    _, mats, _, feats = grads.shape
    rank = basis.shape[2]
    out = jax.ShapeDtypeStruct((2, mats, unit_rows, rank), BF16)
    block = (1, 1, unit_rows, rank)
    return pl.pallas_call(
        project_kernel,
        out_shape=(out, out),
        grid_spec=pltpu.PrefetchScalarGridSpec(
            num_scalar_prefetch=1,
            grid=(mats, QUAD),
            in_specs=[
                pl.BlockSpec((1, 1, unit_rows, feats), lambda m, j, u: (0, m, u[j], 0)),
                pl.BlockSpec((1, feats, rank), lambda m, j, u: (m, 0, 0)),
            ],
            out_specs=(
                pl.BlockSpec(block, lambda m, j, u: (jnp.minimum(j, 1), m, 0, 0)),
                pl.BlockSpec(block, lambda m, j, u: (jnp.maximum(j - 2, 0), m, 0, 0)),
            ),
        ),
        cost_estimate=pl.CostEstimate(
            flops=2 * mats * QUAD * unit_rows * feats * rank,
            bytes_accessed=2 * mats * QUAD * unit_rows * (feats + rank),
            transcendentals=0,
        ),
        name="project",
    )(units, grads, basis)


def expand_kernel(units, *refs):
    parts, basis_ref, out_ref = refs[:QUAD], refs[QUAD], refs[-1]
    j = pl.program_id(1)
    for i, ref in enumerate(parts):

        @pl.when(j == i)
        def _():
            out_ref[0] = dot_bf16(ref[0], basis_ref[0], ((1,), (1,))).astype(BF16)


def expand(parts, basis, units, target, local_rows):
    mats, unit_rows, rank = parts[0].shape
    feats = basis.shape[1]
    part = pl.BlockSpec((1, unit_rows, rank), lambda m, j, u: (m, 0, 0))
    in_specs = [part] * QUAD + [pl.BlockSpec((1, feats, rank), lambda m, j, u: (m, 0, 0))]
    args = [units, *parts, basis]
    aliases = {}
    if target is not None:
        in_specs.append(pl.BlockSpec(memory_space=pl.ANY))
        aliases = {len(args): 0}
        args.append(target)
    return pl.pallas_call(
        expand_kernel,
        out_shape=jax.ShapeDtypeStruct((mats, local_rows, feats), BF16),
        grid_spec=pltpu.PrefetchScalarGridSpec(
            num_scalar_prefetch=1,
            grid=(mats, QUAD),
            in_specs=in_specs,
            out_specs=pl.BlockSpec((1, unit_rows, feats), lambda m, j, u: (m, u[j], 0)),
        ),
        input_output_aliases=aliases,
        cost_estimate=pl.CostEstimate(
            flops=2 * mats * QUAD * unit_rows * feats * rank,
            bytes_accessed=2 * mats * QUAD * unit_rows * (feats + rank),
            transcendentals=0,
        ),
        name="expand",
    )(*args)


def new_moments(first, second, grad_rows):
    new_first = 0.9 * first + 0.1 * grad_rows
    new_second = 0.999 * second + 0.001 * grad_rows * grad_rows
    return new_first, new_second


def adam_update(first, second, grad_rows):
    new_first, new_second = new_moments(first, second, grad_rows)
    scaled = (
        6.0 * (new_first / (1.0 - 0.9**10)) / (jnp.sqrt(new_second / (1.0 - 0.999**10)) + 1e-08)
    )
    return scaled.astype(BF16)


def shards(grads, raw_proj, bucket_owner, first_moment, second_moment):
    mats, local_rows = grads.shape[1], grads.shape[2]
    local_feats, rank = raw_proj.shape[1], raw_proj.shape[2]
    buckets = bucket_owner.shape[1]
    capacity = first_moment.shape[2]
    bucket_rows = local_rows // buckets
    replicas = lax.axis_size("dp")
    splits = lax.axis_size("fsdp")
    depth = replicas // QUAD
    unit_rows = local_rows // replicas
    unit_buckets = buckets // replicas
    me = lax.axis_index("dp")
    my_z, my_quad = me // QUAD, me % QUAD

    def to_core(v):
        return lax.ppermute(v, "dp", [(i, i ^ 1) for i in range(replicas)])

    def to_x(v):
        return lax.ppermute(v, "dp", [(i, i ^ 2) for i in range(replicas)])

    def to_z(v):
        return lax.ppermute(v, "dp", [(i, (i + QUAD) % replicas) for i in range(replicas)])

    quarter = local_feats // QUAD
    part = lax.dynamic_slice_in_dim(raw_proj, my_quad * quarter, quarter, 1)
    my_f = lax.axis_index("fsdp")
    pieces, offsets = [], [my_f * local_feats]
    for shift in range(1, splits):
        fetched = lax.ppermute(part, "fsdp", [(i, (i + shift) % splits) for i in range(splits)])
        across = to_x(fetched)
        base = ((my_f + splits - shift) % splits) * local_feats
        for piece, flip in ((fetched, 0), (across, 2), (to_core(fetched), 1), (to_core(across), 3)):
            pieces.append(piece)
            offsets.append(base + (my_quad ^ flip) * quarter)
    offsets = jnp.stack(offsets).astype(jnp.int32)

    same = bucket_owner[:, :, None] == bucket_owner[:, None, :]
    order = jnp.arange(buckets, dtype=jnp.int32)
    earlier = order[None, :] < order[:, None]
    ranks = jnp.sum(jnp.logical_and(same, earlier).astype(jnp.int32), axis=-1)
    local_slot = jnp.where(bucket_owner == me, ranks, -1)
    matches = local_slot[:, None, :] == jnp.arange(capacity, dtype=jnp.int32)[None, :, None]
    occupied = jnp.any(matches, axis=2)
    bucket_of = jnp.sum(jnp.where(matches, order[None, None, :], 0), axis=2)

    spread = spread_moments(
        first_moment, second_moment, jnp.where(occupied, bucket_of, -1).astype(jnp.int32), buckets
    )
    spread = spread.reshape(2 * mats, local_rows, rank)
    unit_moments = lax.psum_scatter(spread, "dp", scatter_dimension=1, tiled=True)

    basis = orthonormal_basis(raw_proj, pieces, offsets, splits * local_feats)

    held = None
    for k in range(1, depth + 1):
        group = (my_z + depth - k) % depth
        units = jnp.stack(
            [group * QUAD + (my_quad ^ flip) for flip in (3, 1, 2, 0)]
        ).astype(jnp.int32)
        other, own = project(grads, basis, units, unit_rows)
        arrived = to_core(other)
        send = (own[0].astype(F32) + arrived[0].astype(F32)).astype(BF16)
        crossed = to_x(send)
        total = own[1].astype(F32) + arrived[1].astype(F32) + crossed.astype(F32)
        if held is not None:
            total = total + to_z(held).astype(F32)
        held = total.astype(BF16)
    grad_rows = total

    def ring(unit):
        groups = []
        for k in range(depth):
            across = to_x(unit)
            groups.append((unit, across, to_core(unit), to_core(across)))
            if k + 1 < depth:
                unit = to_z(unit)
        return groups

    grad_groups = ring(held)
    update = adam_update(
        unit_moments[:mats].astype(F32), unit_moments[mats:].astype(F32), grad_rows
    )
    update_groups = ring(update)

    weight_delta = None
    for k, parts in enumerate(update_groups):
        group = (my_z + depth - k) % depth
        units = jnp.stack(
            [group * QUAD + (my_quad ^ flip) for flip in (0, 2, 1, 3)]
        ).astype(jnp.int32)
        weight_delta = expand(parts, basis, units, weight_delta, local_rows)

    stacked = jnp.stack([p for parts in grad_groups for p in parts])
    table = stacked.reshape(replicas * mats * unit_buckets, bucket_rows, rank)
    unit = bucket_of // unit_buckets
    back = (my_z + depth - unit // QUAD) % depth
    flip = (unit % QUAD) ^ my_quad
    place = back * QUAD + (flip % 2) * 2 + flip // 2
    mat_id = jnp.arange(mats, dtype=jnp.int32)[:, None]
    index = (place * mats + mat_id) * unit_buckets + bucket_of % unit_buckets
    rows = jnp.take(table, index, axis=0).astype(F32)
    first, second = first_moment[:, 0], second_moment[:, 0]
    new_first, new_second = new_moments(first, second, rows)
    keep = occupied[:, :, None, None]
    first_out = jnp.where(keep, new_first, first)[:, None]
    second_out = jnp.where(keep, new_second, second)[:, None]
    return weight_delta, first_out, second_out


def solution(mesh):
    return jax.shard_map(
        shards,
        mesh=mesh,
        in_specs=(
            P("dp", None, "fsdp", None),
            P(None, "fsdp", None),
            P(None, "fsdp"),
            P(None, "fsdp", "dp", None, None),
            P(None, "fsdp", "dp", None, None),
        ),
        out_specs=(
            P(None, "fsdp", None),
            P(None, "fsdp", "dp", None, None),
            P(None, "fsdp", "dp", None, None),
        ),
        check_vma=False,
    )
```

```python
import functools

import jax
import jax.numpy as jnp
from jax import lax
from jax.experimental import pallas as pl
from jax.experimental.pallas import tpu as pltpu
from jax.sharding import PartitionSpec as P


PANEL = 8
BLOCK = 128
WIDE = 256
QUAD = 4
F32 = jnp.float32
BF16 = jnp.bfloat16


def dot_f32(a, b, dims):
    return lax.dot_general(
        a, b, (dims, ((), ())), precision=lax.Precision.HIGHEST, preferred_element_type=F32
    )


def dot_bf16(a, b, dims):
    return lax.dot_general(a, b, (dims, ((), ())), preferred_element_type=F32)


def halves(x):
    high = x.astype(BF16)
    return high, (x - high.astype(F32)).astype(BF16)


def dot_split(a, b, dims):
    (a_high, a_low), (b_high, b_low) = halves(a), halves(b)
    return (
        dot_bf16(a_low, b_high, dims)
        + dot_bf16(a_high, b_low, dims)
        + dot_bf16(a_high, b_high, dims)
    )


def eliminate_panel(block_ref, inverse_ref, scale_ref, m, start, size):
    rows = block_ref[m, pl.ds(start, PANEL), :]
    inv_rows = inverse_ref[m, pl.ds(start, PANEL), :]
    sub = lax.broadcasted_iota(jnp.int32, rows.shape, 0)
    cols = [
        jnp.take_along_axis(
            rows, jnp.full(rows.shape, start + j, jnp.int32), axis=1, mode="promise_in_bounds"
        )
        for j in range(PANEL)
    ]
    recip = jnp.zeros_like(rows)
    for j in range(PANEL):
        r = 1.0 / jnp.broadcast_to(cols[j][j : j + 1, :], rows.shape)
        recip = jnp.where(sub == j, r, recip)
        if j + 1 < PANEL:
            mult = jnp.where(sub > j, cols[j] * r, 0.0)
            for k in range(j + 1, PANEL):
                cols[k] = cols[k] - mult * jnp.broadcast_to(cols[k][j : j + 1, :], rows.shape)
            rows = rows - mult * jnp.broadcast_to(rows[j : j + 1, :], rows.shape)
            inv_rows = inv_rows - mult * jnp.broadcast_to(inv_rows[j : j + 1, :], rows.shape)
    inverse_ref[m, pl.ds(start, PANEL), :] = inv_rows
    scale_ref[m, pl.ds(start, PANEL), :] = recip
    return rows, inv_rows, recip


def eliminate_block(block_ref, inverse_ref, scale_ref, mats, size):
    row_id = lax.broadcasted_iota(jnp.int32, (size, size), 0)
    lane_id = lax.broadcasted_iota(jnp.int32, (size, size), 1)
    for m in range(mats):
        inverse_ref[m] = jnp.where(row_id == lane_id, 1.0, 0.0)

    def panel(p, _):
        start = pl.multiple_of(p * PANEL, PANEL)
        done = [
            eliminate_panel(block_ref, inverse_ref, scale_ref, m, start, size) for m in range(mats)
        ]
        below = row_id >= start + PANEL
        for m in range(mats):
            rows, inv_rows, recip = done[m]
            both = jnp.concatenate([rows, inv_rows], axis=1)
            change = dot_f32(rows * recip, both, ((0,), (0,)))
            block_ref[m] = block_ref[m] - jnp.where(below, change[:, :size], 0.0)
            inverse_ref[m] = inverse_ref[m] - jnp.where(below, change[:, size:], 0.0)
        return 0

    lax.fori_loop(0, size // PANEL, panel, 0)


def basis_kernel(offsets, *refs, pieces):
    own_ref = refs[0]
    piece_refs = refs[1 : 1 + pieces]
    basis_ref = refs[1 + pieces]
    raw, gram, low, inv, block, binv, scale = refs[2 + pieces :]
    mats, feats, rank = raw.shape
    n = rank // BLOCK

    def sl(i):
        return slice(i * BLOCK, (i + 1) * BLOCK)

    for i, ref in enumerate((own_ref, *piece_refs)):
        at = pl.multiple_of(offsets[i], 8)
        raw[:, pl.ds(at, ref.shape[1]), :] = ref[...]

    def grams(m, _):
        for j in range(0, rank, WIDE):
            gram[m, j:, j : j + WIDE] = dot_f32(raw[m, :, j:], raw[m, :, j : j + WIDE], ((0,), (0,)))
        return 0

    lax.fori_loop(0, mats, grams, 0)
    for b in range(n):
        below = (b + 1) * BLOCK
        for m in range(mats):
            block[m] = gram[m, sl(b), sl(b)]
        eliminate_block(block, binv, scale, mats, BLOCK)
        for m in range(mats):
            d_inv = binv[m] * jnp.sqrt(scale[m])
            inv[m, sl(b), sl(b)] = d_inv
            if b > 0:
                acc = dot_f32(
                    low[m, sl(b), : b * BLOCK], inv[m, : b * BLOCK, : b * BLOCK], ((1,), (0,))
                )
                inv[m, sl(b), : b * BLOCK] = -dot_f32(d_inv, acc, ((1,), (0,)))
            if b + 1 < n:
                low[m, below:, sl(b)] = dot_f32(gram[m, below:, sl(b)], d_inv, ((1,), (1,)))
                inv[m, sl(b), below:] = jnp.zeros((BLOCK, rank - below), F32)
                for j in range(b + 1, n):
                    gram[m, j * BLOCK :, sl(j)] = gram[m, j * BLOCK :, sl(j)] - dot_f32(
                        low[m, j * BLOCK :, sl(b)], low[m, sl(j), sl(b)], ((1,), (1,))
                    )

    def bases(m, _):
        for j in range(0, rank, WIDE):
            end = j + WIDE
            basis_ref[m, :, j:end] = dot_split(
                raw[m, :, :end], inv[m, j:end, :end], ((1,), (1,))
            ).astype(BF16)
        return 0

    lax.fori_loop(0, mats, bases, 0)


def orthonormal_basis(own, pieces, offsets, feats):
    mats, _, rank = own.shape
    vmem = pl.BlockSpec(memory_space=pltpu.VMEM)
    smem = pl.BlockSpec(memory_space=pltpu.SMEM)
    return pl.pallas_call(
        functools.partial(basis_kernel, pieces=len(pieces)),
        out_shape=jax.ShapeDtypeStruct((mats, feats, rank), BF16),
        in_specs=[smem] + [vmem] * (1 + len(pieces)),
        out_specs=vmem,
        scratch_shapes=[pltpu.VMEM((mats, feats, rank), F32)]
        + [pltpu.VMEM((mats, rank, rank), F32)] * 3
        + [pltpu.VMEM((mats, BLOCK, BLOCK), F32)] * 3,
        cost_estimate=pl.CostEstimate(
            flops=90_000_000_000, bytes_accessed=6 * mats * feats * rank, transcendentals=0
        ),
        name="basis",
    )(offsets, own, *pieces)


def spread_kernel(bucket_of, first_ref, second_ref, out_ref):
    m = pl.program_id(0)
    capacity = first_ref.shape[2]

    for which, ref in enumerate((first_ref, second_ref)):
        out_ref[which] = jnp.zeros(out_ref.shape[1:], BF16)

        def place(s, _):
            bucket = bucket_of[m, s]

            @pl.when(bucket >= 0)
            def _():
                out_ref[which, 0, jnp.maximum(bucket, 0)] = ref[0, 0, s].astype(BF16)

            return 0

        lax.fori_loop(0, capacity, place, 0)


def spread_moments(first, second, bucket_of, buckets):
    mats, _, capacity, rows, rank = first.shape
    spec = pl.BlockSpec((1, 1, capacity, rows, rank), lambda m, t: (m, 0, 0, 0, 0))
    return pl.pallas_call(
        spread_kernel,
        out_shape=jax.ShapeDtypeStruct((2, mats, buckets, rows, rank), BF16),
        grid_spec=pltpu.PrefetchScalarGridSpec(
            num_scalar_prefetch=1,
            grid=(mats,),
            in_specs=[spec, spec],
            out_specs=pl.BlockSpec((2, 1, buckets, rows, rank), lambda m, t: (0, m, 0, 0, 0)),
        ),
        cost_estimate=pl.CostEstimate(
            flops=0, bytes_accessed=4 * mats * buckets * rows * rank, transcendentals=0
        ),
        name="spread",
    )(bucket_of, first, second)


def project_kernel(quads, group, grads_ref, basis_ref, other_ref, own_ref, result):
    unit_rows = other_ref.shape[2]
    result[...] = dot_bf16(grads_ref[0, 0], basis_ref[0], ((1,), (0,))).astype(BF16)
    for i, ref in ((0, other_ref), (1, other_ref), (2, own_ref), (3, own_ref)):
        at = pl.multiple_of(quads[i] * unit_rows, unit_rows)
        ref[i % 2, 0] = result[pl.ds(at, unit_rows), :]


def project(grads, basis, quads, group, unit_rows):
    _, mats, _, feats = grads.shape
    rank = basis.shape[2]
    rows = QUAD * unit_rows
    out = jax.ShapeDtypeStruct((2, mats, unit_rows, rank), BF16)
    out_spec = pl.BlockSpec((2, 1, unit_rows, rank), lambda m, q, g: (0, m, 0, 0))
    return pl.pallas_call(
        project_kernel,
        out_shape=(out, out),
        grid_spec=pltpu.PrefetchScalarGridSpec(
            num_scalar_prefetch=2,
            grid=(mats,),
            in_specs=[
                pl.BlockSpec((1, 1, rows, feats), lambda m, q, g: (0, m, g[0], 0)),
                pl.BlockSpec((1, feats, rank), lambda m, q, g: (m, 0, 0)),
            ],
            out_specs=(out_spec, out_spec),
            scratch_shapes=[pltpu.VMEM((rows, rank), BF16)],
        ),
        cost_estimate=pl.CostEstimate(
            flops=2 * mats * rows * feats * rank,
            bytes_accessed=2 * mats * rows * (feats + rank),
            transcendentals=0,
        ),
        name="project",
    )(quads, group, grads, basis)


def expand_kernel(quads, group, *refs):
    parts, basis_ref = refs[:QUAD], refs[QUAD]
    out_ref, joined = refs[-2:]
    unit_rows = parts[0].shape[1]
    for i, ref in enumerate(parts):
        at = pl.multiple_of(quads[i] * unit_rows, unit_rows)
        joined[pl.ds(at, unit_rows), :] = ref[0]
    out_ref[0] = dot_bf16(joined[...], basis_ref[0], ((1,), (1,))).astype(BF16)


def expand(parts, basis, quads, group, target, local_rows):
    mats, unit_rows, rank = parts[0].shape
    feats = basis.shape[1]
    rows = QUAD * unit_rows
    part = pl.BlockSpec((1, unit_rows, rank), lambda m, q, g: (m, 0, 0))
    in_specs = [part] * QUAD + [pl.BlockSpec((1, feats, rank), lambda m, q, g: (m, 0, 0))]
    args = [quads, group, *parts, basis]
    aliases = {}
    if target is not None:
        in_specs.append(pl.BlockSpec(memory_space=pl.ANY))
        aliases = {len(args): 0}
        args.append(target)
    return pl.pallas_call(
        expand_kernel,
        out_shape=jax.ShapeDtypeStruct((mats, local_rows, feats), BF16),
        grid_spec=pltpu.PrefetchScalarGridSpec(
            num_scalar_prefetch=2,
            grid=(mats,),
            in_specs=in_specs,
            out_specs=pl.BlockSpec((1, rows, feats), lambda m, q, g: (m, g[0], 0)),
            scratch_shapes=[pltpu.VMEM((rows, rank), BF16)],
        ),
        input_output_aliases=aliases,
        cost_estimate=pl.CostEstimate(
            flops=2 * mats * rows * feats * rank,
            bytes_accessed=2 * mats * rows * (feats + rank),
            transcendentals=0,
        ),
        name="expand",
    )(*args)


def new_moments(first, second, grad_rows):
    new_first = 0.9 * first + 0.1 * grad_rows
    new_second = 0.999 * second + 0.001 * grad_rows * grad_rows
    return new_first, new_second


def settle_kernel(piece_of, row_of, held, *refs, pieces):
    piece_refs = refs[:pieces]
    first_ref, second_ref, first_out, second_out, rows, sem = refs[pieces:]
    m = pl.program_id(0)
    capacity, bucket_rows = rows.shape[0], rows.shape[1]

    def fetch(s, _):
        piece = piece_of[m, s]
        at = pl.multiple_of(row_of[m, s], bucket_rows)
        for i, ref in enumerate(piece_refs):

            @pl.when(piece == i)
            def _():
                pltpu.make_async_copy(ref.at[m, pl.ds(at, bucket_rows), :], rows.at[s], sem).start()

        return 0

    lax.fori_loop(0, capacity, fetch, 0)
    pltpu.make_async_copy(rows, rows, sem).wait()

    def settle(s, _):
        first, second = first_ref[0, 0, s], second_ref[0, 0, s]
        new_first, new_second = new_moments(first, second, rows[s].astype(F32))
        keep = held[m, s] > 0
        first_out[0, 0, s] = jnp.where(keep, new_first, first)
        second_out[0, 0, s] = jnp.where(keep, new_second, second)
        return 0

    lax.fori_loop(0, capacity, settle, 0)


def settle_moments(first, second, pieces, piece_of, row_of, held):
    mats, _, capacity, bucket_rows, rank = first.shape
    spec = pl.BlockSpec((1, 1, capacity, bucket_rows, rank), lambda m, *_: (m, 0, 0, 0, 0))
    return pl.pallas_call(
        functools.partial(settle_kernel, pieces=len(pieces)),
        out_shape=(
            jax.ShapeDtypeStruct(first.shape, F32),
            jax.ShapeDtypeStruct(second.shape, F32),
        ),
        grid_spec=pltpu.PrefetchScalarGridSpec(
            num_scalar_prefetch=3,
            grid=(mats,),
            in_specs=[pl.BlockSpec(memory_space=pl.ANY)] * len(pieces) + [spec, spec],
            out_specs=(spec, spec),
            scratch_shapes=[
                pltpu.VMEM((capacity, bucket_rows, rank), BF16),
                pltpu.SemaphoreType.DMA,
            ],
        ),
        cost_estimate=pl.CostEstimate(
            flops=8 * first.size, bytes_accessed=18 * first.size, transcendentals=0
        ),
        name="settle",
    )(piece_of, row_of, held, *pieces, first, second)


def adam_update(first, second, grad_rows):
    new_first, new_second = new_moments(first, second, grad_rows)
    scaled = (
        6.0 * (new_first / (1.0 - 0.9**10)) / (jnp.sqrt(new_second / (1.0 - 0.999**10)) + 1e-08)
    )
    return scaled.astype(BF16)


def shards(grads, raw_proj, bucket_owner, first_moment, second_moment):
    mats, local_rows = grads.shape[1], grads.shape[2]
    local_feats, rank = raw_proj.shape[1], raw_proj.shape[2]
    buckets = bucket_owner.shape[1]
    capacity = first_moment.shape[2]
    bucket_rows = local_rows // buckets
    replicas = lax.axis_size("dp")
    splits = lax.axis_size("fsdp")
    depth = replicas // QUAD
    unit_rows = local_rows // replicas
    unit_buckets = buckets // replicas
    me = lax.axis_index("dp")
    my_z, my_quad = me // QUAD, me % QUAD

    def to_core(v):
        return lax.ppermute(v, "dp", [(i, i ^ 1) for i in range(replicas)])

    def to_x(v):
        return lax.ppermute(v, "dp", [(i, i ^ 2) for i in range(replicas)])

    def to_z(v):
        return lax.ppermute(v, "dp", [(i, (i + QUAD) % replicas) for i in range(replicas)])

    quarter = local_feats // QUAD
    part = lax.dynamic_slice_in_dim(raw_proj, my_quad * quarter, quarter, 1)
    my_f = lax.axis_index("fsdp")
    pieces, offsets = [], [my_f * local_feats]
    for shift in range(1, splits):
        fetched = lax.ppermute(part, "fsdp", [(i, (i + shift) % splits) for i in range(splits)])
        across = to_x(fetched)
        base = ((my_f + splits - shift) % splits) * local_feats
        for piece, flip in ((fetched, 0), (across, 2), (to_core(fetched), 1), (to_core(across), 3)):
            pieces.append(piece)
            offsets.append(base + (my_quad ^ flip) * quarter)
    offsets = jnp.stack(offsets).astype(jnp.int32)

    same = bucket_owner[:, :, None] == bucket_owner[:, None, :]
    order = jnp.arange(buckets, dtype=jnp.int32)
    earlier = order[None, :] < order[:, None]
    ranks = jnp.sum(jnp.logical_and(same, earlier).astype(jnp.int32), axis=-1)
    local_slot = jnp.where(bucket_owner == me, ranks, -1)
    matches = local_slot[:, None, :] == jnp.arange(capacity, dtype=jnp.int32)[None, :, None]
    occupied = jnp.any(matches, axis=2)
    bucket_of = jnp.sum(jnp.where(matches, order[None, None, :], 0), axis=2)

    spread = spread_moments(
        first_moment, second_moment, jnp.where(occupied, bucket_of, -1).astype(jnp.int32), buckets
    )
    spread = spread.reshape(2 * mats, local_rows, rank)
    unit_moments = lax.psum_scatter(spread, "dp", scatter_dimension=1, tiled=True)

    basis = orthonormal_basis(raw_proj, pieces, offsets, splits * local_feats)

    send_quads = jnp.stack([my_quad ^ flip for flip in (3, 1, 2, 0)]).astype(jnp.int32)
    held = None
    for k in range(1, depth + 1):
        group = ((my_z + depth - k) % depth).astype(jnp.int32)[None]
        other, own = project(grads, basis, send_quads, group, unit_rows)
        arrived = to_core(other)
        send = (own[0].astype(F32) + arrived[0].astype(F32)).astype(BF16)
        crossed = to_x(send)
        total = own[1].astype(F32) + arrived[1].astype(F32) + crossed.astype(F32)
        if held is not None:
            total = total + to_z(held).astype(F32)
        held = total.astype(BF16)
    grad_rows = total

    def ring(unit):
        groups = []
        for k in range(depth):
            across = to_x(unit)
            groups.append((unit, across, to_core(unit), to_core(across)))
            if k + 1 < depth:
                unit = to_z(unit)
        return groups

    grad_groups = ring(held)
    update = adam_update(
        unit_moments[:mats].astype(F32), unit_moments[mats:].astype(F32), grad_rows
    )
    update_groups = ring(update)

    part_quads = jnp.stack([my_quad ^ flip for flip in (0, 2, 1, 3)]).astype(jnp.int32)
    weight_delta = None
    for k, parts in enumerate(update_groups):
        group = ((my_z + depth - k) % depth).astype(jnp.int32)[None]
        weight_delta = expand(parts, basis, part_quads, group, weight_delta, local_rows)

    unit = bucket_of // unit_buckets
    back = (my_z + depth - unit // QUAD) % depth
    flip = (unit % QUAD) ^ my_quad
    piece_of = back * QUAD + (flip % 2) * 2 + flip // 2
    row_of = (bucket_of % unit_buckets) * bucket_rows
    first_out, second_out = settle_moments(
        first_moment,
        second_moment,
        [p for parts in grad_groups for p in parts],
        piece_of.astype(jnp.int32),
        row_of.astype(jnp.int32),
        occupied.astype(jnp.int32),
    )
    return weight_delta, first_out, second_out


def solution(mesh):
    return jax.shard_map(
        shards,
        mesh=mesh,
        in_specs=(
            P("dp", None, "fsdp", None),
            P(None, "fsdp", None),
            P(None, "fsdp"),
            P(None, "fsdp", "dp", None, None),
            P(None, "fsdp", "dp", None, None),
        ),
        out_specs=(
            P(None, "fsdp", None),
            P(None, "fsdp", "dp", None, None),
            P(None, "fsdp", "dp", None, None),
        ),
        check_vma=False,
    )
```

```python
import functools

import jax
import jax.numpy as jnp
from jax import lax
from jax.experimental import pallas as pl
from jax.experimental.pallas import tpu as pltpu
from jax.sharding import PartitionSpec as P


PANEL = 8
BLOCK = 128
WIDE = 256
QUAD = 4
F32 = jnp.float32
BF16 = jnp.bfloat16


def dot_f32(a, b, dims):
    return lax.dot_general(
        a, b, (dims, ((), ())), precision=lax.Precision.HIGHEST, preferred_element_type=F32
    )


def dot_bf16(a, b, dims):
    return lax.dot_general(a, b, (dims, ((), ())), preferred_element_type=F32)


def halves(x):
    high = x.astype(BF16)
    return high, (x - high.astype(F32)).astype(BF16)


def dot_split(a, b, dims):
    (a_high, a_low), (b_high, b_low) = halves(a), halves(b)
    return (
        dot_bf16(a_low, b_high, dims)
        + dot_bf16(a_high, b_low, dims)
        + dot_bf16(a_high, b_high, dims)
    )


def eliminate_panel(block_ref, inverse_ref, scale_ref, m, start):
    rows = block_ref[m, pl.ds(start, PANEL), :]
    inv_rows = inverse_ref[m, pl.ds(start, PANEL), :]
    sub = lax.broadcasted_iota(jnp.int32, rows.shape, 0)
    cols = [
        jnp.take_along_axis(
            rows, jnp.full(rows.shape, start + j, jnp.int32), axis=1, mode="promise_in_bounds"
        )
        for j in range(PANEL)
    ]
    recip = jnp.zeros_like(rows)
    for j in range(PANEL):
        r = 1.0 / jnp.broadcast_to(cols[j][j : j + 1, :], rows.shape)
        recip = jnp.where(sub == j, r, recip)
        if j + 1 < PANEL:
            mult = jnp.where(sub > j, cols[j] * r, 0.0)
            for k in range(j + 1, PANEL):
                cols[k] = cols[k] - mult * jnp.broadcast_to(cols[k][j : j + 1, :], rows.shape)
            rows = rows - mult * jnp.broadcast_to(rows[j : j + 1, :], rows.shape)
            inv_rows = inv_rows - mult * jnp.broadcast_to(inv_rows[j : j + 1, :], rows.shape)
    inverse_ref[m, pl.ds(start, PANEL), :] = inv_rows
    scale_ref[m, pl.ds(start, PANEL), :] = recip
    return rows, inv_rows, recip


def eliminate_block(block_ref, inverse_ref, scale_ref, mats, size):
    row_id = lax.broadcasted_iota(jnp.int32, (size, size), 0)
    lane_id = lax.broadcasted_iota(jnp.int32, (size, size), 1)
    for m in range(mats):
        inverse_ref[m] = jnp.where(row_id == lane_id, 1.0, 0.0)

    def panel(p, _):
        start = pl.multiple_of(p * PANEL, PANEL)
        done = [eliminate_panel(block_ref, inverse_ref, scale_ref, m, start) for m in range(mats)]
        below = row_id >= start + PANEL
        for m in range(mats):
            rows, inv_rows, recip = done[m]
            both = jnp.concatenate([rows, inv_rows], axis=1)
            change = dot_f32(rows * recip, both, ((0,), (0,)))
            block_ref[m] = block_ref[m] - jnp.where(below, change[:, :size], 0.0)
            inverse_ref[m] = inverse_ref[m] - jnp.where(below, change[:, size:], 0.0)
        return 0

    lax.fori_loop(0, size // PANEL, panel, 0)


def basis_kernel(offsets, *refs, pieces):
    own_ref = refs[0]
    piece_refs = refs[1 : 1 + pieces]
    basis_ref = refs[1 + pieces]
    raw, gram, low, inv, block, binv, scale = refs[2 + pieces :]
    mats, _, rank = raw.shape
    n = rank // BLOCK

    def sl(i):
        return slice(i * BLOCK, (i + 1) * BLOCK)

    for i, ref in enumerate((own_ref, *piece_refs)):
        at = pl.multiple_of(offsets[i], 8)
        raw[:, pl.ds(at, ref.shape[1]), :] = ref[...]

    def grams(m, _):
        for j in range(0, rank, WIDE):
            gram[m, j:, j : j + WIDE] = dot_f32(raw[m, :, j:], raw[m, :, j : j + WIDE], ((0,), (0,)))
        return 0

    lax.fori_loop(0, mats, grams, 0)
    for b in range(n):
        below = (b + 1) * BLOCK
        for m in range(mats):
            block[m] = gram[m, sl(b), sl(b)]
        eliminate_block(block, binv, scale, mats, BLOCK)
        for m in range(mats):
            d_inv = binv[m] * jnp.sqrt(scale[m])
            inv[m, sl(b), sl(b)] = d_inv
            if b > 0:
                acc = dot_f32(
                    low[m, sl(b), : b * BLOCK], inv[m, : b * BLOCK, : b * BLOCK], ((1,), (0,))
                )
                inv[m, sl(b), : b * BLOCK] = -dot_f32(d_inv, acc, ((1,), (0,)))
            if b + 1 < n:
                low[m, below:, sl(b)] = dot_f32(gram[m, below:, sl(b)], d_inv, ((1,), (1,)))
                inv[m, sl(b), below:] = jnp.zeros((BLOCK, rank - below), F32)
                for j in range(b + 1, n):
                    gram[m, j * BLOCK :, sl(j)] = gram[m, j * BLOCK :, sl(j)] - dot_f32(
                        low[m, j * BLOCK :, sl(b)], low[m, sl(j), sl(b)], ((1,), (1,))
                    )

    def bases(m, _):
        for j in range(0, rank, WIDE):
            end = j + WIDE
            basis_ref[m, :, j:end] = dot_split(
                raw[m, :, :end], inv[m, j:end, :end], ((1,), (1,))
            ).astype(BF16)
        return 0

    lax.fori_loop(0, mats, bases, 0)


def orthonormal_basis(own, pieces, offsets, feats):
    mats, _, rank = own.shape
    vmem = pl.BlockSpec(memory_space=pltpu.VMEM)
    smem = pl.BlockSpec(memory_space=pltpu.SMEM)
    return pl.pallas_call(
        functools.partial(basis_kernel, pieces=len(pieces)),
        out_shape=jax.ShapeDtypeStruct((mats, feats, rank), BF16),
        in_specs=[smem] + [vmem] * (1 + len(pieces)),
        out_specs=vmem,
        scratch_shapes=[pltpu.VMEM((mats, feats, rank), F32)]
        + [pltpu.VMEM((mats, rank, rank), F32)] * 3
        + [pltpu.VMEM((mats, BLOCK, BLOCK), F32)] * 3,
        cost_estimate=pl.CostEstimate(
            flops=90_000_000_000, bytes_accessed=6 * mats * feats * rank, transcendentals=0
        ),
        name="basis",
    )(offsets, own, *pieces)


def collect_kernel(places, *refs):
    m = pl.program_id(1)
    owner_refs, group_refs = refs[:QUAD], refs[QUAD:]
    capacity, bucket_rows = owner_refs[0].shape[2], owner_refs[0].shape[3]
    unit_rows = group_refs[0].shape[2]
    for ref in group_refs:
        ref[...] = jnp.zeros(ref.shape, BF16)
    for i, owner_ref in enumerate(owner_refs):

        def pick(s, _):
            place = places[i, m, s]
            at = pl.multiple_of(lax.rem(jnp.maximum(place, 0), unit_rows), bucket_rows)
            for k, ref in enumerate(group_refs):

                @pl.when(jnp.logical_and(place >= k * unit_rows, place < (k + 1) * unit_rows))
                def _():
                    ref[0, 0, pl.ds(at, bucket_rows), :] = owner_ref[0, 0, s]

            return 0

        lax.fori_loop(0, capacity, pick, 0)


def collect_moments(owners, places, depth, unit_rows):
    kinds, mats, capacity, bucket_rows, rank = owners[0].shape
    slots = pl.BlockSpec((1, 1, capacity, bucket_rows, rank), lambda a, m, p: (a, m, 0, 0, 0))
    group = pl.BlockSpec((1, 1, unit_rows, rank), lambda a, m, p: (a, m, 0, 0))
    return pl.pallas_call(
        collect_kernel,
        out_shape=(jax.ShapeDtypeStruct((kinds, mats, unit_rows, rank), BF16),) * depth,
        grid_spec=pltpu.PrefetchScalarGridSpec(
            num_scalar_prefetch=1,
            grid=(kinds, mats),
            in_specs=[slots] * QUAD,
            out_specs=(group,) * depth,
        ),
        cost_estimate=pl.CostEstimate(
            flops=0, bytes_accessed=4 * QUAD * owners[0].size, transcendentals=0
        ),
        name="collect",
    )(places, *owners)


def project_kernel(quads, group, grads_ref, basis_ref, other_ref, own_ref, result):
    unit_rows = other_ref.shape[2]
    result[...] = dot_bf16(grads_ref[0, 0], basis_ref[0], ((1,), (0,))).astype(BF16)
    for i, ref in ((0, other_ref), (1, other_ref), (2, own_ref), (3, own_ref)):
        at = pl.multiple_of(quads[i] * unit_rows, unit_rows)
        ref[i % 2, 0] = result[pl.ds(at, unit_rows), :]


def project(grads, basis, quads, group, unit_rows):
    _, mats, _, feats = grads.shape
    rank = basis.shape[2]
    rows = QUAD * unit_rows
    out = jax.ShapeDtypeStruct((2, mats, unit_rows, rank), BF16)
    out_spec = pl.BlockSpec((2, 1, unit_rows, rank), lambda m, q, g: (0, m, 0, 0))
    return pl.pallas_call(
        project_kernel,
        out_shape=(out, out),
        grid_spec=pltpu.PrefetchScalarGridSpec(
            num_scalar_prefetch=2,
            grid=(mats,),
            in_specs=[
                pl.BlockSpec((1, 1, rows, feats), lambda m, q, g: (0, m, g[0], 0)),
                pl.BlockSpec((1, feats, rank), lambda m, q, g: (m, 0, 0)),
            ],
            out_specs=(out_spec, out_spec),
            scratch_shapes=[pltpu.VMEM((rows, rank), BF16)],
        ),
        cost_estimate=pl.CostEstimate(
            flops=2 * mats * rows * feats * rank,
            bytes_accessed=2 * mats * rows * (feats + rank),
            transcendentals=0,
        ),
        name="project",
    )(quads, group, grads, basis)


def expand_kernel(quads, group, *refs):
    parts, basis_ref = refs[:QUAD], refs[QUAD]
    out_ref, joined = refs[-2:]
    unit_rows = parts[0].shape[1]
    for i, ref in enumerate(parts):
        at = pl.multiple_of(quads[i] * unit_rows, unit_rows)
        joined[pl.ds(at, unit_rows), :] = ref[0]
    out_ref[0] = dot_bf16(joined[...], basis_ref[0], ((1,), (1,))).astype(BF16)


def expand(parts, basis, quads, group, target, local_rows):
    mats, unit_rows, rank = parts[0].shape
    feats = basis.shape[1]
    rows = QUAD * unit_rows
    part = pl.BlockSpec((1, unit_rows, rank), lambda m, q, g: (m, 0, 0))
    in_specs = [part] * QUAD + [pl.BlockSpec((1, feats, rank), lambda m, q, g: (m, 0, 0))]
    args = [quads, group, *parts, basis]
    aliases = {}
    if target is not None:
        in_specs.append(pl.BlockSpec(memory_space=pl.ANY))
        aliases = {len(args): 0}
        args.append(target)
    return pl.pallas_call(
        expand_kernel,
        out_shape=jax.ShapeDtypeStruct((mats, local_rows, feats), BF16),
        grid_spec=pltpu.PrefetchScalarGridSpec(
            num_scalar_prefetch=2,
            grid=(mats,),
            in_specs=in_specs,
            out_specs=pl.BlockSpec((1, rows, feats), lambda m, q, g: (m, g[0], 0)),
            scratch_shapes=[pltpu.VMEM((rows, rank), BF16)],
        ),
        input_output_aliases=aliases,
        cost_estimate=pl.CostEstimate(
            flops=2 * mats * rows * feats * rank,
            bytes_accessed=2 * mats * rows * (feats + rank),
            transcendentals=0,
        ),
        name="expand",
    )(*args)


def new_moments(first, second, grad_rows):
    new_first = 0.9 * first + 0.1 * grad_rows
    new_second = 0.999 * second + 0.001 * grad_rows * grad_rows
    return new_first, new_second


def settle_kernel(piece_of, row_of, held, *refs, pieces):
    piece_refs = refs[:pieces]
    first_ref, second_ref, first_out, second_out, rows, sem = refs[pieces:]
    m = pl.program_id(0)
    capacity, bucket_rows = rows.shape[0], rows.shape[1]

    def fetch(s, _):
        piece = piece_of[m, s]
        at = pl.multiple_of(row_of[m, s], bucket_rows)
        for i, ref in enumerate(piece_refs):

            @pl.when(piece == i)
            def _():
                pltpu.make_async_copy(ref.at[m, pl.ds(at, bucket_rows), :], rows.at[s], sem).start()

        return 0

    lax.fori_loop(0, capacity, fetch, 0)
    pltpu.make_async_copy(rows, rows, sem).wait()

    def settle(s, _):
        first, second = first_ref[0, 0, s], second_ref[0, 0, s]
        new_first, new_second = new_moments(first, second, rows[s].astype(F32))
        keep = held[m, s] > 0
        first_out[0, 0, s] = jnp.where(keep, new_first, first)
        second_out[0, 0, s] = jnp.where(keep, new_second, second)
        return 0

    lax.fori_loop(0, capacity, settle, 0)


def settle_moments(first, second, pieces, piece_of, row_of, held):
    mats, _, capacity, bucket_rows, rank = first.shape
    spec = pl.BlockSpec((1, 1, capacity, bucket_rows, rank), lambda m, *_: (m, 0, 0, 0, 0))
    return pl.pallas_call(
        functools.partial(settle_kernel, pieces=len(pieces)),
        out_shape=(
            jax.ShapeDtypeStruct(first.shape, F32),
            jax.ShapeDtypeStruct(second.shape, F32),
        ),
        grid_spec=pltpu.PrefetchScalarGridSpec(
            num_scalar_prefetch=3,
            grid=(mats,),
            in_specs=[pl.BlockSpec(memory_space=pl.ANY)] * len(pieces) + [spec, spec],
            out_specs=(spec, spec),
            scratch_shapes=[
                pltpu.VMEM((capacity, bucket_rows, rank), BF16),
                pltpu.SemaphoreType.DMA,
            ],
        ),
        cost_estimate=pl.CostEstimate(
            flops=8 * first.size, bytes_accessed=18 * first.size, transcendentals=0
        ),
        name="settle",
    )(piece_of, row_of, held, *pieces, first, second)


def adam_update(first, second, grad_rows):
    new_first, new_second = new_moments(first, second, grad_rows)
    scaled = (
        6.0 * (new_first / (1.0 - 0.9**10)) / (jnp.sqrt(new_second / (1.0 - 0.999**10)) + 1e-08)
    )
    return scaled.astype(BF16)


def shards(grads, raw_proj, bucket_owner, first_moment, second_moment):
    local_rows = grads.shape[2]
    local_feats = raw_proj.shape[1]
    buckets = bucket_owner.shape[1]
    capacity = first_moment.shape[2]
    bucket_rows = local_rows // buckets
    replicas = lax.axis_size("dp")
    splits = lax.axis_size("fsdp")
    depth = replicas // QUAD
    unit_rows = local_rows // replicas
    unit_buckets = buckets // replicas
    me = lax.axis_index("dp")
    my_z, my_quad = me // QUAD, me % QUAD

    def permute(v, target):
        return lax.ppermute(v, "dp", [(i, target(i)) for i in range(replicas)])

    def to_core(v):
        return permute(v, lambda i: i ^ 1)

    def to_x(v):
        return permute(v, lambda i: i ^ 2)

    def to_z(v):
        return permute(v, lambda i: (i + QUAD) % replicas)

    quarter = local_feats // QUAD
    part = lax.dynamic_slice_in_dim(raw_proj, my_quad * quarter, quarter, 1)
    my_f = lax.axis_index("fsdp")
    pieces, offsets = [], [my_f * local_feats]
    for shift in range(1, splits):
        fetched = lax.ppermute(part, "fsdp", [(i, (i + shift) % splits) for i in range(splits)])
        across = to_x(fetched)
        base = ((my_f + splits - shift) % splits) * local_feats
        for piece, flip in ((fetched, 0), (across, 2), (to_core(fetched), 1), (to_core(across), 3)):
            pieces.append(piece)
            offsets.append(base + (my_quad ^ flip) * quarter)
    offsets = jnp.stack(offsets).astype(jnp.int32)

    same = bucket_owner[:, :, None] == bucket_owner[:, None, :]
    order = jnp.arange(buckets, dtype=jnp.int32)
    earlier = order[None, :] < order[:, None]
    ranks = jnp.sum(jnp.logical_and(same, earlier).astype(jnp.int32), axis=-1)
    owner_ids = jnp.stack([me ^ flip for flip in (0, 2, 1, 3)])
    local_slot = jnp.where(bucket_owner[None] == owner_ids[:, None, None], ranks[None], -1)
    slot_ids = jnp.arange(capacity, dtype=jnp.int32)
    matches = local_slot[:, :, None, :] == slot_ids[None, None, :, None]
    quad_occupied = jnp.any(matches, axis=3)
    quad_buckets = jnp.sum(jnp.where(matches, order[None, None, None, :], 0), axis=3)
    occupied, bucket_of = quad_occupied[0], quad_buckets[0]
    quad_units = quad_buckets // unit_buckets
    steps = (my_z + depth - 1 - quad_units // QUAD) % depth
    places = steps * unit_rows + (quad_buckets % unit_buckets) * bucket_rows
    wanted = jnp.logical_and(quad_occupied, quad_units % QUAD == my_quad)
    places = jnp.where(wanted, places, -1).astype(jnp.int32)

    slots = jnp.stack([first_moment[:, 0], second_moment[:, 0]]).astype(BF16)
    slots, pieces = lax.optimization_barrier((slots, pieces))
    slots_across = to_x(slots)
    slots_core = to_core(slots)

    basis = orthonormal_basis(raw_proj, pieces, offsets, splits * local_feats)

    owners = (slots, slots_across, slots_core, to_core(slots_across))
    moment_groups = collect_moments(owners, places, depth, unit_rows)
    unit_moments = moment_groups[0]
    for k in range(1, depth):
        unit_moments = to_z(unit_moments) + moment_groups[k]

    send_quads = jnp.stack([my_quad ^ flip for flip in (3, 1, 2, 0)]).astype(jnp.int32)
    held = None
    for k in range(1, depth + 1):
        group = ((my_z + depth - k) % depth).astype(jnp.int32)[None]
        other, own = project(grads, basis, send_quads, group, unit_rows)
        arrived = to_core(other)
        send = (own[0].astype(F32) + arrived[0].astype(F32)).astype(BF16)
        crossed = to_x(send)
        total = own[1].astype(F32) + arrived[1].astype(F32) + crossed.astype(F32)
        if held is not None:
            total = total + to_z(held).astype(F32)
        held = total.astype(BF16)
    held, grad_rows = lax.optimization_barrier((held, total))

    def ring(unit):
        groups = []
        for k in range(depth):
            across = to_x(unit)
            core = to_core(unit)
            groups.append((unit, across, core, to_core(across)))
            if k + 1 < depth:
                unit = to_z(unit)
        return groups

    grad_groups = ring(held)
    update = adam_update(unit_moments[0].astype(F32), unit_moments[1].astype(F32), grad_rows)
    update_groups = ring(update)

    part_quads = jnp.stack([my_quad ^ flip for flip in (0, 2, 1, 3)]).astype(jnp.int32)
    weight_delta = None
    for k, parts in enumerate(update_groups):
        group = ((my_z + depth - k) % depth).astype(jnp.int32)[None]
        weight_delta = expand(parts, basis, part_quads, group, weight_delta, local_rows)

    unit = bucket_of // unit_buckets
    back = (my_z + depth - unit // QUAD) % depth
    flip = (unit % QUAD) ^ my_quad
    piece_of = back * QUAD + (flip % 2) * 2 + flip // 2
    row_of = (bucket_of % unit_buckets) * bucket_rows
    first_out, second_out = settle_moments(
        first_moment,
        second_moment,
        [p for parts in grad_groups for p in parts],
        piece_of.astype(jnp.int32),
        row_of.astype(jnp.int32),
        occupied.astype(jnp.int32),
    )
    return weight_delta, first_out, second_out


def solution(mesh):
    return jax.shard_map(
        shards,
        mesh=mesh,
        in_specs=(
            P("dp", None, "fsdp", None),
            P(None, "fsdp", None),
            P(None, "fsdp"),
            P(None, "fsdp", "dp", None, None),
            P(None, "fsdp", "dp", None, None),
        ),
        out_specs=(
            P(None, "fsdp", None),
            P(None, "fsdp", "dp", None, None),
            P(None, "fsdp", "dp", None, None),
        ),
        check_vma=False,
    )
```

```python
import functools

import jax
import jax.numpy as jnp
from jax import lax
from jax.experimental import pallas as pl
from jax.experimental.pallas import tpu as pltpu
from jax.sharding import PartitionSpec as P


PANEL = 8
BLOCK = 128
WIDE = 256
QUAD = 4
F32 = jnp.float32
BF16 = jnp.bfloat16


def dot_f32(a, b, dims):
    return lax.dot_general(
        a, b, (dims, ((), ())), precision=lax.Precision.HIGHEST, preferred_element_type=F32
    )


def dot_bf16(a, b, dims):
    return lax.dot_general(a, b, (dims, ((), ())), preferred_element_type=F32)


def halves(x):
    high = x.astype(BF16)
    return high, (x - high.astype(F32)).astype(BF16)


def dot_split(a, b, dims):
    (a_high, a_low), (b_high, b_low) = halves(a), halves(b)
    return (
        dot_bf16(a_low, b_high, dims)
        + dot_bf16(a_high, b_low, dims)
        + dot_bf16(a_high, b_high, dims)
    )


def thirds(x):
    first = x.astype(BF16).astype(F32)
    rest = x - first
    second = rest.astype(BF16).astype(F32)
    return first, second, rest - second


def dot_packed(a, b, dims):
    a1, a2, a3 = thirds(a)
    b1, b2, b3 = thirds(b)
    (a_dim,), (b_dim,) = dims
    left = jnp.concatenate([a1, a2, a1, a3, a2, a1], axis=a_dim).astype(BF16)
    right = jnp.concatenate([b3, b2, b2, b1, b1, b1], axis=b_dim).astype(BF16)
    return dot_bf16(left, right, dims)


def eliminate_panel(block_ref, inverse_ref, scale_ref, m, start):
    rows = block_ref[m, pl.ds(start, PANEL), :]
    inv_rows = inverse_ref[m, pl.ds(start, PANEL), :]
    sub = lax.broadcasted_iota(jnp.int32, rows.shape, 0)
    cols = [
        jnp.take_along_axis(
            rows, jnp.full(rows.shape, start + j, jnp.int32), axis=1, mode="promise_in_bounds"
        )
        for j in range(PANEL)
    ]
    recip = jnp.zeros_like(rows)
    for j in range(PANEL):
        r = 1.0 / jnp.broadcast_to(cols[j][j : j + 1, :], rows.shape)
        recip = jnp.where(sub == j, r, recip)
        if j + 1 < PANEL:
            mult = jnp.where(sub > j, cols[j] * r, 0.0)
            for k in range(j + 1, PANEL):
                cols[k] = cols[k] - mult * jnp.broadcast_to(cols[k][j : j + 1, :], rows.shape)
            rows = rows - mult * jnp.broadcast_to(rows[j : j + 1, :], rows.shape)
            inv_rows = inv_rows - mult * jnp.broadcast_to(inv_rows[j : j + 1, :], rows.shape)
    inverse_ref[m, pl.ds(start, PANEL), :] = inv_rows
    scale_ref[m, pl.ds(start, PANEL), :] = recip
    return rows, inv_rows, recip


def eliminate_block(block_ref, inverse_ref, scale_ref, mats, size):
    row_id = lax.broadcasted_iota(jnp.int32, (size, size), 0)
    lane_id = lax.broadcasted_iota(jnp.int32, (size, size), 1)
    for m in range(mats):
        inverse_ref[m] = jnp.where(row_id == lane_id, 1.0, 0.0)

    def panel(p, _):
        start = pl.multiple_of(p * PANEL, PANEL)
        done = [eliminate_panel(block_ref, inverse_ref, scale_ref, m, start) for m in range(mats)]
        below = row_id >= start + PANEL
        for m in range(mats):
            rows, inv_rows, recip = done[m]
            both = jnp.concatenate([rows, inv_rows], axis=1)
            change = dot_packed(rows * recip, both, ((0,), (0,)))
            block_ref[m] = block_ref[m] - jnp.where(below, change[:, :size], 0.0)
            inverse_ref[m] = inverse_ref[m] - jnp.where(below, change[:, size:], 0.0)
        return 0

    lax.fori_loop(0, size // PANEL, panel, 0)


def add_gram(gram, pieces, held):
    mats, rank, _ = gram.shape

    def one(m, _):
        for j in range(0, rank, WIDE):
            total = None if held is None else held[m, j:, j : j + WIDE]
            for ref in pieces:
                part = dot_f32(ref[m, :, j:], ref[m, :, j : j + WIDE], ((0,), (0,)))
                total = part if total is None else total + part
            gram[m, j:, j : j + WIDE] = total
        return 0

    lax.fori_loop(0, mats, one, 0)


def gram_kernel(*refs, pieces):
    held = refs[pieces] if len(refs) > pieces + 1 else None
    add_gram(refs[-1], refs[:pieces], held)


def gram_of(pieces, held=None):
    mats, _, rank = pieces[0].shape
    args = list(pieces) + ([] if held is None else [held])
    depth = sum(p.shape[1] for p in pieces)
    vmem = pl.BlockSpec(memory_space=pltpu.VMEM)
    return pl.pallas_call(
        functools.partial(gram_kernel, pieces=len(pieces)),
        out_shape=jax.ShapeDtypeStruct((mats, rank, rank), F32),
        in_specs=[vmem] * len(args),
        out_specs=vmem,
        cost_estimate=pl.CostEstimate(
            flops=12 * mats * depth * rank * rank,
            bytes_accessed=4 * mats * rank * (rank + depth),
            transcendentals=0,
        ),
        name="gram",
    )(*args)


def basis_kernel(offsets, *refs, pieces, fresh):
    own_ref = refs[0]
    piece_refs = refs[1 : 1 + pieces]
    held, basis_ref = refs[1 + pieces : 3 + pieces]
    raw, gram, low, inv, block, binv, scale = refs[3 + pieces :]
    mats, _, rank = raw.shape
    n = rank // BLOCK

    def sl(i):
        return slice(i * BLOCK, (i + 1) * BLOCK)

    for i, ref in enumerate((own_ref, *piece_refs)):
        at = pl.multiple_of(offsets[i], 8)
        raw[:, pl.ds(at, ref.shape[1]), :] = ref[...]

    add_gram(gram, [piece_refs[i] for i in fresh], held)
    for b in range(n):
        below = (b + 1) * BLOCK
        for m in range(mats):
            block[m] = gram[m, sl(b), sl(b)]
        eliminate_block(block, binv, scale, mats, BLOCK)
        for m in range(mats):
            d_inv = binv[m] * jnp.sqrt(scale[m])
            inv[m, sl(b), sl(b)] = d_inv
            if b > 0:
                acc = dot_packed(
                    low[m, sl(b), : b * BLOCK], inv[m, : b * BLOCK, : b * BLOCK], ((1,), (0,))
                )
                inv[m, sl(b), : b * BLOCK] = -dot_packed(d_inv, acc, ((1,), (0,)))
            if b + 1 < n:
                low[m, below:, sl(b)] = dot_packed(gram[m, below:, sl(b)], d_inv, ((1,), (1,)))
                inv[m, sl(b), below:] = jnp.zeros((BLOCK, rank - below), F32)
                for j in range(b + 1, n):
                    gram[m, j * BLOCK :, sl(j)] = gram[m, j * BLOCK :, sl(j)] - dot_packed(
                        low[m, j * BLOCK :, sl(b)], low[m, sl(j), sl(b)], ((1,), (1,))
                    )

    def bases(m, _):
        for j in range(0, rank, WIDE):
            end = j + WIDE
            basis_ref[m, :, j:end] = dot_split(
                raw[m, :, :end], inv[m, j:end, :end], ((1,), (1,))
            ).astype(BF16)
        return 0

    lax.fori_loop(0, mats, bases, 0)


def orthonormal_basis(own, pieces, offsets, held, fresh, feats):
    mats, _, rank = own.shape
    vmem = pl.BlockSpec(memory_space=pltpu.VMEM)
    smem = pl.BlockSpec(memory_space=pltpu.SMEM)
    return pl.pallas_call(
        functools.partial(basis_kernel, pieces=len(pieces), fresh=tuple(fresh)),
        out_shape=jax.ShapeDtypeStruct((mats, feats, rank), BF16),
        in_specs=[smem] + [vmem] * (2 + len(pieces)),
        out_specs=vmem,
        scratch_shapes=[pltpu.VMEM((mats, feats, rank), F32)]
        + [pltpu.VMEM((mats, rank, rank), F32)] * 3
        + [pltpu.VMEM((mats, BLOCK, BLOCK), F32)] * 3,
        cost_estimate=pl.CostEstimate(
            flops=40_000_000_000, bytes_accessed=6 * mats * feats * rank, transcendentals=0
        ),
        name="basis",
    )(offsets, own, *pieces, held)


def collect_kernel(places, counts, *refs):
    m = pl.program_id(1)
    owner_refs, group_ref = refs[:QUAD], refs[QUAD]
    bucket_rows = owner_refs[0].shape[3]
    group_ref[...] = jnp.zeros(group_ref.shape, BF16)
    for i, owner_ref in enumerate(owner_refs):

        def pick(s, _):
            place = places[i, m, s]

            @pl.when(place >= 0)
            def _():
                at = pl.multiple_of(jnp.maximum(place, 0), bucket_rows)
                group_ref[0, 0, pl.ds(at, bucket_rows), :] = owner_ref[0, 0, s]

            return 0

        lax.fori_loop(0, counts[i, m], pick, 0)


def collect_moments(owners, places, counts, column_rows):
    kinds, mats, capacity, bucket_rows, rank = owners[0].shape
    slots = pl.BlockSpec((1, 1, capacity, bucket_rows, rank), lambda a, m, *_: (a, m, 0, 0, 0))
    return pl.pallas_call(
        collect_kernel,
        out_shape=jax.ShapeDtypeStruct((kinds, mats, column_rows, rank), BF16),
        grid_spec=pltpu.PrefetchScalarGridSpec(
            num_scalar_prefetch=2,
            grid=(kinds, mats),
            in_specs=[slots] * QUAD,
            out_specs=pl.BlockSpec((1, 1, column_rows, rank), lambda a, m, *_: (a, m, 0, 0)),
        ),
        cost_estimate=pl.CostEstimate(
            flops=0, bytes_accessed=4 * QUAD * owners[0].size, transcendentals=0
        ),
        name="collect",
    )(places, counts, *owners)


def project_kernel(quads, group, grads_ref, basis_ref, other_ref, own_ref, result):
    unit_rows = other_ref.shape[2]
    result[...] = dot_bf16(grads_ref[0, 0], basis_ref[0], ((1,), (0,))).astype(BF16)
    for i, ref in ((0, other_ref), (1, other_ref), (2, own_ref), (3, own_ref)):
        at = pl.multiple_of(quads[i] * unit_rows, unit_rows)
        ref[i % 2, 0] = result[pl.ds(at, unit_rows), :]


def project(grads, basis, quads, group, unit_rows):
    _, mats, _, feats = grads.shape
    rank = basis.shape[2]
    rows = QUAD * unit_rows
    out = jax.ShapeDtypeStruct((2, mats, unit_rows, rank), BF16)
    out_spec = pl.BlockSpec((2, 1, unit_rows, rank), lambda m, q, g: (0, m, 0, 0))
    return pl.pallas_call(
        project_kernel,
        out_shape=(out, out),
        grid_spec=pltpu.PrefetchScalarGridSpec(
            num_scalar_prefetch=2,
            grid=(mats,),
            in_specs=[
                pl.BlockSpec((1, 1, rows, feats), lambda m, q, g: (0, m, g[0], 0)),
                pl.BlockSpec((1, feats, rank), lambda m, q, g: (m, 0, 0)),
            ],
            out_specs=(out_spec, out_spec),
            scratch_shapes=[pltpu.VMEM((rows, rank), BF16)],
        ),
        cost_estimate=pl.CostEstimate(
            flops=2 * mats * rows * feats * rank,
            bytes_accessed=2 * mats * rows * (feats + rank),
            transcendentals=0,
        ),
        name="project",
    )(quads, group, grads, basis)


def expand_kernel(quads, group, *refs):
    parts, basis_ref = refs[:QUAD], refs[QUAD]
    out_ref, joined = refs[-2:]
    unit_rows = parts[0].shape[1]
    for i, ref in enumerate(parts):
        at = pl.multiple_of(quads[i] * unit_rows, unit_rows)
        joined[pl.ds(at, unit_rows), :] = ref[0]
    out_ref[0] = dot_bf16(joined[...], basis_ref[0], ((1,), (1,))).astype(BF16)


def expand(parts, basis, quads, group, target, local_rows):
    mats, unit_rows, rank = parts[0].shape
    feats = basis.shape[1]
    rows = QUAD * unit_rows
    part = pl.BlockSpec((1, unit_rows, rank), lambda m, q, g: (m, 0, 0))
    in_specs = [part] * QUAD + [pl.BlockSpec((1, feats, rank), lambda m, q, g: (m, 0, 0))]
    args = [quads, group, *parts, basis]
    aliases = {}
    if target is not None:
        in_specs.append(pl.BlockSpec(memory_space=pl.ANY))
        aliases = {len(args): 0}
        args.append(target)
    return pl.pallas_call(
        expand_kernel,
        out_shape=jax.ShapeDtypeStruct((mats, local_rows, feats), BF16),
        grid_spec=pltpu.PrefetchScalarGridSpec(
            num_scalar_prefetch=2,
            grid=(mats,),
            in_specs=in_specs,
            out_specs=pl.BlockSpec((1, rows, feats), lambda m, q, g: (m, g[0], 0)),
            scratch_shapes=[pltpu.VMEM((rows, rank), BF16)],
        ),
        input_output_aliases=aliases,
        cost_estimate=pl.CostEstimate(
            flops=2 * mats * rows * feats * rank,
            bytes_accessed=2 * mats * rows * (feats + rank),
            transcendentals=0,
        ),
        name="expand",
    )(*args)


def new_moments(first, second, grad_rows):
    new_first = 0.9 * first + 0.1 * grad_rows
    new_second = 0.999 * second + 0.001 * grad_rows * grad_rows
    return new_first, new_second


def settle_kernel(piece_of, row_of, held, *refs, pieces):
    piece_refs = refs[:pieces]
    first_ref, second_ref, first_out, second_out, rows, sem = refs[pieces:]
    m = pl.program_id(0)
    capacity, bucket_rows = rows.shape[0], rows.shape[1]

    def fetch(s, _):
        piece = piece_of[m, s]
        at = pl.multiple_of(row_of[m, s], bucket_rows)
        for i, ref in enumerate(piece_refs):

            @pl.when(piece == i)
            def _():
                pltpu.make_async_copy(ref.at[m, pl.ds(at, bucket_rows), :], rows.at[s], sem).start()

        return 0

    lax.fori_loop(0, capacity, fetch, 0)
    pltpu.make_async_copy(rows, rows, sem).wait()

    def settle(s, _):
        first, second = first_ref[0, 0, s], second_ref[0, 0, s]
        new_first, new_second = new_moments(first, second, rows[s].astype(F32))
        keep = held[m, s] > 0
        first_out[0, 0, s] = jnp.where(keep, new_first, first)
        second_out[0, 0, s] = jnp.where(keep, new_second, second)
        return 0

    lax.fori_loop(0, capacity, settle, 0)


def settle_moments(first, second, pieces, piece_of, row_of, held):
    mats, _, capacity, bucket_rows, rank = first.shape
    spec = pl.BlockSpec((1, 1, capacity, bucket_rows, rank), lambda m, *_: (m, 0, 0, 0, 0))
    return pl.pallas_call(
        functools.partial(settle_kernel, pieces=len(pieces)),
        out_shape=(
            jax.ShapeDtypeStruct(first.shape, F32),
            jax.ShapeDtypeStruct(second.shape, F32),
        ),
        grid_spec=pltpu.PrefetchScalarGridSpec(
            num_scalar_prefetch=3,
            grid=(mats,),
            in_specs=[pl.BlockSpec(memory_space=pl.ANY)] * len(pieces) + [spec, spec],
            out_specs=(spec, spec),
            scratch_shapes=[
                pltpu.VMEM((capacity, bucket_rows, rank), BF16),
                pltpu.SemaphoreType.DMA,
            ],
        ),
        cost_estimate=pl.CostEstimate(
            flops=8 * first.size, bytes_accessed=18 * first.size, transcendentals=0
        ),
        name="settle",
    )(piece_of, row_of, held, *pieces, first, second)


def adam_update(first, second, grad_rows):
    new_first, new_second = new_moments(first, second, grad_rows)
    scaled = (
        6.0 * (new_first / (1.0 - 0.9**10)) / (jnp.sqrt(new_second / (1.0 - 0.999**10)) + 1e-08)
    )
    return scaled.astype(BF16)


def shards(grads, raw_proj, bucket_owner, first_moment, second_moment):
    mats, local_rows = grads.shape[1], grads.shape[2]
    local_feats = raw_proj.shape[1]
    buckets = bucket_owner.shape[1]
    capacity = first_moment.shape[2]
    bucket_rows = local_rows // buckets
    replicas = lax.axis_size("dp")
    splits = lax.axis_size("fsdp")
    depth = replicas // QUAD
    unit_rows = local_rows // replicas
    unit_buckets = buckets // replicas
    me = lax.axis_index("dp")
    my_z, my_quad = me // QUAD, me % QUAD

    def permute(v, target):
        return lax.ppermute(v, "dp", [(i, target(i)) for i in range(replicas)])

    def to_core(v):
        return permute(v, lambda i: i ^ 1)

    def to_x(v):
        return permute(v, lambda i: i ^ 2)

    def to_z(v):
        return permute(v, lambda i: (i + QUAD) % replicas)

    quarter = local_feats // QUAD
    part = lax.dynamic_slice_in_dim(raw_proj, my_quad * quarter, quarter, 1)
    my_f = lax.axis_index("fsdp")
    gram = gram_of([raw_proj])
    pieces, offsets, early, fresh = [], [my_f * local_feats], [], []
    for shift in range(1, splits):
        fetched = lax.ppermute(part, "fsdp", [(i, (i + shift) % splits) for i in range(splits)])
        across = to_x(fetched)
        base = ((my_f + splits - shift) % splits) * local_feats
        for piece, flip in ((fetched, 0), (across, 2), (to_core(fetched), 1), (to_core(across), 3)):
            (fresh if flip & 2 else early).append(len(pieces))
            pieces.append(piece)
            offsets.append(base + (my_quad ^ flip) * quarter)
    offsets = jnp.stack(offsets).astype(jnp.int32)
    if early:
        gram = gram_of([pieces[i] for i in early], gram)

    same = bucket_owner[:, :, None] == bucket_owner[:, None, :]
    order = jnp.arange(buckets, dtype=jnp.int32)
    earlier = order[None, :] < order[:, None]
    ranks = jnp.sum(jnp.logical_and(same, earlier).astype(jnp.int32), axis=-1)
    owner_ids = jnp.stack([me ^ flip for flip in (0, 2, 1, 3)])
    local_slot = jnp.where(bucket_owner[None] == owner_ids[:, None, None], ranks[None], -1)
    slot_ids = jnp.arange(capacity, dtype=jnp.int32)
    matches = local_slot[:, :, None, :] == slot_ids[None, None, :, None]
    quad_occupied = jnp.any(matches, axis=3)
    quad_buckets = jnp.sum(jnp.where(matches, order[None, None, None, :], 0), axis=3)
    quad_counts = jnp.sum(quad_occupied.astype(jnp.int32), axis=2)
    occupied, bucket_of = quad_occupied[0], quad_buckets[0]
    quad_units = quad_buckets // unit_buckets
    steps = (my_z + depth - 1 - quad_units // QUAD) % depth
    places = steps * unit_rows + (quad_buckets % unit_buckets) * bucket_rows
    wanted = jnp.logical_and(quad_occupied, quad_units % QUAD == my_quad)
    places = jnp.where(wanted, places, -1).astype(jnp.int32)

    slots = jnp.stack([first_moment[:, 0], second_moment[:, 0]]).astype(BF16)
    slots, pieces = lax.optimization_barrier((slots, pieces))
    slots_across = to_x(slots)
    slots_core = to_core(slots)

    basis = orthonormal_basis(raw_proj, pieces, offsets, gram, fresh, splits * local_feats)

    owners = (slots, slots_across, slots_core, to_core(slots_across))
    column = collect_moments(owners, places, quad_counts, depth * unit_rows)
    moment_groups = [column[:, :, k * unit_rows : (k + 1) * unit_rows] for k in range(depth)]
    unit_moments = moment_groups[0]
    for k in range(1, depth):
        unit_moments = to_z(unit_moments) + moment_groups[k]

    send_quads = jnp.stack([my_quad ^ flip for flip in (3, 1, 2, 0)]).astype(jnp.int32)
    held = None
    for k in range(1, depth + 1):
        group = ((my_z + depth - k) % depth).astype(jnp.int32)[None]
        other, own = project(grads, basis, send_quads, group, unit_rows)
        arrived = to_core(other)
        send = (own[0].astype(F32) + arrived[0].astype(F32)).astype(BF16)
        crossed = to_x(send)
        total = own[1].astype(F32) + arrived[1].astype(F32) + crossed.astype(F32)
        if held is not None:
            total = total + to_z(held).astype(F32)
        held = total.astype(BF16)
    held, grad_rows = lax.optimization_barrier((held, total))

    def ring(unit):
        groups = []
        across = None
        half = mats // 2
        for k in range(depth):
            if 0 < k == depth - 1:
                over_z = to_z(across[half:])
                across = jnp.concatenate([to_x(unit[:half]), over_z])
            else:
                across = to_x(unit)
            core = to_core(unit)
            groups.append((unit, across, core, to_core(across)))
            if k + 1 < depth:
                unit = to_z(unit)
        return groups

    grad_groups = ring(held)
    update = adam_update(unit_moments[0].astype(F32), unit_moments[1].astype(F32), grad_rows)
    update_groups = ring(update)

    part_quads = jnp.stack([my_quad ^ flip for flip in (0, 2, 1, 3)]).astype(jnp.int32)
    weight_delta = None
    for k, parts in enumerate(update_groups):
        group = ((my_z + depth - k) % depth).astype(jnp.int32)[None]
        weight_delta = expand(parts, basis, part_quads, group, weight_delta, local_rows)

    unit = bucket_of // unit_buckets
    back = (my_z + depth - unit // QUAD) % depth
    flip = (unit % QUAD) ^ my_quad
    piece_of = back * QUAD + (flip % 2) * 2 + flip // 2
    row_of = (bucket_of % unit_buckets) * bucket_rows
    first_out, second_out = settle_moments(
        first_moment,
        second_moment,
        [p for parts in grad_groups for p in parts],
        piece_of.astype(jnp.int32),
        row_of.astype(jnp.int32),
        occupied.astype(jnp.int32),
    )
    return weight_delta, first_out, second_out


def solution(mesh):
    return jax.shard_map(
        shards,
        mesh=mesh,
        in_specs=(
            P("dp", None, "fsdp", None),
            P(None, "fsdp", None),
            P(None, "fsdp"),
            P(None, "fsdp", "dp", None, None),
            P(None, "fsdp", "dp", None, None),
        ),
        out_specs=(
            P(None, "fsdp", None),
            P(None, "fsdp", "dp", None, None),
            P(None, "fsdp", "dp", None, None),
        ),
        check_vma=False,
    )
```

```python
import functools

import jax
import jax.numpy as jnp
from jax import lax
from jax.experimental import pallas as pl
from jax.experimental.pallas import tpu as pltpu
from jax.sharding import PartitionSpec as P


PANEL = 8
BLOCK = 128
WIDE = 256
QUAD = 4
F32 = jnp.float32
BF16 = jnp.bfloat16


def dot_f32(a, b, dims):
    return lax.dot_general(
        a, b, (dims, ((), ())), precision=lax.Precision.HIGHEST, preferred_element_type=F32
    )


def dot_bf16(a, b, dims):
    return lax.dot_general(a, b, (dims, ((), ())), preferred_element_type=F32)


def halves(x):
    high = x.astype(BF16)
    return high, (x - high.astype(F32)).astype(BF16)


def dot_split(a, b, dims):
    (a_high, a_low), (b_high, b_low) = halves(a), halves(b)
    return (
        dot_bf16(a_low, b_high, dims)
        + dot_bf16(a_high, b_low, dims)
        + dot_bf16(a_high, b_high, dims)
    )


def thirds(x):
    first = x.astype(BF16).astype(F32)
    rest = x - first
    second = rest.astype(BF16).astype(F32)
    return first, second, rest - second


def dot_packed(a, b, dims):
    a1, a2, a3 = thirds(a)
    b1, b2, b3 = thirds(b)
    (a_dim,), (b_dim,) = dims
    left = jnp.concatenate([a1, a2, a1, a3, a2, a1], axis=a_dim).astype(BF16)
    right = jnp.concatenate([b3, b2, b2, b1, b1, b1], axis=b_dim).astype(BF16)
    return dot_bf16(left, right, dims)


def eliminate_panel(block_ref, inverse_ref, scale_ref, m, start):
    rows = block_ref[m, pl.ds(start, PANEL), :]
    inv_rows = inverse_ref[m, pl.ds(start, PANEL), :]
    sub = lax.broadcasted_iota(jnp.int32, rows.shape, 0)
    cols = [
        jnp.take_along_axis(
            rows, jnp.full(rows.shape, start + j, jnp.int32), axis=1, mode="promise_in_bounds"
        )
        for j in range(PANEL)
    ]
    recip = jnp.zeros_like(rows)
    for j in range(PANEL):
        r = 1.0 / jnp.broadcast_to(cols[j][j : j + 1, :], rows.shape)
        recip = jnp.where(sub == j, r, recip)
        if j + 1 < PANEL:
            mult = jnp.where(sub > j, cols[j] * r, 0.0)
            for k in range(j + 1, PANEL):
                cols[k] = cols[k] - mult * jnp.broadcast_to(cols[k][j : j + 1, :], rows.shape)
            rows = rows - mult * jnp.broadcast_to(rows[j : j + 1, :], rows.shape)
            inv_rows = inv_rows - mult * jnp.broadcast_to(inv_rows[j : j + 1, :], rows.shape)
    inverse_ref[m, pl.ds(start, PANEL), :] = inv_rows
    scale_ref[m, pl.ds(start, PANEL), :] = recip
    return rows, inv_rows, recip


def eliminate_block(block_ref, inverse_ref, scale_ref, mats, size):
    row_id = lax.broadcasted_iota(jnp.int32, (size, size), 0)
    lane_id = lax.broadcasted_iota(jnp.int32, (size, size), 1)
    for m in range(mats):
        inverse_ref[m] = jnp.where(row_id == lane_id, 1.0, 0.0)

    def panel(p, _):
        start = pl.multiple_of(p * PANEL, PANEL)
        done = [eliminate_panel(block_ref, inverse_ref, scale_ref, m, start) for m in range(mats)]
        below = row_id >= start + PANEL
        for m in range(mats):
            rows, inv_rows, recip = done[m]
            both = jnp.concatenate([rows, inv_rows], axis=1)
            change = dot_packed(rows * recip, both, ((0,), (0,)))
            block_ref[m] = block_ref[m] - jnp.where(below, change[:, :size], 0.0)
            inverse_ref[m] = inverse_ref[m] - jnp.where(below, change[:, size:], 0.0)
        return 0

    lax.fori_loop(0, size // PANEL, panel, 0)


def add_gram(gram, pieces, held):
    mats, rank, _ = gram.shape

    def one(m, _):
        for j in range(0, rank, WIDE):
            total = None if held is None else held[m, j:, j : j + WIDE]
            for ref in pieces:
                part = dot_f32(ref[m, :, j:], ref[m, :, j : j + WIDE], ((0,), (0,)))
                total = part if total is None else total + part
            gram[m, j:, j : j + WIDE] = total
        return 0

    lax.fori_loop(0, mats, one, 0)


def gram_kernel(*refs, pieces):
    held = refs[pieces] if len(refs) > pieces + 1 else None
    add_gram(refs[-1], refs[:pieces], held)


def gram_of(pieces, held=None):
    mats, _, rank = pieces[0].shape
    args = list(pieces) + ([] if held is None else [held])
    depth = sum(p.shape[1] for p in pieces)
    vmem = pl.BlockSpec(memory_space=pltpu.VMEM)
    return pl.pallas_call(
        functools.partial(gram_kernel, pieces=len(pieces)),
        out_shape=jax.ShapeDtypeStruct((mats, rank, rank), F32),
        in_specs=[vmem] * len(args),
        out_specs=vmem,
        cost_estimate=pl.CostEstimate(
            flops=12 * mats * depth * rank * rank,
            bytes_accessed=4 * mats * rank * (rank + depth),
            transcendentals=0,
        ),
        name="gram",
    )(*args)


def basis_kernel(offsets, *refs, pieces, fresh):
    own_ref = refs[0]
    piece_refs = refs[1 : 1 + pieces]
    held, basis_ref = refs[1 + pieces : 3 + pieces]
    raw, gram, low, inv, block, binv, scale = refs[3 + pieces :]
    mats, _, rank = raw.shape
    n = rank // BLOCK

    def sl(i):
        return slice(i * BLOCK, (i + 1) * BLOCK)

    for i, ref in enumerate((own_ref, *piece_refs)):
        at = pl.multiple_of(offsets[i], 8)
        raw[:, pl.ds(at, ref.shape[1]), :] = ref[...]

    add_gram(gram, [piece_refs[i] for i in fresh], held)
    for b in range(n):
        below = (b + 1) * BLOCK
        for m in range(mats):
            block[m] = gram[m, sl(b), sl(b)]
        eliminate_block(block, binv, scale, mats, BLOCK)
        for m in range(mats):
            d_inv = binv[m] * jnp.sqrt(scale[m])
            inv[m, sl(b), sl(b)] = d_inv
            if b > 0:
                acc = dot_packed(
                    low[m, sl(b), : b * BLOCK], inv[m, : b * BLOCK, : b * BLOCK], ((1,), (0,))
                )
                inv[m, sl(b), : b * BLOCK] = -dot_packed(d_inv, acc, ((1,), (0,)))
            if b + 1 < n:
                low[m, below:, sl(b)] = dot_packed(gram[m, below:, sl(b)], d_inv, ((1,), (1,)))
                inv[m, sl(b), below:] = jnp.zeros((BLOCK, rank - below), F32)
                for j in range(b + 1, n):
                    gram[m, j * BLOCK :, sl(j)] = gram[m, j * BLOCK :, sl(j)] - dot_packed(
                        low[m, j * BLOCK :, sl(b)], low[m, sl(j), sl(b)], ((1,), (1,))
                    )

    def bases(m, _):
        for j in range(0, rank, WIDE):
            end = j + WIDE
            basis_ref[m, :, j:end] = dot_split(
                raw[m, :, :end], inv[m, j:end, :end], ((1,), (1,))
            ).astype(BF16)
        return 0

    lax.fori_loop(0, mats, bases, 0)


def orthonormal_basis(own, pieces, offsets, held, fresh, feats):
    mats, _, rank = own.shape
    vmem = pl.BlockSpec(memory_space=pltpu.VMEM)
    smem = pl.BlockSpec(memory_space=pltpu.SMEM)
    return pl.pallas_call(
        functools.partial(basis_kernel, pieces=len(pieces), fresh=tuple(fresh)),
        out_shape=jax.ShapeDtypeStruct((mats, feats, rank), BF16),
        in_specs=[smem] + [vmem] * (2 + len(pieces)),
        out_specs=vmem,
        scratch_shapes=[pltpu.VMEM((mats, feats, rank), F32)]
        + [pltpu.VMEM((mats, rank, rank), F32)] * 3
        + [pltpu.VMEM((mats, BLOCK, BLOCK), F32)] * 3,
        cost_estimate=pl.CostEstimate(
            flops=40_000_000_000, bytes_accessed=6 * mats * feats * rank, transcendentals=0
        ),
        name="basis",
    )(offsets, own, *pieces, held)


def collect_kernel(places, counts, *refs):
    m = pl.program_id(1)
    owner_refs, (head_ref, rest_ref) = refs[:QUAD], refs[QUAD:]
    bucket_rows, head_rows = owner_refs[0].shape[3], head_ref.shape[2]
    for ref in (head_ref, rest_ref):
        ref[...] = jnp.zeros(ref.shape, BF16)
    for i, owner_ref in enumerate(owner_refs):

        def pick(s, _):
            place = places[i, m, s]

            @pl.when(jnp.logical_and(place >= 0, place < head_rows))
            def _():
                at = pl.multiple_of(jnp.maximum(place, 0), bucket_rows)
                head_ref[0, 0, pl.ds(at, bucket_rows), :] = owner_ref[0, 0, s]

            @pl.when(place >= head_rows)
            def _():
                at = pl.multiple_of(jnp.maximum(place - head_rows, 0), bucket_rows)
                rest_ref[0, 0, pl.ds(at, bucket_rows), :] = owner_ref[0, 0, s]

            return 0

        lax.fori_loop(0, counts[i, m], pick, 0)


def collect_moments(owners, places, counts, head_rows, rest_rows):
    kinds, mats, capacity, bucket_rows, rank = owners[0].shape
    slots = pl.BlockSpec((1, 1, capacity, bucket_rows, rank), lambda a, m, *_: (a, m, 0, 0, 0))
    return pl.pallas_call(
        collect_kernel,
        out_shape=tuple(
            jax.ShapeDtypeStruct((kinds, mats, rows, rank), BF16) for rows in (head_rows, rest_rows)
        ),
        grid_spec=pltpu.PrefetchScalarGridSpec(
            num_scalar_prefetch=2,
            grid=(kinds, mats),
            in_specs=[slots] * QUAD,
            out_specs=tuple(
                pl.BlockSpec((1, 1, rows, rank), lambda a, m, *_: (a, m, 0, 0))
                for rows in (head_rows, rest_rows)
            ),
        ),
        cost_estimate=pl.CostEstimate(
            flops=0, bytes_accessed=4 * QUAD * owners[0].size, transcendentals=0
        ),
        name="collect",
    )(places, counts, *owners)


def project_kernel(quads, group, grads_ref, basis_ref, other_ref, own_ref, result):
    unit_rows = other_ref.shape[2]
    result[...] = dot_bf16(grads_ref[0, 0], basis_ref[0], ((1,), (0,))).astype(BF16)
    for i, ref in ((0, other_ref), (1, other_ref), (2, own_ref), (3, own_ref)):
        at = pl.multiple_of(quads[i] * unit_rows, unit_rows)
        ref[i % 2, 0] = result[pl.ds(at, unit_rows), :]


def project(grads, basis, quads, group, unit_rows):
    _, mats, _, feats = grads.shape
    rank = basis.shape[2]
    rows = QUAD * unit_rows
    out = jax.ShapeDtypeStruct((2, mats, unit_rows, rank), BF16)
    out_spec = pl.BlockSpec((2, 1, unit_rows, rank), lambda m, q, g: (0, m, 0, 0))
    return pl.pallas_call(
        project_kernel,
        out_shape=(out, out),
        grid_spec=pltpu.PrefetchScalarGridSpec(
            num_scalar_prefetch=2,
            grid=(mats,),
            in_specs=[
                pl.BlockSpec((1, 1, rows, feats), lambda m, q, g: (0, m, g[0], 0)),
                pl.BlockSpec((1, feats, rank), lambda m, q, g: (m, 0, 0)),
            ],
            out_specs=(out_spec, out_spec),
            scratch_shapes=[pltpu.VMEM((rows, rank), BF16)],
        ),
        cost_estimate=pl.CostEstimate(
            flops=2 * mats * rows * feats * rank,
            bytes_accessed=2 * mats * rows * (feats + rank),
            transcendentals=0,
        ),
        name="project",
    )(quads, group, grads, basis)


def expand_kernel(quads, group, *refs):
    parts, basis_ref = refs[:QUAD], refs[QUAD]
    out_ref, joined = refs[-2:]
    unit_rows = parts[0].shape[1]
    for i, ref in enumerate(parts):
        at = pl.multiple_of(quads[i] * unit_rows, unit_rows)
        joined[pl.ds(at, unit_rows), :] = ref[0]
    out_ref[0] = dot_bf16(joined[...], basis_ref[0], ((1,), (1,))).astype(BF16)


def expand(parts, basis, quads, group, target, local_rows):
    mats, unit_rows, rank = parts[0].shape
    feats = basis.shape[1]
    rows = QUAD * unit_rows
    part = pl.BlockSpec((1, unit_rows, rank), lambda m, q, g: (m, 0, 0))
    in_specs = [part] * QUAD + [pl.BlockSpec((1, feats, rank), lambda m, q, g: (m, 0, 0))]
    args = [quads, group, *parts, basis]
    aliases = {}
    if target is not None:
        in_specs.append(pl.BlockSpec(memory_space=pl.ANY))
        aliases = {len(args): 0}
        args.append(target)
    return pl.pallas_call(
        expand_kernel,
        out_shape=jax.ShapeDtypeStruct((mats, local_rows, feats), BF16),
        grid_spec=pltpu.PrefetchScalarGridSpec(
            num_scalar_prefetch=2,
            grid=(mats,),
            in_specs=in_specs,
            out_specs=pl.BlockSpec((1, rows, feats), lambda m, q, g: (m, g[0], 0)),
            scratch_shapes=[pltpu.VMEM((rows, rank), BF16)],
        ),
        input_output_aliases=aliases,
        cost_estimate=pl.CostEstimate(
            flops=2 * mats * rows * feats * rank,
            bytes_accessed=2 * mats * rows * (feats + rank),
            transcendentals=0,
        ),
        name="expand",
    )(*args)


def new_moments(first, second, grad_rows):
    new_first = 0.9 * first + 0.1 * grad_rows
    new_second = 0.999 * second + 0.001 * grad_rows * grad_rows
    return new_first, new_second


def settle_kernel(piece_of, row_of, held, *refs, pieces):
    piece_refs = refs[:pieces]
    first_ref, second_ref, first_out, second_out, rows, sem = refs[pieces:]
    m = pl.program_id(0)
    capacity, bucket_rows = rows.shape[0], rows.shape[1]

    def fetch(s, _):
        piece = piece_of[m, s]
        at = pl.multiple_of(row_of[m, s], bucket_rows)
        for i, ref in enumerate(piece_refs):

            @pl.when(piece == i)
            def _():
                pltpu.make_async_copy(ref.at[m, pl.ds(at, bucket_rows), :], rows.at[s], sem).start()

        return 0

    lax.fori_loop(0, capacity, fetch, 0)
    pltpu.make_async_copy(rows, rows, sem).wait()

    def settle(s, _):
        first, second = first_ref[0, 0, s], second_ref[0, 0, s]
        new_first, new_second = new_moments(first, second, rows[s].astype(F32))
        keep = held[m, s] > 0
        first_out[0, 0, s] = jnp.where(keep, new_first, first)
        second_out[0, 0, s] = jnp.where(keep, new_second, second)
        return 0

    lax.fori_loop(0, capacity, settle, 0)


def settle_moments(first, second, pieces, piece_of, row_of, held):
    mats, _, capacity, bucket_rows, rank = first.shape
    spec = pl.BlockSpec((1, 1, capacity, bucket_rows, rank), lambda m, *_: (m, 0, 0, 0, 0))
    return pl.pallas_call(
        functools.partial(settle_kernel, pieces=len(pieces)),
        out_shape=(
            jax.ShapeDtypeStruct(first.shape, F32),
            jax.ShapeDtypeStruct(second.shape, F32),
        ),
        grid_spec=pltpu.PrefetchScalarGridSpec(
            num_scalar_prefetch=3,
            grid=(mats,),
            in_specs=[pl.BlockSpec(memory_space=pl.ANY)] * len(pieces) + [spec, spec],
            out_specs=(spec, spec),
            scratch_shapes=[
                pltpu.VMEM((capacity, bucket_rows, rank), BF16),
                pltpu.SemaphoreType.DMA,
            ],
        ),
        cost_estimate=pl.CostEstimate(
            flops=8 * first.size, bytes_accessed=18 * first.size, transcendentals=0
        ),
        name="settle",
    )(piece_of, row_of, held, *pieces, first, second)


def adam_update(first, second, grad_rows):
    new_first, new_second = new_moments(first, second, grad_rows)
    scaled = (
        6.0 * (new_first / (1.0 - 0.9**10)) / (jnp.sqrt(new_second / (1.0 - 0.999**10)) + 1e-08)
    )
    return scaled.astype(BF16)


def shards(grads, raw_proj, bucket_owner, first_moment, second_moment):
    mats, local_rows = grads.shape[1], grads.shape[2]
    local_feats = raw_proj.shape[1]
    buckets = bucket_owner.shape[1]
    capacity = first_moment.shape[2]
    bucket_rows = local_rows // buckets
    replicas = lax.axis_size("dp")
    splits = lax.axis_size("fsdp")
    depth = replicas // QUAD
    unit_rows = local_rows // replicas
    unit_buckets = buckets // replicas
    me = lax.axis_index("dp")
    my_z, my_quad = me // QUAD, me % QUAD

    def permute(v, target):
        return lax.ppermute(v, "dp", [(i, target(i)) for i in range(replicas)])

    def to_core(v):
        return permute(v, lambda i: i ^ 1)

    def to_x(v):
        return permute(v, lambda i: i ^ 2)

    def to_z(v):
        return permute(v, lambda i: (i + QUAD) % replicas)

    quarter = local_feats // QUAD
    my_core = me % 2
    parts = [
        lax.dynamic_slice_in_dim(raw_proj, (2 * my_core + i) * quarter, quarter, 1) for i in range(2)
    ]
    my_f = lax.axis_index("fsdp")
    gram = gram_of([raw_proj])
    pieces, offsets, early, fresh = [], [my_f * local_feats], [], []
    for shift in range(1, splits):
        base = ((my_f + splits - shift) % splits) * local_feats
        for i, indices in ((0, early), (1, fresh)):
            fetched = lax.ppermute(
                parts[i], "fsdp", [(j, (j + shift) % splits) for j in range(splits)]
            )
            for piece, core in ((fetched, my_core), (to_core(fetched), 1 - my_core)):
                indices.append(len(pieces))
                pieces.append(piece)
                offsets.append(base + (2 * core + i) * quarter)
    offsets = jnp.stack(offsets).astype(jnp.int32)
    if early:
        gram = gram_of([pieces[i] for i in early], gram)

    same = bucket_owner[:, :, None] == bucket_owner[:, None, :]
    order = jnp.arange(buckets, dtype=jnp.int32)
    earlier = order[None, :] < order[:, None]
    ranks = jnp.sum(jnp.logical_and(same, earlier).astype(jnp.int32), axis=-1)
    owner_ids = jnp.stack([me ^ flip for flip in (0, 2, 1, 3)])
    local_slot = jnp.where(bucket_owner[None] == owner_ids[:, None, None], ranks[None], -1)
    slot_ids = jnp.arange(capacity, dtype=jnp.int32)
    matches = local_slot[:, :, None, :] == slot_ids[None, None, :, None]
    quad_occupied = jnp.any(matches, axis=3)
    quad_buckets = jnp.sum(jnp.where(matches, order[None, None, None, :], 0), axis=3)
    quad_counts = jnp.sum(quad_occupied.astype(jnp.int32), axis=2)
    occupied, bucket_of = quad_occupied[0], quad_buckets[0]
    quad_units = quad_buckets // unit_buckets
    steps = (my_z + depth - 1 - quad_units // QUAD) % depth
    places = steps * unit_rows + (quad_buckets % unit_buckets) * bucket_rows
    wanted = jnp.logical_and(quad_occupied, quad_units % QUAD == my_quad)
    places = jnp.where(wanted, places, -1).astype(jnp.int32)

    slots = jnp.stack([first_moment[:, 0], second_moment[:, 0]]).astype(BF16)
    slots_across = to_x(slots)
    slots_core = to_core(slots)

    basis = orthonormal_basis(raw_proj, pieces, offsets, gram, fresh, splits * local_feats)

    owners = (slots, slots_across, slots_core, to_core(slots_across))
    unit_moments, rest = collect_moments(
        owners, places, quad_counts, unit_rows, (depth - 1) * unit_rows
    )
    for k in range(1, depth):
        unit_moments = to_z(unit_moments) + rest[:, :, (k - 1) * unit_rows : k * unit_rows]

    send_quads = jnp.stack([my_quad ^ flip for flip in (3, 1, 2, 0)]).astype(jnp.int32)
    held = None
    for k in range(1, depth + 1):
        group = ((my_z + depth - k) % depth).astype(jnp.int32)[None]
        other, own = project(grads, basis, send_quads, group, unit_rows)
        arrived = to_core(other)
        send = (own[0].astype(F32) + arrived[0].astype(F32)).astype(BF16)
        crossed = to_x(send)
        total = own[1].astype(F32) + arrived[1].astype(F32) + crossed.astype(F32)
        if held is not None:
            total = total + to_z(held).astype(F32)
        held = total.astype(BF16)
    held, grad_rows = lax.optimization_barrier((held, total))

    def ring(unit):
        groups = []
        across = None
        half = mats // 2
        for k in range(depth):
            if 0 < k == depth - 1:
                over_z = to_z(across[half:])
                across = jnp.concatenate([to_x(unit[:half]), over_z])
            else:
                across = to_x(unit)
            core = to_core(unit)
            groups.append((unit, across, core, to_core(across)))
            if k + 1 < depth:
                unit = to_z(unit)
        return groups

    grad_groups = ring(held)
    update = adam_update(unit_moments[0].astype(F32), unit_moments[1].astype(F32), grad_rows)
    update_groups = ring(update)

    part_quads = jnp.stack([my_quad ^ flip for flip in (0, 2, 1, 3)]).astype(jnp.int32)
    weight_delta = None
    for k, parts in enumerate(update_groups):
        group = ((my_z + depth - k) % depth).astype(jnp.int32)[None]
        weight_delta = expand(parts, basis, part_quads, group, weight_delta, local_rows)

    unit = bucket_of // unit_buckets
    back = (my_z + depth - unit // QUAD) % depth
    flip = (unit % QUAD) ^ my_quad
    piece_of = back * QUAD + (flip % 2) * 2 + flip // 2
    row_of = (bucket_of % unit_buckets) * bucket_rows
    first_out, second_out = settle_moments(
        first_moment,
        second_moment,
        [p for parts in grad_groups for p in parts],
        piece_of.astype(jnp.int32),
        row_of.astype(jnp.int32),
        occupied.astype(jnp.int32),
    )
    return weight_delta, first_out, second_out


def solution(mesh):
    return jax.shard_map(
        shards,
        mesh=mesh,
        in_specs=(
            P("dp", None, "fsdp", None),
            P(None, "fsdp", None),
            P(None, "fsdp"),
            P(None, "fsdp", "dp", None, None),
            P(None, "fsdp", "dp", None, None),
        ),
        out_specs=(
            P(None, "fsdp", None),
            P(None, "fsdp", "dp", None, None),
            P(None, "fsdp", "dp", None, None),
        ),
        check_vma=False,
    )
```

```python
import functools

import jax
import jax.numpy as jnp
from jax import lax
from jax.experimental import pallas as pl
from jax.experimental.pallas import tpu as pltpu
from jax.sharding import PartitionSpec as P


PANEL = 8
BLOCK = 128
WIDE = 256
QUAD = 4
F32 = jnp.float32
BF16 = jnp.bfloat16


def dot_f32(a, b, dims):
    return lax.dot_general(
        a, b, (dims, ((), ())), precision=lax.Precision.HIGHEST, preferred_element_type=F32
    )


def dot_bf16(a, b, dims):
    return lax.dot_general(a, b, (dims, ((), ())), preferred_element_type=F32)


def halves(x):
    high = x.astype(BF16)
    return high, (x - high.astype(F32)).astype(BF16)


def dot_split(a, b, dims):
    (a_high, a_low), (b_high, b_low) = halves(a), halves(b)
    return (
        dot_bf16(a_low, b_high, dims)
        + dot_bf16(a_high, b_low, dims)
        + dot_bf16(a_high, b_high, dims)
    )


def thirds(x):
    first = x.astype(BF16).astype(F32)
    rest = x - first
    second = rest.astype(BF16).astype(F32)
    return first, second, rest - second


def dot_packed(a, b, dims):
    a1, a2, a3 = thirds(a)
    b1, b2, b3 = thirds(b)
    (a_dim,), (b_dim,) = dims
    left = jnp.concatenate([a1, a2, a1, a3, a2, a1], axis=a_dim).astype(BF16)
    right = jnp.concatenate([b3, b2, b2, b1, b1, b1], axis=b_dim).astype(BF16)
    return dot_bf16(left, right, dims)


def eliminate_panel(block_ref, inverse_ref, scale_ref, m, start):
    rows = block_ref[m, pl.ds(start, PANEL), :]
    inv_rows = inverse_ref[m, pl.ds(start, PANEL), :]
    sub = lax.broadcasted_iota(jnp.int32, rows.shape, 0)
    cols = [
        jnp.take_along_axis(
            rows, jnp.full(rows.shape, start + j, jnp.int32), axis=1, mode="promise_in_bounds"
        )
        for j in range(PANEL)
    ]
    recip = jnp.zeros_like(rows)
    for j in range(PANEL):
        r = 1.0 / jnp.broadcast_to(cols[j][j : j + 1, :], rows.shape)
        recip = jnp.where(sub == j, r, recip)
        if j + 1 < PANEL:
            mult = jnp.where(sub > j, cols[j] * r, 0.0)
            for k in range(j + 1, PANEL):
                cols[k] = cols[k] - mult * jnp.broadcast_to(cols[k][j : j + 1, :], rows.shape)
            rows = rows - mult * jnp.broadcast_to(rows[j : j + 1, :], rows.shape)
            inv_rows = inv_rows - mult * jnp.broadcast_to(inv_rows[j : j + 1, :], rows.shape)
    inverse_ref[m, pl.ds(start, PANEL), :] = inv_rows
    scale_ref[m, pl.ds(start, PANEL), :] = recip
    return rows, inv_rows, recip


def eliminate_block(block_ref, inverse_ref, scale_ref, mats, size):
    row_id = lax.broadcasted_iota(jnp.int32, (size, size), 0)
    lane_id = lax.broadcasted_iota(jnp.int32, (size, size), 1)
    for m in range(mats):
        inverse_ref[m] = jnp.where(row_id == lane_id, 1.0, 0.0)

    def panel(p, _):
        start = pl.multiple_of(p * PANEL, PANEL)
        done = [eliminate_panel(block_ref, inverse_ref, scale_ref, m, start) for m in range(mats)]
        below = row_id >= start + PANEL
        for m in range(mats):
            rows, inv_rows, recip = done[m]
            both = jnp.concatenate([rows, inv_rows], axis=1)
            change = dot_packed(rows * recip, both, ((0,), (0,)))
            block_ref[m] = block_ref[m] - jnp.where(below, change[:, :size], 0.0)
            inverse_ref[m] = inverse_ref[m] - jnp.where(below, change[:, size:], 0.0)
        return 0

    lax.fori_loop(0, size // PANEL, panel, 0)


def add_gram(gram, pieces, held):
    mats, rank, _ = gram.shape

    def one(m, _):
        for j in range(0, rank, WIDE):
            total = None if held is None else held[m, j:, j : j + WIDE]
            for ref in pieces:
                part = dot_f32(ref[m, :, j:], ref[m, :, j : j + WIDE], ((0,), (0,)))
                total = part if total is None else total + part
            gram[m, j:, j : j + WIDE] = total
        return 0

    lax.fori_loop(0, mats, one, 0)


def gram_kernel(*refs, pieces):
    held = refs[pieces] if len(refs) > pieces + 1 else None
    add_gram(refs[-1], refs[:pieces], held)


def gram_of(pieces, held=None):
    mats, _, rank = pieces[0].shape
    args = list(pieces) + ([] if held is None else [held])
    depth = sum(p.shape[1] for p in pieces)
    vmem = pl.BlockSpec(memory_space=pltpu.VMEM)
    return pl.pallas_call(
        functools.partial(gram_kernel, pieces=len(pieces)),
        out_shape=jax.ShapeDtypeStruct((mats, rank, rank), F32),
        in_specs=[vmem] * len(args),
        out_specs=vmem,
        cost_estimate=pl.CostEstimate(
            flops=12 * mats * depth * rank * rank,
            bytes_accessed=4 * mats * rank * (rank + depth),
            transcendentals=0,
        ),
        name="gram",
    )(*args)


def factor(gram, inv, low, block, binv, scale, size):
    mats = block.shape[0]
    n = size // BLOCK

    def sl(i):
        return slice(i * BLOCK, (i + 1) * BLOCK)

    for b in range(n):
        below = (b + 1) * BLOCK
        for m in range(mats):
            block[m] = gram[m, sl(b), sl(b)]
        eliminate_block(block, binv, scale, mats, BLOCK)
        for m in range(mats):
            d_inv = binv[m] * jnp.sqrt(scale[m])
            inv[m, sl(b), sl(b)] = d_inv
            if b > 0:
                acc = dot_packed(
                    low[m, sl(b), : b * BLOCK], inv[m, : b * BLOCK, : b * BLOCK], ((1,), (0,))
                )
                inv[m, sl(b), : b * BLOCK] = -dot_packed(d_inv, acc, ((1,), (0,)))
            if b + 1 < n:
                low[m, below:size, sl(b)] = dot_packed(gram[m, below:size, sl(b)], d_inv, ((1,), (1,)))
                inv[m, sl(b), below:size] = jnp.zeros((BLOCK, size - below), F32)
                for j in range(b + 1, n):
                    gram[m, j * BLOCK : size, sl(j)] = gram[m, j * BLOCK : size, sl(j)] - dot_packed(
                        low[m, j * BLOCK : size, sl(b)], low[m, sl(j), sl(b)], ((1,), (1,))
                    )


def first_half_kernel(*refs, pieces):
    held, inv_out, low_out, rest_out, gram, low, block, binv, scale = refs[pieces:]
    mats, rank, _ = gram.shape
    half = rank // 2
    add_gram(gram, refs[:pieces], held)
    factor(gram, inv_out, low, block, binv, scale, half)
    for m in range(mats):
        side = dot_f32(gram[m, half:, :half], inv_out[m], ((1,), (1,)))
        low_out[m] = side
        rest_out[m] = gram[m, half:, half:] - dot_f32(side, side, ((1,), (1,)))


def second_half_kernel(offsets, *refs, pieces):
    own_ref = refs[0]
    piece_refs = refs[1 : 1 + pieces]
    inv_ref, side_ref, rest_ref, basis_ref = refs[1 + pieces : 5 + pieces]
    raw, gram, inv, low, block, binv, scale = refs[5 + pieces :]
    mats, _, rank = raw.shape
    half = rank // 2
    for i, ref in enumerate((own_ref, *piece_refs)):
        at = pl.multiple_of(offsets[i], 8)
        raw[:, pl.ds(at, ref.shape[1]), :] = ref[...]
    gram[...] = rest_ref[...]
    factor(gram, inv, low, block, binv, scale, half)

    def bases(m, _):
        acc = dot_f32(side_ref[m], inv_ref[m], ((1,), (0,)))
        left = -dot_f32(inv[m], acc, ((1,), (0,)))
        basis_ref[m, :, :half] = dot_split(raw[m, :, :half], inv_ref[m], ((1,), (1,))).astype(BF16)
        both = jnp.concatenate([left, inv[m]], axis=1)
        basis_ref[m, :, half:] = dot_split(raw[m], both, ((1,), (1,))).astype(BF16)
        return 0

    lax.fori_loop(0, mats, bases, 0)


def first_half(fresh, held):
    mats, rank, _ = held.shape
    half = rank // 2
    vmem = pl.BlockSpec(memory_space=pltpu.VMEM)
    state = jax.ShapeDtypeStruct((mats, half, half), F32)
    return pl.pallas_call(
        functools.partial(first_half_kernel, pieces=len(fresh)),
        out_shape=(state,) * 3,
        in_specs=[vmem] * (len(fresh) + 1),
        out_specs=(vmem,) * 3,
        scratch_shapes=[
            pltpu.VMEM((mats, rank, rank), F32),
            pltpu.VMEM((mats, half, half), F32),
        ]
        + [pltpu.VMEM((mats, BLOCK, BLOCK), F32)] * 3,
        cost_estimate=pl.CostEstimate(
            flops=20_000_000_000, bytes_accessed=4 * mats * rank * rank, transcendentals=0
        ),
        name="first_half",
    )(*fresh, held)


def second_half(own, pieces, offsets, state, feats):
    mats, _, rank = own.shape
    half = rank // 2
    vmem = pl.BlockSpec(memory_space=pltpu.VMEM)
    smem = pl.BlockSpec(memory_space=pltpu.SMEM)
    return pl.pallas_call(
        functools.partial(second_half_kernel, pieces=len(pieces)),
        out_shape=jax.ShapeDtypeStruct((mats, feats, rank), BF16),
        in_specs=[smem] + [vmem] * (4 + len(pieces)),
        out_specs=vmem,
        scratch_shapes=[pltpu.VMEM((mats, feats, rank), F32)]
        + [pltpu.VMEM((mats, half, half), F32)] * 3
        + [pltpu.VMEM((mats, BLOCK, BLOCK), F32)] * 3,
        cost_estimate=pl.CostEstimate(
            flops=20_000_000_000, bytes_accessed=6 * mats * feats * rank, transcendentals=0
        ),
        name="second_half",
    )(offsets, own, *pieces, *state)


def collect_kernel(places, counts, *refs):
    m = pl.program_id(0)
    owner_refs, (head_ref, rest_ref) = refs[:QUAD], refs[QUAD:]
    bucket_rows, head_rows = owner_refs[0].shape[2], head_ref.shape[1]
    for ref in (head_ref, rest_ref):
        ref[...] = jnp.zeros(ref.shape, BF16)
    for i, owner_ref in enumerate(owner_refs):

        def pick(s, _):
            place = places[i, m, s]

            @pl.when(jnp.logical_and(place >= 0, place < head_rows))
            def _():
                at = pl.multiple_of(jnp.maximum(place, 0), bucket_rows)
                head_ref[0, pl.ds(at, bucket_rows), :] = owner_ref[0, s]

            @pl.when(place >= head_rows)
            def _():
                at = pl.multiple_of(jnp.maximum(place - head_rows, 0), bucket_rows)
                rest_ref[0, pl.ds(at, bucket_rows), :] = owner_ref[0, s]

            return 0

        lax.fori_loop(0, counts[i, m], pick, 0)


def collect_moments(owners, places, counts, head_rows, rest_rows):
    mats, capacity, bucket_rows, rank = owners[0].shape
    slots = pl.BlockSpec((1, capacity, bucket_rows, rank), lambda m, *_: (m, 0, 0, 0))
    return pl.pallas_call(
        collect_kernel,
        out_shape=tuple(
            jax.ShapeDtypeStruct((mats, rows, rank), BF16) for rows in (head_rows, rest_rows)
        ),
        grid_spec=pltpu.PrefetchScalarGridSpec(
            num_scalar_prefetch=2,
            grid=(mats,),
            in_specs=[slots] * QUAD,
            out_specs=tuple(
                pl.BlockSpec((1, rows, rank), lambda m, *_: (m, 0, 0))
                for rows in (head_rows, rest_rows)
            ),
        ),
        cost_estimate=pl.CostEstimate(
            flops=0, bytes_accessed=4 * QUAD * owners[0].size, transcendentals=0
        ),
        name="collect",
    )(places, counts, *owners)


def project_kernel(quads, group, grads_ref, basis_ref, other_ref, own_ref, result):
    unit_rows = other_ref.shape[2]
    result[...] = dot_bf16(grads_ref[0, 0], basis_ref[0], ((1,), (0,))).astype(BF16)
    for i, ref in ((0, other_ref), (1, other_ref), (2, own_ref), (3, own_ref)):
        at = pl.multiple_of(quads[i] * unit_rows, unit_rows)
        ref[i % 2, 0] = result[pl.ds(at, unit_rows), :]


def project(grads, basis, quads, group, unit_rows):
    _, mats, _, feats = grads.shape
    rank = basis.shape[2]
    rows = QUAD * unit_rows
    out = jax.ShapeDtypeStruct((2, mats, unit_rows, rank), BF16)
    out_spec = pl.BlockSpec((2, 1, unit_rows, rank), lambda m, q, g: (0, m, 0, 0))
    return pl.pallas_call(
        project_kernel,
        out_shape=(out, out),
        grid_spec=pltpu.PrefetchScalarGridSpec(
            num_scalar_prefetch=2,
            grid=(mats,),
            in_specs=[
                pl.BlockSpec((1, 1, rows, feats), lambda m, q, g: (0, m, g[0], 0)),
                pl.BlockSpec((1, feats, rank), lambda m, q, g: (m, 0, 0)),
            ],
            out_specs=(out_spec, out_spec),
            scratch_shapes=[pltpu.VMEM((rows, rank), BF16)],
        ),
        cost_estimate=pl.CostEstimate(
            flops=2 * mats * rows * feats * rank,
            bytes_accessed=2 * mats * rows * (feats + rank),
            transcendentals=0,
        ),
        name="project",
    )(quads, group, grads, basis)


def expand_kernel(quads, group, *refs):
    parts, basis_ref = refs[:QUAD], refs[QUAD]
    out_ref, joined = refs[-2:]
    unit_rows = parts[0].shape[1]
    for i, ref in enumerate(parts):
        at = pl.multiple_of(quads[i] * unit_rows, unit_rows)
        joined[pl.ds(at, unit_rows), :] = ref[0]
    out_ref[0] = dot_bf16(joined[...], basis_ref[0], ((1,), (1,))).astype(BF16)


def expand(parts, basis, quads, group, target, local_rows):
    mats, unit_rows, rank = parts[0].shape
    feats = basis.shape[1]
    rows = QUAD * unit_rows
    part = pl.BlockSpec((1, unit_rows, rank), lambda m, q, g: (m, 0, 0))
    in_specs = [part] * QUAD + [pl.BlockSpec((1, feats, rank), lambda m, q, g: (m, 0, 0))]
    args = [quads, group, *parts, basis]
    aliases = {}
    if target is not None:
        in_specs.append(pl.BlockSpec(memory_space=pl.ANY))
        aliases = {len(args): 0}
        args.append(target)
    return pl.pallas_call(
        expand_kernel,
        out_shape=jax.ShapeDtypeStruct((mats, local_rows, feats), BF16),
        grid_spec=pltpu.PrefetchScalarGridSpec(
            num_scalar_prefetch=2,
            grid=(mats,),
            in_specs=in_specs,
            out_specs=pl.BlockSpec((1, rows, feats), lambda m, q, g: (m, g[0], 0)),
            scratch_shapes=[pltpu.VMEM((rows, rank), BF16)],
        ),
        input_output_aliases=aliases,
        cost_estimate=pl.CostEstimate(
            flops=2 * mats * rows * feats * rank,
            bytes_accessed=2 * mats * rows * (feats + rank),
            transcendentals=0,
        ),
        name="expand",
    )(*args)


def new_moments(first, second, grad_rows):
    new_first = 0.9 * first + 0.1 * grad_rows
    new_second = 0.999 * second + 0.001 * grad_rows * grad_rows
    return new_first, new_second


def settle_kernel(piece_of, row_of, held, *refs, pieces):
    piece_refs = refs[:pieces]
    first_ref, second_ref, first_out, second_out, rows, sem = refs[pieces:]
    m = pl.program_id(0)
    capacity, bucket_rows = rows.shape[0], rows.shape[1]

    def fetch(s, _):
        piece = piece_of[m, s]
        at = pl.multiple_of(row_of[m, s], bucket_rows)
        for i, ref in enumerate(piece_refs):

            @pl.when(piece == i)
            def _():
                pltpu.make_async_copy(ref.at[m, pl.ds(at, bucket_rows), :], rows.at[s], sem).start()

        return 0

    lax.fori_loop(0, capacity, fetch, 0)
    pltpu.make_async_copy(rows, rows, sem).wait()

    def settle(s, _):
        first, second = first_ref[0, 0, s], second_ref[0, 0, s]
        new_first, new_second = new_moments(first, second, rows[s].astype(F32))
        keep = held[m, s] > 0
        first_out[0, 0, s] = jnp.where(keep, new_first, first)
        second_out[0, 0, s] = jnp.where(keep, new_second, second)
        return 0

    lax.fori_loop(0, capacity, settle, 0)


def settle_moments(first, second, pieces, piece_of, row_of, held):
    mats, _, capacity, bucket_rows, rank = first.shape
    spec = pl.BlockSpec((1, 1, capacity, bucket_rows, rank), lambda m, *_: (m, 0, 0, 0, 0))
    return pl.pallas_call(
        functools.partial(settle_kernel, pieces=len(pieces)),
        out_shape=(
            jax.ShapeDtypeStruct(first.shape, F32),
            jax.ShapeDtypeStruct(second.shape, F32),
        ),
        grid_spec=pltpu.PrefetchScalarGridSpec(
            num_scalar_prefetch=3,
            grid=(mats,),
            in_specs=[pl.BlockSpec(memory_space=pl.ANY)] * len(pieces) + [spec, spec],
            out_specs=(spec, spec),
            scratch_shapes=[
                pltpu.VMEM((capacity, bucket_rows, rank), BF16),
                pltpu.SemaphoreType.DMA,
            ],
        ),
        cost_estimate=pl.CostEstimate(
            flops=8 * first.size, bytes_accessed=18 * first.size, transcendentals=0
        ),
        name="settle",
    )(piece_of, row_of, held, *pieces, first, second)


def adam_update(first, second, grad_rows):
    new_first, new_second = new_moments(first, second, grad_rows)
    scaled = (
        6.0 * (new_first / (1.0 - 0.9**10)) / (jnp.sqrt(new_second / (1.0 - 0.999**10)) + 1e-08)
    )
    return scaled.astype(BF16)


def shards(grads, raw_proj, bucket_owner, first_moment, second_moment):
    mats, local_rows = grads.shape[1], grads.shape[2]
    local_feats = raw_proj.shape[1]
    buckets = bucket_owner.shape[1]
    capacity = first_moment.shape[2]
    bucket_rows = local_rows // buckets
    replicas = lax.axis_size("dp")
    splits = lax.axis_size("fsdp")
    depth = replicas // QUAD
    unit_rows = local_rows // replicas
    unit_buckets = buckets // replicas
    me = lax.axis_index("dp")
    my_z, my_quad = me // QUAD, me % QUAD

    def permute(v, target):
        return lax.ppermute(v, "dp", [(i, target(i)) for i in range(replicas)])

    def to_core(v):
        return permute(v, lambda i: i ^ 1)

    def to_x(v):
        return permute(v, lambda i: i ^ 2)

    def to_z(v):
        return permute(v, lambda i: (i + QUAD) % replicas)

    quarter = local_feats // QUAD
    my_core = me % 2
    parts = [
        lax.dynamic_slice_in_dim(raw_proj, (2 * my_core + i) * quarter, quarter, 1) for i in range(2)
    ]
    my_f = lax.axis_index("fsdp")
    gram = gram_of([raw_proj])
    pieces, offsets, early, fresh = [], [my_f * local_feats], [], []
    for shift in range(1, splits):
        base = ((my_f + splits - shift) % splits) * local_feats
        for i, indices in ((0, early), (1, fresh)):
            fetched = lax.ppermute(
                parts[i], "fsdp", [(j, (j + shift) % splits) for j in range(splits)]
            )
            for piece, core in ((fetched, my_core), (to_core(fetched), 1 - my_core)):
                indices.append(len(pieces))
                pieces.append(piece)
                offsets.append(base + (2 * core + i) * quarter)
    offsets = jnp.stack(offsets).astype(jnp.int32)
    if early:
        gram = gram_of([pieces[i] for i in early], gram)

    same = bucket_owner[:, :, None] == bucket_owner[:, None, :]
    order = jnp.arange(buckets, dtype=jnp.int32)
    earlier = order[None, :] < order[:, None]
    ranks = jnp.sum(jnp.logical_and(same, earlier).astype(jnp.int32), axis=-1)
    owner_ids = jnp.stack([me ^ flip for flip in (0, 2, 1, 3)])
    local_slot = jnp.where(bucket_owner[None] == owner_ids[:, None, None], ranks[None], -1)
    slot_ids = jnp.arange(capacity, dtype=jnp.int32)
    matches = local_slot[:, :, None, :] == slot_ids[None, None, :, None]
    quad_occupied = jnp.any(matches, axis=3)
    quad_buckets = jnp.sum(jnp.where(matches, order[None, None, None, :], 0), axis=3)
    quad_counts = jnp.sum(quad_occupied.astype(jnp.int32), axis=2)
    occupied, bucket_of = quad_occupied[0], quad_buckets[0]
    quad_units = quad_buckets // unit_buckets
    steps = (my_z + depth - 1 - quad_units // QUAD) % depth
    places = steps * unit_rows + (quad_buckets % unit_buckets) * bucket_rows
    wanted = jnp.logical_and(quad_occupied, quad_units % QUAD == my_quad)
    places = jnp.where(wanted, places, -1).astype(jnp.int32)

    def unit_moments(moment):
        slots = moment[:, 0].astype(BF16)
        across = to_x(slots)
        owners = (slots, across, to_core(slots), to_core(across))
        held, rest = collect_moments(
            owners, places, quad_counts, unit_rows, (depth - 1) * unit_rows
        )
        for k in range(1, depth):
            held = to_z(held) + rest[:, (k - 1) * unit_rows : k * unit_rows]
        return held

    first_unit = unit_moments(first_moment)
    second_unit = unit_moments(second_moment)

    state = first_half([pieces[i] for i in fresh], gram)
    basis = second_half(raw_proj, pieces, offsets, state, splits * local_feats)

    send_quads = jnp.stack([my_quad ^ flip for flip in (3, 1, 2, 0)]).astype(jnp.int32)
    held = None
    for k in range(1, depth + 1):
        group = ((my_z + depth - k) % depth).astype(jnp.int32)[None]
        other, own = project(grads, basis, send_quads, group, unit_rows)
        arrived = to_core(other)
        send = (own[0].astype(F32) + arrived[0].astype(F32)).astype(BF16)
        crossed = to_x(send)
        total = own[1].astype(F32) + arrived[1].astype(F32) + crossed.astype(F32)
        if held is not None:
            total = total + to_z(held).astype(F32)
        held = total.astype(BF16)
    held, grad_rows = lax.optimization_barrier((held, total))

    def ring(unit):
        groups = []
        across = None
        half = mats // 2
        for k in range(depth):
            if 0 < k == depth - 1:
                over_z = to_z(across[half:])
                across = jnp.concatenate([to_x(unit[:half]), over_z])
            else:
                across = to_x(unit)
            core = to_core(unit)
            groups.append((unit, across, core, to_core(across)))
            if k + 1 < depth:
                unit = to_z(unit)
        return groups

    grad_groups = ring(held)
    update = adam_update(first_unit.astype(F32), second_unit.astype(F32), grad_rows)
    update_groups = ring(update)

    part_quads = jnp.stack([my_quad ^ flip for flip in (0, 2, 1, 3)]).astype(jnp.int32)
    weight_delta = None
    for k, parts in enumerate(update_groups):
        group = ((my_z + depth - k) % depth).astype(jnp.int32)[None]
        weight_delta = expand(parts, basis, part_quads, group, weight_delta, local_rows)

    unit = bucket_of // unit_buckets
    back = (my_z + depth - unit // QUAD) % depth
    flip = (unit % QUAD) ^ my_quad
    piece_of = back * QUAD + (flip % 2) * 2 + flip // 2
    row_of = (bucket_of % unit_buckets) * bucket_rows
    first_out, second_out = settle_moments(
        first_moment,
        second_moment,
        [p for parts in grad_groups for p in parts],
        piece_of.astype(jnp.int32),
        row_of.astype(jnp.int32),
        occupied.astype(jnp.int32),
    )
    return weight_delta, first_out, second_out


def solution(mesh):
    return jax.shard_map(
        shards,
        mesh=mesh,
        in_specs=(
            P("dp", None, "fsdp", None),
            P(None, "fsdp", None),
            P(None, "fsdp"),
            P(None, "fsdp", "dp", None, None),
            P(None, "fsdp", "dp", None, None),
        ),
        out_specs=(
            P(None, "fsdp", None),
            P(None, "fsdp", "dp", None, None),
            P(None, "fsdp", "dp", None, None),
        ),
        check_vma=False,
    )
```

```python
import functools

import jax
import jax.numpy as jnp
from jax import lax
from jax.experimental import pallas as pl
from jax.experimental.pallas import tpu as pltpu
from jax.sharding import PartitionSpec as P


PANEL = 8
BLOCK = 128
WIDE = 256
QUAD = 4
F32 = jnp.float32
BF16 = jnp.bfloat16


def dot_f32(a, b, dims):
    return lax.dot_general(
        a, b, (dims, ((), ())), precision=lax.Precision.HIGHEST, preferred_element_type=F32
    )


def dot_bf16(a, b, dims):
    return lax.dot_general(a, b, (dims, ((), ())), preferred_element_type=F32)


def halves(x):
    high = x.astype(BF16)
    return high, (x - high.astype(F32)).astype(BF16)


def dot_split(a, b, dims):
    (a_high, a_low), (b_high, b_low) = halves(a), halves(b)
    return (
        dot_bf16(a_low, b_high, dims)
        + dot_bf16(a_high, b_low, dims)
        + dot_bf16(a_high, b_high, dims)
    )


def thirds(x):
    first = x.astype(BF16).astype(F32)
    rest = x - first
    second = rest.astype(BF16).astype(F32)
    return first, second, rest - second


def dot_packed(a, b, dims):
    a1, a2, a3 = thirds(a)
    b1, b2, b3 = thirds(b)
    (a_dim,), (b_dim,) = dims
    left = jnp.concatenate([a1, a2, a1, a3, a2, a1], axis=a_dim).astype(BF16)
    right = jnp.concatenate([b3, b2, b2, b1, b1, b1], axis=b_dim).astype(BF16)
    return dot_bf16(left, right, dims)


def eliminate_panel(block_ref, inverse_ref, scale_ref, m, start):
    rows = block_ref[m, pl.ds(start, PANEL), :]
    inv_rows = inverse_ref[m, pl.ds(start, PANEL), :]
    sub = lax.broadcasted_iota(jnp.int32, rows.shape, 0)
    cols = [
        jnp.take_along_axis(
            rows, jnp.full(rows.shape, start + j, jnp.int32), axis=1, mode="promise_in_bounds"
        )
        for j in range(PANEL)
    ]
    recip = jnp.zeros_like(rows)
    for j in range(PANEL):
        r = 1.0 / jnp.broadcast_to(cols[j][j : j + 1, :], rows.shape)
        recip = jnp.where(sub == j, r, recip)
        if j + 1 < PANEL:
            mult = jnp.where(sub > j, cols[j] * r, 0.0)
            for k in range(j + 1, PANEL):
                cols[k] = cols[k] - mult * jnp.broadcast_to(cols[k][j : j + 1, :], rows.shape)
            rows = rows - mult * jnp.broadcast_to(rows[j : j + 1, :], rows.shape)
            inv_rows = inv_rows - mult * jnp.broadcast_to(inv_rows[j : j + 1, :], rows.shape)
    inverse_ref[m, pl.ds(start, PANEL), :] = inv_rows
    scale_ref[m, pl.ds(start, PANEL), :] = recip
    return rows, inv_rows, recip


def eliminate_block(block_ref, inverse_ref, scale_ref, mats, size):
    row_id = lax.broadcasted_iota(jnp.int32, (size, size), 0)
    lane_id = lax.broadcasted_iota(jnp.int32, (size, size), 1)
    for m in range(mats):
        inverse_ref[m] = jnp.where(row_id == lane_id, 1.0, 0.0)

    def panel(p, _):
        start = pl.multiple_of(p * PANEL, PANEL)
        done = [eliminate_panel(block_ref, inverse_ref, scale_ref, m, start) for m in range(mats)]
        below = row_id >= start + PANEL
        for m in range(mats):
            rows, inv_rows, recip = done[m]
            both = jnp.concatenate([rows, inv_rows], axis=1)
            change = dot_packed(rows * recip, both, ((0,), (0,)))
            block_ref[m] = block_ref[m] - jnp.where(below, change[:, :size], 0.0)
            inverse_ref[m] = inverse_ref[m] - jnp.where(below, change[:, size:], 0.0)
        return 0

    lax.fori_loop(0, size // PANEL, panel, 0)


def add_gram(gram, pieces, held):
    mats, rank, _ = gram.shape

    def one(m, _):
        for j in range(0, rank, WIDE):
            total = None if held is None else held[m, j:, j : j + WIDE]
            for ref in pieces:
                part = dot_f32(ref[m, :, j:], ref[m, :, j : j + WIDE], ((0,), (0,)))
                total = part if total is None else total + part
            gram[m, j:, j : j + WIDE] = total
        return 0

    lax.fori_loop(0, mats, one, 0)


def gram_kernel(*refs, pieces):
    held = refs[pieces] if len(refs) > pieces + 1 else None
    add_gram(refs[-1], refs[:pieces], held)


def gram_of(pieces, held=None):
    mats, _, rank = pieces[0].shape
    args = list(pieces) + ([] if held is None else [held])
    depth = sum(p.shape[1] for p in pieces)
    vmem = pl.BlockSpec(memory_space=pltpu.VMEM)
    return pl.pallas_call(
        functools.partial(gram_kernel, pieces=len(pieces)),
        out_shape=jax.ShapeDtypeStruct((mats, rank, rank), F32),
        in_specs=[vmem] * len(args),
        out_specs=vmem,
        cost_estimate=pl.CostEstimate(
            flops=12 * mats * depth * rank * rank,
            bytes_accessed=4 * mats * rank * (rank + depth),
            transcendentals=0,
        ),
        name="gram",
    )(*args)


def factor(gram, inv, low, block, binv, scale, size):
    mats = block.shape[0]
    n = size // BLOCK

    def sl(i):
        return slice(i * BLOCK, (i + 1) * BLOCK)

    for b in range(n):
        below = (b + 1) * BLOCK
        for m in range(mats):
            block[m] = gram[m, sl(b), sl(b)]
        eliminate_block(block, binv, scale, mats, BLOCK)
        for m in range(mats):
            d_inv = binv[m] * jnp.sqrt(scale[m])
            inv[m, sl(b), sl(b)] = d_inv
            if b > 0:
                acc = dot_packed(
                    low[m, sl(b), : b * BLOCK], inv[m, : b * BLOCK, : b * BLOCK], ((1,), (0,))
                )
                inv[m, sl(b), : b * BLOCK] = -dot_packed(d_inv, acc, ((1,), (0,)))
            if b + 1 < n:
                low[m, below:size, sl(b)] = dot_packed(gram[m, below:size, sl(b)], d_inv, ((1,), (1,)))
                inv[m, sl(b), below:size] = jnp.zeros((BLOCK, size - below), F32)
                for j in range(b + 1, n):
                    gram[m, j * BLOCK : size, sl(j)] = gram[m, j * BLOCK : size, sl(j)] - dot_packed(
                        low[m, j * BLOCK : size, sl(b)], low[m, sl(j), sl(b)], ((1,), (1,))
                    )


def first_half_kernel(*refs, pieces):
    held, inv_out, low_out, rest_out, gram, low, block, binv, scale = refs[pieces:]
    mats, rank, _ = gram.shape
    half = rank // 2
    add_gram(gram, refs[:pieces], held)
    factor(gram, inv_out, low, block, binv, scale, half)
    for m in range(mats):
        side = dot_f32(gram[m, half:, :half], inv_out[m], ((1,), (1,)))
        low_out[m] = side
        rest_out[m] = gram[m, half:, half:] - dot_f32(side, side, ((1,), (1,)))


def second_half_kernel(offsets, *refs, pieces):
    own_ref = refs[0]
    piece_refs = refs[1 : 1 + pieces]
    inv_ref, side_ref, rest_ref, basis_ref = refs[1 + pieces : 5 + pieces]
    raw, gram, inv, low, block, binv, scale = refs[5 + pieces :]
    mats, _, rank = raw.shape
    half = rank // 2
    for i, ref in enumerate((own_ref, *piece_refs)):
        at = pl.multiple_of(offsets[i], 8)
        raw[:, pl.ds(at, ref.shape[1]), :] = ref[...]
    gram[...] = rest_ref[...]
    factor(gram, inv, low, block, binv, scale, half)

    def bases(m, _):
        acc = dot_f32(side_ref[m], inv_ref[m], ((1,), (0,)))
        left = -dot_f32(inv[m], acc, ((1,), (0,)))
        basis_ref[m, :, :half] = dot_split(raw[m, :, :half], inv_ref[m], ((1,), (1,))).astype(BF16)
        both = jnp.concatenate([left, inv[m]], axis=1)
        basis_ref[m, :, half:] = dot_split(raw[m], both, ((1,), (1,))).astype(BF16)
        return 0

    lax.fori_loop(0, mats, bases, 0)


def first_half(fresh, held):
    mats, rank, _ = held.shape
    half = rank // 2
    vmem = pl.BlockSpec(memory_space=pltpu.VMEM)
    state = jax.ShapeDtypeStruct((mats, half, half), F32)
    return pl.pallas_call(
        functools.partial(first_half_kernel, pieces=len(fresh)),
        out_shape=(state,) * 3,
        in_specs=[vmem] * (len(fresh) + 1),
        out_specs=(vmem,) * 3,
        scratch_shapes=[
            pltpu.VMEM((mats, rank, rank), F32),
            pltpu.VMEM((mats, half, half), F32),
        ]
        + [pltpu.VMEM((mats, BLOCK, BLOCK), F32)] * 3,
        cost_estimate=pl.CostEstimate(
            flops=20_000_000_000, bytes_accessed=4 * mats * rank * rank, transcendentals=0
        ),
        name="first_half",
    )(*fresh, held)


def second_half(own, pieces, offsets, state, feats):
    mats, _, rank = own.shape
    half = rank // 2
    vmem = pl.BlockSpec(memory_space=pltpu.VMEM)
    smem = pl.BlockSpec(memory_space=pltpu.SMEM)
    return pl.pallas_call(
        functools.partial(second_half_kernel, pieces=len(pieces)),
        out_shape=jax.ShapeDtypeStruct((mats, feats, rank), BF16),
        in_specs=[smem] + [vmem] * (4 + len(pieces)),
        out_specs=vmem,
        scratch_shapes=[pltpu.VMEM((mats, feats, rank), F32)]
        + [pltpu.VMEM((mats, half, half), F32)] * 3
        + [pltpu.VMEM((mats, BLOCK, BLOCK), F32)] * 3,
        cost_estimate=pl.CostEstimate(
            flops=20_000_000_000, bytes_accessed=6 * mats * feats * rank, transcendentals=0
        ),
        name="second_half",
    )(offsets, own, *pieces, *state)


def collect_kernel(places, counts, *refs):
    m = pl.program_id(0)
    owner_refs, group_refs = refs[:QUAD], refs[QUAD:]
    bucket_rows, unit_rows = owner_refs[0].shape[2], group_refs[0].shape[1]
    for ref in group_refs:
        ref[...] = jnp.zeros(ref.shape, BF16)
    for i, owner_ref in enumerate(owner_refs):

        def pick(s, _):
            place = places[i, m, s]

            @pl.when(place >= 0)
            def _():
                group = place // unit_rows
                at = pl.multiple_of(place - group * unit_rows, bucket_rows)
                for k, ref in enumerate(group_refs):

                    @pl.when(group == k)
                    def _():
                        ref[0, pl.ds(at, bucket_rows), :] = owner_ref[0, s]

            return 0

        lax.fori_loop(0, counts[i, m], pick, 0)


def collect_moments(owners, places, counts, depth, unit_rows):
    mats, capacity, bucket_rows, rank = owners[0].shape
    slots = pl.BlockSpec((1, capacity, bucket_rows, rank), lambda m, *_: (m, 0, 0, 0))
    group = pl.BlockSpec((1, unit_rows, rank), lambda m, *_: (m, 0, 0))
    return pl.pallas_call(
        collect_kernel,
        out_shape=(jax.ShapeDtypeStruct((mats, unit_rows, rank), BF16),) * depth,
        grid_spec=pltpu.PrefetchScalarGridSpec(
            num_scalar_prefetch=2,
            grid=(mats,),
            in_specs=[slots] * QUAD,
            out_specs=(group,) * depth,
        ),
        cost_estimate=pl.CostEstimate(
            flops=0, bytes_accessed=4 * QUAD * owners[0].size, transcendentals=0
        ),
        name="collect",
    )(places, counts, *owners)


def project_kernel(quads, group, grads_ref, basis_ref, other_ref, own_ref, result):
    unit_rows = other_ref.shape[2]
    result[...] = dot_bf16(grads_ref[0, 0], basis_ref[0], ((1,), (0,))).astype(BF16)
    for i, ref in ((0, other_ref), (1, other_ref), (2, own_ref), (3, own_ref)):
        at = pl.multiple_of(quads[i] * unit_rows, unit_rows)
        ref[i % 2, 0] = result[pl.ds(at, unit_rows), :]


def project(grads, basis, quads, group, unit_rows):
    _, mats, _, feats = grads.shape
    rank = basis.shape[2]
    rows = QUAD * unit_rows
    out = jax.ShapeDtypeStruct((2, mats, unit_rows, rank), BF16)
    out_spec = pl.BlockSpec((2, 1, unit_rows, rank), lambda m, q, g: (0, m, 0, 0))
    return pl.pallas_call(
        project_kernel,
        out_shape=(out, out),
        grid_spec=pltpu.PrefetchScalarGridSpec(
            num_scalar_prefetch=2,
            grid=(mats,),
            in_specs=[
                pl.BlockSpec((1, 1, rows, feats), lambda m, q, g: (0, m, g[0], 0)),
                pl.BlockSpec((1, feats, rank), lambda m, q, g: (m, 0, 0)),
            ],
            out_specs=(out_spec, out_spec),
            scratch_shapes=[pltpu.VMEM((rows, rank), BF16)],
        ),
        cost_estimate=pl.CostEstimate(
            flops=2 * mats * rows * feats * rank,
            bytes_accessed=2 * mats * rows * (feats + rank),
            transcendentals=0,
        ),
        name="project",
    )(quads, group, grads, basis)


def expand_kernel(quads, group, *refs, parts):
    basis_ref = refs[parts]
    out_ref, joined = refs[-2:]
    m = pl.program_id(0)
    unit_rows = refs[0].shape[1]
    used = 0
    for i in range(QUAD):
        at = pl.multiple_of(quads[i] * unit_rows, unit_rows)
        if parts == QUAD or i % 2 == 0:
            joined[pl.ds(at, unit_rows), :] = refs[used][0]
            used += 1
        else:
            low, high = refs[used], refs[used + 1]
            used += 2
            joined[pl.ds(at, unit_rows), :] = jnp.where(m < pl.num_programs(0) // 2, low[0], high[0])
    out_ref[0] = dot_bf16(joined[...], basis_ref[0], ((1,), (1,))).astype(BF16)


def expand(parts, basis, quads, group, target, local_rows):
    mats, feats, rank = basis.shape
    unit_rows = parts[0][0].shape[1]
    rows = QUAD * unit_rows
    block = (1, unit_rows, rank)
    half = mats // 2
    in_specs, args = [], [quads, group]
    for part in parts:
        if len(part) == 1:
            in_specs.append(pl.BlockSpec(block, lambda m, q, g: (m, 0, 0)))
        else:
            in_specs.append(pl.BlockSpec(block, lambda m, q, g: (jnp.minimum(m, half - 1), 0, 0)))
            in_specs.append(pl.BlockSpec(block, lambda m, q, g: (jnp.maximum(m - half, 0), 0, 0)))
        args += part
    pieces = len(in_specs)
    in_specs.append(pl.BlockSpec((1, feats, rank), lambda m, q, g: (m, 0, 0)))
    args.append(basis)
    aliases = {}
    if target is not None:
        in_specs.append(pl.BlockSpec(memory_space=pl.ANY))
        aliases = {len(args): 0}
        args.append(target)
    return pl.pallas_call(
        functools.partial(expand_kernel, parts=pieces),
        out_shape=jax.ShapeDtypeStruct((mats, local_rows, feats), BF16),
        grid_spec=pltpu.PrefetchScalarGridSpec(
            num_scalar_prefetch=2,
            grid=(mats,),
            in_specs=in_specs,
            out_specs=pl.BlockSpec((1, rows, feats), lambda m, q, g: (m, g[0], 0)),
            scratch_shapes=[pltpu.VMEM((rows, rank), BF16)],
        ),
        input_output_aliases=aliases,
        cost_estimate=pl.CostEstimate(
            flops=2 * mats * rows * feats * rank,
            bytes_accessed=2 * mats * rows * (feats + rank),
            transcendentals=0,
        ),
        name="expand",
    )(*args)


def new_moments(first, second, grad_rows):
    new_first = 0.9 * first + 0.1 * grad_rows
    new_second = 0.999 * second + 0.001 * grad_rows * grad_rows
    return new_first, new_second


def settle_kernel(piece_of, row_of, held, *refs, pieces):
    count = sum(pieces)
    first_ref, second_ref, first_out, second_out, rows, sem = refs[count:]
    m = pl.program_id(0)
    half = pl.num_programs(0) // 2
    sources = []
    for i, parts in enumerate(pieces):
        at = sum(pieces[:i])
        if parts == 1:
            sources.append((i, refs[at], None, 0))
        else:
            sources += [(i, refs[at], m < half, 0), (i, refs[at + 1], m >= half, half)]
    capacity, bucket_rows = rows.shape[0], rows.shape[1]

    def fetch(s, _):
        piece = piece_of[m, s]
        at = pl.multiple_of(row_of[m, s], bucket_rows)
        for i, ref, mine, base in sources:

            @pl.when(piece == i if mine is None else jnp.logical_and(piece == i, mine))
            def _():
                source = ref.at[m - base, pl.ds(at, bucket_rows), :]
                pltpu.make_async_copy(source, rows.at[s], sem).start()

        return 0

    lax.fori_loop(0, capacity, fetch, 0)
    pltpu.make_async_copy(rows, rows, sem).wait()

    def settle(s, _):
        first, second = first_ref[0, 0, s], second_ref[0, 0, s]
        new_first, new_second = new_moments(first, second, rows[s].astype(F32))
        keep = held[m, s] > 0
        first_out[0, 0, s] = jnp.where(keep, new_first, first)
        second_out[0, 0, s] = jnp.where(keep, new_second, second)
        return 0

    lax.fori_loop(0, capacity, settle, 0)


def settle_moments(first, second, pieces, piece_of, row_of, held):
    mats, _, capacity, bucket_rows, rank = first.shape
    spec = pl.BlockSpec((1, 1, capacity, bucket_rows, rank), lambda m, *_: (m, 0, 0, 0, 0))
    return pl.pallas_call(
        functools.partial(settle_kernel, pieces=tuple(len(p) for p in pieces)),
        out_shape=(
            jax.ShapeDtypeStruct(first.shape, F32),
            jax.ShapeDtypeStruct(second.shape, F32),
        ),
        grid_spec=pltpu.PrefetchScalarGridSpec(
            num_scalar_prefetch=3,
            grid=(mats,),
            in_specs=[pl.BlockSpec(memory_space=pl.ANY)] * sum(len(p) for p in pieces) + [spec, spec],
            out_specs=(spec, spec),
            scratch_shapes=[
                pltpu.VMEM((capacity, bucket_rows, rank), BF16),
                pltpu.SemaphoreType.DMA,
            ],
        ),
        cost_estimate=pl.CostEstimate(
            flops=8 * first.size, bytes_accessed=18 * first.size, transcendentals=0
        ),
        name="settle",
    )(piece_of, row_of, held, *(v for p in pieces for v in p), first, second)


def adam_update(first, second, grad_rows):
    new_first, new_second = new_moments(first, second, grad_rows)
    scaled = (
        6.0 * (new_first / (1.0 - 0.9**10)) / (jnp.sqrt(new_second / (1.0 - 0.999**10)) + 1e-08)
    )
    return scaled.astype(BF16)


def shards(grads, raw_proj, bucket_owner, first_moment, second_moment):
    mats, local_rows = grads.shape[1], grads.shape[2]
    local_feats = raw_proj.shape[1]
    buckets = bucket_owner.shape[1]
    capacity = first_moment.shape[2]
    bucket_rows = local_rows // buckets
    replicas = lax.axis_size("dp")
    splits = lax.axis_size("fsdp")
    depth = replicas // QUAD
    unit_rows = local_rows // replicas
    unit_buckets = buckets // replicas
    me = lax.axis_index("dp")
    my_z, my_quad = me // QUAD, me % QUAD

    def permute(v, target):
        return lax.ppermute(v, "dp", [(i, target(i)) for i in range(replicas)])

    def to_core(v):
        return permute(v, lambda i: i ^ 1)

    def to_x(v):
        return permute(v, lambda i: i ^ 2)

    def to_z(v, layers=1):
        return permute(v, lambda i: (i + layers * QUAD) % replicas)

    quarter = local_feats // QUAD
    my_core = me % 2
    parts = [
        lax.dynamic_slice_in_dim(raw_proj, (2 * my_core + i) * quarter, quarter, 1) for i in range(2)
    ]
    my_f = lax.axis_index("fsdp")
    gram = gram_of([raw_proj])
    pieces, offsets, early, fresh = [], [my_f * local_feats], [], []
    for shift in range(1, splits):
        base = ((my_f + splits - shift) % splits) * local_feats
        for i, indices in ((0, early), (1, fresh)):
            fetched = lax.ppermute(
                parts[i], "fsdp", [(j, (j + shift) % splits) for j in range(splits)]
            )
            for piece, core in ((fetched, my_core), (to_core(fetched), 1 - my_core)):
                indices.append(len(pieces))
                pieces.append(piece)
                offsets.append(base + (2 * core + i) * quarter)
    offsets = jnp.stack(offsets).astype(jnp.int32)
    if early:
        gram = gram_of([pieces[i] for i in early], gram)

    same = bucket_owner[:, :, None] == bucket_owner[:, None, :]
    order = jnp.arange(buckets, dtype=jnp.int32)
    earlier = order[None, :] < order[:, None]
    ranks = jnp.sum(jnp.logical_and(same, earlier).astype(jnp.int32), axis=-1)
    owner_ids = jnp.stack([me ^ flip for flip in (0, 2, 1, 3)])
    local_slot = jnp.where(bucket_owner[None] == owner_ids[:, None, None], ranks[None], -1)
    slot_ids = jnp.arange(capacity, dtype=jnp.int32)
    matches = local_slot[:, :, None, :] == slot_ids[None, None, :, None]
    quad_occupied = jnp.any(matches, axis=3)
    quad_buckets = jnp.sum(jnp.where(matches, order[None, None, None, :], 0), axis=3)
    quad_counts = jnp.sum(quad_occupied.astype(jnp.int32), axis=2)
    occupied, bucket_of = quad_occupied[0], quad_buckets[0]
    quad_units = quad_buckets // unit_buckets
    steps = (quad_units // QUAD + depth - my_z) % depth
    places = steps * unit_rows + (quad_buckets % unit_buckets) * bucket_rows
    wanted = jnp.logical_and(quad_occupied, quad_units % QUAD == my_quad)
    places = jnp.where(wanted, places, -1).astype(jnp.int32)

    def unit_moments(moment):
        slots = moment[:, 0].astype(BF16)
        across = to_x(slots)
        owners = (slots, across, to_core(slots), to_core(across))
        groups = collect_moments(owners, places, quad_counts, depth, unit_rows)
        total = groups[0]
        for k in range(1, depth):
            total = total + to_z(groups[k], k)
        return total

    first_unit, second_unit = unit_moments(first_moment), unit_moments(second_moment)
    first_unit, second_unit = lax.optimization_barrier((first_unit, second_unit))

    state = first_half([pieces[i] for i in fresh], gram)
    basis = second_half(raw_proj, pieces, offsets, state, splits * local_feats)

    send_quads = jnp.stack([my_quad ^ flip for flip in (3, 1, 2, 0)]).astype(jnp.int32)
    held = None
    for k in range(1, depth + 1):
        group = ((my_z + depth - k) % depth).astype(jnp.int32)[None]
        other, own = project(grads, basis, send_quads, group, unit_rows)
        arrived = to_core(other)
        send = (own[0].astype(F32) + arrived[0].astype(F32)).astype(BF16)
        crossed = to_x(send)
        total = own[1].astype(F32) + arrived[1].astype(F32) + crossed.astype(F32)
        if held is not None:
            total = total + to_z(held).astype(F32)
        held = total.astype(BF16)
    held, grad_rows = lax.optimization_barrier((held, total))

    def ring(unit):
        groups = []
        across = (None,)
        half = mats // 2
        for k in range(depth):
            if 0 < k == depth - 1:
                over_z = to_z(across[0][half:])
                across = (to_x(unit[:half]), over_z)
            else:
                across = (to_x(unit),)
            core = to_core(unit)
            both = tuple(to_core(v) for v in across)
            groups.append(((unit,), across, (core,), both))
            if k + 1 < depth:
                unit = to_z(unit)
        return groups

    grad_groups = ring(held)
    update = adam_update(first_unit.astype(F32), second_unit.astype(F32), grad_rows)
    update_groups = ring(update)

    part_quads = jnp.stack([my_quad ^ flip for flip in (0, 2, 1, 3)]).astype(jnp.int32)
    weight_delta = None
    for k, parts in enumerate(update_groups):
        group = ((my_z + depth - k) % depth).astype(jnp.int32)[None]
        weight_delta = expand(parts, basis, part_quads, group, weight_delta, local_rows)

    unit = bucket_of // unit_buckets
    back = (my_z + depth - unit // QUAD) % depth
    flip = (unit % QUAD) ^ my_quad
    piece_of = back * QUAD + (flip % 2) * 2 + flip // 2
    row_of = (bucket_of % unit_buckets) * bucket_rows
    first_out, second_out = settle_moments(
        first_moment,
        second_moment,
        [p for parts in grad_groups for p in parts],
        piece_of.astype(jnp.int32),
        row_of.astype(jnp.int32),
        occupied.astype(jnp.int32),
    )
    return weight_delta, first_out, second_out


def solution(mesh):
    return jax.shard_map(
        shards,
        mesh=mesh,
        in_specs=(
            P("dp", None, "fsdp", None),
            P(None, "fsdp", None),
            P(None, "fsdp"),
            P(None, "fsdp", "dp", None, None),
            P(None, "fsdp", "dp", None, None),
        ),
        out_specs=(
            P(None, "fsdp", None),
            P(None, "fsdp", "dp", None, None),
            P(None, "fsdp", "dp", None, None),
        ),
        check_vma=False,
    )
```

```python
import functools

import jax
import jax.numpy as jnp
from jax import lax
from jax.experimental import pallas as pl
from jax.experimental.pallas import tpu as pltpu
from jax.sharding import PartitionSpec as P


PANEL = 8
BLOCK = 128
WIDE = 256
QUAD = 4
F32 = jnp.float32
BF16 = jnp.bfloat16


def dot_f32(a, b, dims):
    return lax.dot_general(
        a, b, (dims, ((), ())), precision=lax.Precision.HIGHEST, preferred_element_type=F32
    )


def dot_bf16(a, b, dims):
    return lax.dot_general(a, b, (dims, ((), ())), preferred_element_type=F32)


def halves(x):
    high = x.astype(BF16)
    return high, (x - high.astype(F32)).astype(BF16)


def dot_split(a, b, dims):
    (a_high, a_low), (b_high, b_low) = halves(a), halves(b)
    return (
        dot_bf16(a_low, b_high, dims)
        + dot_bf16(a_high, b_low, dims)
        + dot_bf16(a_high, b_high, dims)
    )


def thirds(x):
    first = x.astype(BF16).astype(F32)
    rest = x - first
    second = rest.astype(BF16).astype(F32)
    return first, second, rest - second


def dot_packed(a, b, dims):
    a1, a2, a3 = thirds(a)
    b1, b2, b3 = thirds(b)
    (a_dim,), (b_dim,) = dims
    left = jnp.concatenate([a1, a2, a1, a3, a2, a1], axis=a_dim).astype(BF16)
    right = jnp.concatenate([b3, b2, b2, b1, b1, b1], axis=b_dim).astype(BF16)
    return dot_bf16(left, right, dims)


def eliminate_panel(block_ref, inverse_ref, scale_ref, m, start):
    rows = block_ref[m, pl.ds(start, PANEL), :]
    inv_rows = inverse_ref[m, pl.ds(start, PANEL), :]
    sub = lax.broadcasted_iota(jnp.int32, rows.shape, 0)
    cols = [
        jnp.take_along_axis(
            rows, jnp.full(rows.shape, start + j, jnp.int32), axis=1, mode="promise_in_bounds"
        )
        for j in range(PANEL)
    ]
    recip = jnp.zeros_like(rows)
    for j in range(PANEL):
        r = 1.0 / jnp.broadcast_to(cols[j][j : j + 1, :], rows.shape)
        recip = jnp.where(sub == j, r, recip)
        if j + 1 < PANEL:
            mult = jnp.where(sub > j, cols[j] * r, 0.0)
            for k in range(j + 1, PANEL):
                cols[k] = cols[k] - mult * jnp.broadcast_to(cols[k][j : j + 1, :], rows.shape)
            rows = rows - mult * jnp.broadcast_to(rows[j : j + 1, :], rows.shape)
            inv_rows = inv_rows - mult * jnp.broadcast_to(inv_rows[j : j + 1, :], rows.shape)
    inverse_ref[m, pl.ds(start, PANEL), :] = inv_rows
    scale_ref[m, pl.ds(start, PANEL), :] = recip
    return rows, inv_rows, recip


def eliminate_block(block_ref, inverse_ref, scale_ref, mats, size):
    row_id = lax.broadcasted_iota(jnp.int32, (size, size), 0)
    lane_id = lax.broadcasted_iota(jnp.int32, (size, size), 1)
    for m in range(mats):
        inverse_ref[m] = jnp.where(row_id == lane_id, 1.0, 0.0)

    def panel(p, _):
        start = pl.multiple_of(p * PANEL, PANEL)
        done = [eliminate_panel(block_ref, inverse_ref, scale_ref, m, start) for m in range(mats)]
        below = row_id >= start + PANEL
        for m in range(mats):
            rows, inv_rows, recip = done[m]
            both = jnp.concatenate([rows, inv_rows], axis=1)
            change = dot_packed(rows * recip, both, ((0,), (0,)))
            block_ref[m] = block_ref[m] - jnp.where(below, change[:, :size], 0.0)
            inverse_ref[m] = inverse_ref[m] - jnp.where(below, change[:, size:], 0.0)
        return 0

    lax.fori_loop(0, size // PANEL, panel, 0)


def add_gram(gram, pieces, held):
    mats, rank, _ = gram.shape

    def one(m, _):
        for j in range(0, rank, WIDE):
            total = None if held is None else held[m, j:, j : j + WIDE]
            for ref in pieces:
                part = dot_f32(ref[m, :, j:], ref[m, :, j : j + WIDE], ((0,), (0,)))
                total = part if total is None else total + part
            gram[m, j:, j : j + WIDE] = total
        return 0

    lax.fori_loop(0, mats, one, 0)


def gram_kernel(*refs, pieces):
    held = refs[pieces] if len(refs) > pieces + 1 else None
    add_gram(refs[-1], refs[:pieces], held)


def gram_of(pieces, held=None):
    mats, _, rank = pieces[0].shape
    args = list(pieces) + ([] if held is None else [held])
    depth = sum(p.shape[1] for p in pieces)
    vmem = pl.BlockSpec(memory_space=pltpu.VMEM)
    return pl.pallas_call(
        functools.partial(gram_kernel, pieces=len(pieces)),
        out_shape=jax.ShapeDtypeStruct((mats, rank, rank), F32),
        in_specs=[vmem] * len(args),
        out_specs=vmem,
        cost_estimate=pl.CostEstimate(
            flops=12 * mats * depth * rank * rank,
            bytes_accessed=4 * mats * rank * (rank + depth),
            transcendentals=0,
        ),
        name="gram",
    )(*args)


def factor(gram, inv, low, block, binv, scale, size):
    mats = block.shape[0]
    n = size // BLOCK

    def sl(i):
        return slice(i * BLOCK, (i + 1) * BLOCK)

    for b in range(n):
        below = (b + 1) * BLOCK
        for m in range(mats):
            block[m] = gram[m, sl(b), sl(b)]
        eliminate_block(block, binv, scale, mats, BLOCK)
        for m in range(mats):
            d_inv = binv[m] * jnp.sqrt(scale[m])
            inv[m, sl(b), sl(b)] = d_inv
            if b > 0:
                acc = dot_packed(
                    low[m, sl(b), : b * BLOCK], inv[m, : b * BLOCK, : b * BLOCK], ((1,), (0,))
                )
                inv[m, sl(b), : b * BLOCK] = -dot_packed(d_inv, acc, ((1,), (0,)))
            if b + 1 < n:
                low[m, below:size, sl(b)] = dot_packed(gram[m, below:size, sl(b)], d_inv, ((1,), (1,)))
                inv[m, sl(b), below:size] = jnp.zeros((BLOCK, size - below), F32)
                for j in range(b + 1, n):
                    gram[m, j * BLOCK : size, sl(j)] = gram[m, j * BLOCK : size, sl(j)] - dot_packed(
                        low[m, j * BLOCK : size, sl(b)], low[m, sl(j), sl(b)], ((1,), (1,))
                    )


def first_half_kernel(*refs, pieces):
    held, inv_out, low_out, rest_out, gram, low, block, binv, scale = refs[pieces:]
    mats, rank, _ = gram.shape
    half = rank // 2
    add_gram(gram, refs[:pieces], held)
    factor(gram, inv_out, low, block, binv, scale, half)
    for m in range(mats):
        side = dot_f32(gram[m, half:, :half], inv_out[m], ((1,), (1,)))
        low_out[m] = side
        rest_out[m] = gram[m, half:, half:] - dot_f32(side, side, ((1,), (1,)))


def second_half_kernel(offsets, *refs, pieces):
    own_ref = refs[0]
    piece_refs = refs[1 : 1 + pieces]
    inv_ref, side_ref, rest_ref, basis_ref = refs[1 + pieces : 5 + pieces]
    raw, gram, inv, low, block, binv, scale = refs[5 + pieces :]
    mats, _, rank = raw.shape
    half = rank // 2
    for i, ref in enumerate((own_ref, *piece_refs)):
        at = pl.multiple_of(offsets[i], 8)
        raw[:, pl.ds(at, ref.shape[1]), :] = ref[...]
    gram[...] = rest_ref[...]
    factor(gram, inv, low, block, binv, scale, half)

    def bases(m, _):
        acc = dot_f32(side_ref[m], inv_ref[m], ((1,), (0,)))
        left = -dot_f32(inv[m], acc, ((1,), (0,)))
        basis_ref[m, :, :half] = dot_split(raw[m, :, :half], inv_ref[m], ((1,), (1,))).astype(BF16)
        both = jnp.concatenate([left, inv[m]], axis=1)
        basis_ref[m, :, half:] = dot_split(raw[m], both, ((1,), (1,))).astype(BF16)
        return 0

    lax.fori_loop(0, mats, bases, 0)


def first_half(fresh, held):
    mats, rank, _ = held.shape
    half = rank // 2
    vmem = pl.BlockSpec(memory_space=pltpu.VMEM)
    state = jax.ShapeDtypeStruct((mats, half, half), F32)
    return pl.pallas_call(
        functools.partial(first_half_kernel, pieces=len(fresh)),
        out_shape=(state,) * 3,
        in_specs=[vmem] * (len(fresh) + 1),
        out_specs=(vmem,) * 3,
        scratch_shapes=[
            pltpu.VMEM((mats, rank, rank), F32),
            pltpu.VMEM((mats, half, half), F32),
        ]
        + [pltpu.VMEM((mats, BLOCK, BLOCK), F32)] * 3,
        cost_estimate=pl.CostEstimate(
            flops=20_000_000_000, bytes_accessed=4 * mats * rank * rank, transcendentals=0
        ),
        name="first_half",
    )(*fresh, held)


def second_half(own, pieces, offsets, state, feats):
    mats, _, rank = own.shape
    half = rank // 2
    vmem = pl.BlockSpec(memory_space=pltpu.VMEM)
    smem = pl.BlockSpec(memory_space=pltpu.SMEM)
    return pl.pallas_call(
        functools.partial(second_half_kernel, pieces=len(pieces)),
        out_shape=jax.ShapeDtypeStruct((mats, feats, rank), BF16),
        in_specs=[smem] + [vmem] * (4 + len(pieces)),
        out_specs=vmem,
        scratch_shapes=[pltpu.VMEM((mats, feats, rank), F32)]
        + [pltpu.VMEM((mats, half, half), F32)] * 3
        + [pltpu.VMEM((mats, BLOCK, BLOCK), F32)] * 3,
        cost_estimate=pl.CostEstimate(
            flops=20_000_000_000, bytes_accessed=6 * mats * feats * rank, transcendentals=0
        ),
        name="second_half",
    )(offsets, own, *pieces, *state)


def collect_kernel(places, counts, *refs):
    m = pl.program_id(0)
    owner_refs, group_refs = refs[:QUAD], refs[QUAD:]
    bucket_rows, unit_rows = owner_refs[0].shape[2], group_refs[0].shape[1]
    for ref in group_refs:
        ref[...] = jnp.zeros(ref.shape, BF16)
    for i, owner_ref in enumerate(owner_refs):

        def pick(s, _):
            place = places[i, m, s]

            @pl.when(place >= 0)
            def _():
                group = place // unit_rows
                at = pl.multiple_of(place - group * unit_rows, bucket_rows)
                for k, ref in enumerate(group_refs):

                    @pl.when(group == k)
                    def _():
                        ref[0, pl.ds(at, bucket_rows), :] = owner_ref[0, s]

            return 0

        lax.fori_loop(0, counts[i, m], pick, 0)


def collect_moments(owners, places, counts, depth, unit_rows):
    mats, capacity, bucket_rows, rank = owners[0].shape
    slots = pl.BlockSpec((1, capacity, bucket_rows, rank), lambda m, *_: (m, 0, 0, 0))
    group = pl.BlockSpec((1, unit_rows, rank), lambda m, *_: (m, 0, 0))
    return pl.pallas_call(
        collect_kernel,
        out_shape=(jax.ShapeDtypeStruct((mats, unit_rows, rank), BF16),) * depth,
        grid_spec=pltpu.PrefetchScalarGridSpec(
            num_scalar_prefetch=2,
            grid=(mats,),
            in_specs=[slots] * QUAD,
            out_specs=(group,) * depth,
        ),
        cost_estimate=pl.CostEstimate(
            flops=0, bytes_accessed=4 * QUAD * owners[0].size, transcendentals=0
        ),
        name="collect",
    )(places, counts, *owners)


def project_kernel(quads, where, grads_ref, own_basis, core_basis, other_ref, own_ref, result):
    unit_rows = other_ref.shape[2]
    for g, basis_ref in enumerate((own_basis, core_basis)):

        @pl.when(pl.program_id(0) == g)
        def _():
            result[...] = dot_bf16(grads_ref[0, 0], basis_ref[0], ((1,), (0,))).astype(BF16)

    for i, ref in ((0, other_ref), (1, other_ref), (2, own_ref), (3, own_ref)):
        at = pl.multiple_of(quads[i] * unit_rows, unit_rows)
        ref[i % 2, 0] = result[pl.ds(at, unit_rows), :]


def project(grads, bases, quads, where, unit_rows):
    _, mats, _, feats = grads.shape
    rank = bases[0].shape[2]
    rows = QUAD * unit_rows
    out = jax.ShapeDtypeStruct((2, mats, unit_rows, rank), BF16)
    out_spec = pl.BlockSpec((2, 1, unit_rows, rank), lambda g, q, w: (0, g ^ w[1], 0, 0))
    basis_spec = pl.BlockSpec((1, feats, rank), lambda g, q, w: (0, 0, 0))
    return pl.pallas_call(
        project_kernel,
        out_shape=(out, out),
        grid_spec=pltpu.PrefetchScalarGridSpec(
            num_scalar_prefetch=2,
            grid=(mats,),
            in_specs=[
                pl.BlockSpec((1, 1, rows, feats), lambda g, q, w: (0, g ^ w[1], w[0], 0)),
                basis_spec,
                basis_spec,
            ],
            out_specs=(out_spec, out_spec),
            scratch_shapes=[pltpu.VMEM((rows, rank), BF16)],
        ),
        cost_estimate=pl.CostEstimate(
            flops=2 * mats * rows * feats * rank,
            bytes_accessed=2 * mats * rows * (feats + rank),
            transcendentals=0,
        ),
        name="project",
    )(quads, where, grads, *bases)


def expand_kernel(quads, where, *refs, parts):
    out_ref, joined = refs[-2:]
    m = pl.program_id(0) ^ where[1]
    unit_rows = refs[0].shape[1]
    used = 0
    for i in range(QUAD):
        at = pl.multiple_of(quads[i] * unit_rows, unit_rows)
        if parts == QUAD or i % 2 == 0:
            joined[pl.ds(at, unit_rows), :] = refs[used][0]
            used += 1
        else:
            low, high = refs[used], refs[used + 1]
            used += 2
            joined[pl.ds(at, unit_rows), :] = jnp.where(m < pl.num_programs(0) // 2, low[0], high[0])
    for g, basis_ref in enumerate(refs[parts : parts + 2]):

        @pl.when(pl.program_id(0) == g)
        def _():
            out_ref[0] = dot_bf16(joined[...], basis_ref[0], ((1,), (1,))).astype(BF16)


def expand(parts, bases, quads, where, target, mats, local_rows):
    _, feats, rank = bases[0].shape
    unit_rows = parts[0][0].shape[1]
    rows = QUAD * unit_rows
    block = (1, unit_rows, rank)
    half = mats // 2
    in_specs, args = [], [quads, where]
    for part in parts:
        if len(part) == 1:
            in_specs.append(pl.BlockSpec(block, lambda g, q, w: (g ^ w[1], 0, 0)))
        else:
            in_specs.append(pl.BlockSpec(block, lambda g, q, w: (jnp.minimum(g ^ w[1], half - 1), 0, 0)))
            in_specs.append(pl.BlockSpec(block, lambda g, q, w: (jnp.maximum((g ^ w[1]) - half, 0), 0, 0)))
        args += part
    pieces = len(in_specs)
    in_specs += [pl.BlockSpec((1, feats, rank), lambda g, q, w: (0, 0, 0))] * 2
    args += bases
    aliases = {}
    if target is not None:
        in_specs.append(pl.BlockSpec(memory_space=pl.ANY))
        aliases = {len(args): 0}
        args.append(target)
    return pl.pallas_call(
        functools.partial(expand_kernel, parts=pieces),
        out_shape=jax.ShapeDtypeStruct((mats, local_rows, feats), BF16),
        grid_spec=pltpu.PrefetchScalarGridSpec(
            num_scalar_prefetch=2,
            grid=(mats,),
            in_specs=in_specs,
            out_specs=pl.BlockSpec((1, rows, feats), lambda g, q, w: (g ^ w[1], w[0], 0)),
            scratch_shapes=[pltpu.VMEM((rows, rank), BF16)],
        ),
        input_output_aliases=aliases,
        cost_estimate=pl.CostEstimate(
            flops=2 * mats * rows * feats * rank,
            bytes_accessed=2 * mats * rows * (feats + rank),
            transcendentals=0,
        ),
        name="expand",
    )(*args)


def new_moments(first, second, grad_rows):
    new_first = 0.9 * first + 0.1 * grad_rows
    new_second = 0.999 * second + 0.001 * grad_rows * grad_rows
    return new_first, new_second


def settle_kernel(piece_of, row_of, held, *refs, pieces):
    count = sum(pieces)
    first_ref, second_ref, first_out, second_out, rows, sem = refs[count:]
    m = pl.program_id(0)
    half = pl.num_programs(0) // 2
    sources = []
    for i, parts in enumerate(pieces):
        at = sum(pieces[:i])
        if parts == 1:
            sources.append((i, refs[at], None, 0))
        else:
            sources += [(i, refs[at], m < half, 0), (i, refs[at + 1], m >= half, half)]
    capacity, bucket_rows = rows.shape[0], rows.shape[1]

    def fetch(s, _):
        piece = piece_of[m, s]
        at = pl.multiple_of(row_of[m, s], bucket_rows)
        for i, ref, mine, base in sources:

            @pl.when(piece == i if mine is None else jnp.logical_and(piece == i, mine))
            def _():
                source = ref.at[m - base, pl.ds(at, bucket_rows), :]
                pltpu.make_async_copy(source, rows.at[s], sem).start()

        return 0

    lax.fori_loop(0, capacity, fetch, 0)
    pltpu.make_async_copy(rows, rows, sem).wait()

    def settle(s, _):
        first, second = first_ref[0, 0, s], second_ref[0, 0, s]
        new_first, new_second = new_moments(first, second, rows[s].astype(F32))
        keep = held[m, s] > 0
        first_out[0, 0, s] = jnp.where(keep, new_first, first)
        second_out[0, 0, s] = jnp.where(keep, new_second, second)
        return 0

    lax.fori_loop(0, capacity, settle, 0)


def settle_moments(first, second, pieces, piece_of, row_of, held):
    mats, _, capacity, bucket_rows, rank = first.shape
    spec = pl.BlockSpec((1, 1, capacity, bucket_rows, rank), lambda m, *_: (m, 0, 0, 0, 0))
    return pl.pallas_call(
        functools.partial(settle_kernel, pieces=tuple(len(p) for p in pieces)),
        out_shape=(
            jax.ShapeDtypeStruct(first.shape, F32),
            jax.ShapeDtypeStruct(second.shape, F32),
        ),
        grid_spec=pltpu.PrefetchScalarGridSpec(
            num_scalar_prefetch=3,
            grid=(mats,),
            in_specs=[pl.BlockSpec(memory_space=pl.ANY)] * sum(len(p) for p in pieces) + [spec, spec],
            out_specs=(spec, spec),
            scratch_shapes=[
                pltpu.VMEM((capacity, bucket_rows, rank), BF16),
                pltpu.SemaphoreType.DMA,
            ],
        ),
        cost_estimate=pl.CostEstimate(
            flops=8 * first.size, bytes_accessed=18 * first.size, transcendentals=0
        ),
        name="settle",
    )(piece_of, row_of, held, *(v for p in pieces for v in p), first, second)


def adam_update(first, second, grad_rows):
    new_first, new_second = new_moments(first, second, grad_rows)
    scaled = (
        6.0 * (new_first / (1.0 - 0.9**10)) / (jnp.sqrt(new_second / (1.0 - 0.999**10)) + 1e-08)
    )
    return scaled.astype(BF16)


def shards(grads, raw_proj, bucket_owner, first_moment, second_moment):
    mats, local_rows = grads.shape[1], grads.shape[2]
    local_feats, rank = raw_proj.shape[1], raw_proj.shape[2]
    buckets = bucket_owner.shape[1]
    capacity = first_moment.shape[2]
    bucket_rows = local_rows // buckets
    replicas = lax.axis_size("dp")
    splits = lax.axis_size("fsdp")
    depth = replicas // QUAD
    unit_rows = local_rows // replicas
    unit_buckets = buckets // replicas
    me = lax.axis_index("dp")
    my_z, my_quad = me // QUAD, me % QUAD

    def permute(v, target):
        return lax.ppermute(v, "dp", [(i, target(i)) for i in range(replicas)])

    def to_core(v):
        return permute(v, lambda i: i ^ 1)

    def to_x(v):
        return permute(v, lambda i: i ^ 2)

    def to_z(v, layers=1):
        return permute(v, lambda i: (i + layers * QUAD) % replicas)

    my_core = me % 2
    half = local_feats // 2
    own = lax.dynamic_slice_in_dim(raw_proj, my_core, 1, 0)
    parts = [
        lax.dynamic_slice(raw_proj, (my_core, i * half, 0), (1, half, rank)) for i in range(2)
    ]
    my_f = lax.axis_index("fsdp")
    gram = gram_of([own])
    pieces, offsets, early, fresh = [], [my_f * local_feats], [], []
    for shift in range(1, splits):
        base = ((my_f + splits - shift) % splits) * local_feats
        for i, indices in ((0, early), (1, fresh)):
            fetched = lax.ppermute(
                parts[i], "fsdp", [(j, (j + shift) % splits) for j in range(splits)]
            )
            indices.append(len(pieces))
            pieces.append(fetched)
            offsets.append(base + i * half)
    offsets = jnp.stack(offsets).astype(jnp.int32)
    gram = gram_of([pieces[i] for i in early], gram)

    same = bucket_owner[:, :, None] == bucket_owner[:, None, :]
    order = jnp.arange(buckets, dtype=jnp.int32)
    earlier = order[None, :] < order[:, None]
    ranks = jnp.sum(jnp.logical_and(same, earlier).astype(jnp.int32), axis=-1)
    owner_ids = jnp.stack([me ^ flip for flip in (0, 2, 1, 3)])
    local_slot = jnp.where(bucket_owner[None] == owner_ids[:, None, None], ranks[None], -1)
    slot_ids = jnp.arange(capacity, dtype=jnp.int32)
    matches = local_slot[:, :, None, :] == slot_ids[None, None, :, None]
    quad_occupied = jnp.any(matches, axis=3)
    quad_buckets = jnp.sum(jnp.where(matches, order[None, None, None, :], 0), axis=3)
    quad_counts = jnp.sum(quad_occupied.astype(jnp.int32), axis=2)
    occupied, bucket_of = quad_occupied[0], quad_buckets[0]
    quad_units = quad_buckets // unit_buckets
    steps = (quad_units // QUAD + depth - my_z) % depth
    places = steps * unit_rows + (quad_buckets % unit_buckets) * bucket_rows
    wanted = jnp.logical_and(quad_occupied, quad_units % QUAD == my_quad)
    places = jnp.where(wanted, places, -1).astype(jnp.int32)

    def unit_moments(moment):
        slots = moment[:, 0].astype(BF16)
        across = to_x(slots)
        owners = (slots, across, to_core(slots), to_core(across))
        groups = collect_moments(owners, places, quad_counts, depth, unit_rows)
        total = groups[0]
        for k in range(1, depth):
            total = total + to_z(groups[k], k)
        return total

    first_unit, second_unit = unit_moments(first_moment), unit_moments(second_moment)
    first_unit, second_unit = lax.optimization_barrier((first_unit, second_unit))

    state = first_half([pieces[i] for i in fresh], gram)
    basis = second_half(own, pieces, offsets, state, splits * local_feats)
    bases = (basis, to_core(basis))

    send_quads = jnp.stack([my_quad ^ flip for flip in (3, 1, 2, 0)]).astype(jnp.int32)
    held = None
    for k in range(1, depth + 1):
        where = jnp.stack([(my_z + depth - k) % depth, my_core]).astype(jnp.int32)
        other, own = project(grads, bases, send_quads, where, unit_rows)
        arrived = to_core(other)
        send = (own[0].astype(F32) + arrived[0].astype(F32)).astype(BF16)
        crossed = to_x(send)
        total = own[1].astype(F32) + arrived[1].astype(F32) + crossed.astype(F32)
        if held is not None:
            total = total + to_z(held).astype(F32)
        held = total.astype(BF16)
    held, grad_rows = lax.optimization_barrier((held, total))

    def ring(unit):
        groups = []
        across = (None,)
        half = mats // 2
        for k in range(depth):
            if 0 < k == depth - 1:
                over_z = to_z(across[0][half:])
                across = (to_x(unit[:half]), over_z)
            else:
                across = (to_x(unit),)
            core = to_core(unit)
            both = tuple(to_core(v) for v in across)
            groups.append(((unit,), across, (core,), both))
            if k + 1 < depth:
                unit = to_z(unit)
        return groups

    grad_groups = ring(held)
    update = adam_update(first_unit.astype(F32), second_unit.astype(F32), grad_rows)
    update_groups = ring(update)

    part_quads = jnp.stack([my_quad ^ flip for flip in (0, 2, 1, 3)]).astype(jnp.int32)
    weight_delta = None
    for k, parts in enumerate(update_groups):
        where = jnp.stack([(my_z + depth - k) % depth, my_core]).astype(jnp.int32)
        weight_delta = expand(
            parts, bases, part_quads, where, weight_delta, mats, local_rows
        )

    unit = bucket_of // unit_buckets
    back = (my_z + depth - unit // QUAD) % depth
    flip = (unit % QUAD) ^ my_quad
    piece_of = back * QUAD + (flip % 2) * 2 + flip // 2
    row_of = (bucket_of % unit_buckets) * bucket_rows
    first_out, second_out = settle_moments(
        first_moment,
        second_moment,
        [p for parts in grad_groups for p in parts],
        piece_of.astype(jnp.int32),
        row_of.astype(jnp.int32),
        occupied.astype(jnp.int32),
    )
    return weight_delta, first_out, second_out


def solution(mesh):
    return jax.shard_map(
        shards,
        mesh=mesh,
        in_specs=(
            P("dp", None, "fsdp", None),
            P(None, "fsdp", None),
            P(None, "fsdp"),
            P(None, "fsdp", "dp", None, None),
            P(None, "fsdp", "dp", None, None),
        ),
        out_specs=(
            P(None, "fsdp", None),
            P(None, "fsdp", "dp", None, None),
            P(None, "fsdp", "dp", None, None),
        ),
        check_vma=False,
    )
```

```python
import functools

import jax
import jax.numpy as jnp
from jax import lax
from jax.experimental import pallas as pl
from jax.experimental.pallas import tpu as pltpu
from jax.sharding import PartitionSpec as P


PANEL = 8
BLOCK = 128
WIDE = 256
QUAD = 4
F32 = jnp.float32
BF16 = jnp.bfloat16


def dot_f32(a, b, dims):
    return lax.dot_general(
        a, b, (dims, ((), ())), precision=lax.Precision.HIGHEST, preferred_element_type=F32
    )


def dot_bf16(a, b, dims):
    return lax.dot_general(a, b, (dims, ((), ())), preferred_element_type=F32)


def halves(x):
    high = x.astype(BF16)
    return high, (x - high.astype(F32)).astype(BF16)


def dot_split(a, b, dims):
    (a_high, a_low), (b_high, b_low) = halves(a), halves(b)
    return (
        dot_bf16(a_low, b_high, dims)
        + dot_bf16(a_high, b_low, dims)
        + dot_bf16(a_high, b_high, dims)
    )


def thirds(x):
    first = x.astype(BF16).astype(F32)
    rest = x - first
    second = rest.astype(BF16).astype(F32)
    return first, second, rest - second


def dot_packed(a, b, dims):
    a1, a2, a3 = thirds(a)
    b1, b2, b3 = thirds(b)
    (a_dim,), (b_dim,) = dims
    left = jnp.concatenate([a1, a2, a1, a3, a2, a1], axis=a_dim).astype(BF16)
    right = jnp.concatenate([b3, b2, b2, b1, b1, b1], axis=b_dim).astype(BF16)
    return dot_bf16(left, right, dims)


def eliminate_panel(block_ref, inverse_ref, scale_ref, m, start):
    rows = block_ref[m, pl.ds(start, PANEL), :]
    inv_rows = inverse_ref[m, pl.ds(start, PANEL), :]
    sub = lax.broadcasted_iota(jnp.int32, rows.shape, 0)
    cols = [
        jnp.take_along_axis(
            rows, jnp.full(rows.shape, start + j, jnp.int32), axis=1, mode="promise_in_bounds"
        )
        for j in range(PANEL)
    ]
    recip = jnp.zeros_like(rows)
    for j in range(PANEL):
        r = 1.0 / jnp.broadcast_to(cols[j][j : j + 1, :], rows.shape)
        recip = jnp.where(sub == j, r, recip)
        if j + 1 < PANEL:
            mult = jnp.where(sub > j, cols[j] * r, 0.0)
            for k in range(j + 1, PANEL):
                cols[k] = cols[k] - mult * jnp.broadcast_to(cols[k][j : j + 1, :], rows.shape)
            rows = rows - mult * jnp.broadcast_to(rows[j : j + 1, :], rows.shape)
            inv_rows = inv_rows - mult * jnp.broadcast_to(inv_rows[j : j + 1, :], rows.shape)
    inverse_ref[m, pl.ds(start, PANEL), :] = inv_rows
    scale_ref[m, pl.ds(start, PANEL), :] = recip
    return rows, inv_rows, recip


def eliminate_block(block_ref, inverse_ref, scale_ref, mats, size):
    row_id = lax.broadcasted_iota(jnp.int32, (size, size), 0)
    lane_id = lax.broadcasted_iota(jnp.int32, (size, size), 1)
    for m in range(mats):
        inverse_ref[m] = jnp.where(row_id == lane_id, 1.0, 0.0)

    def panel(p, _):
        start = pl.multiple_of(p * PANEL, PANEL)
        done = [eliminate_panel(block_ref, inverse_ref, scale_ref, m, start) for m in range(mats)]
        below = row_id >= start + PANEL
        for m in range(mats):
            rows, inv_rows, recip = done[m]
            both = jnp.concatenate([rows, inv_rows], axis=1)
            change = dot_packed(rows * recip, both, ((0,), (0,)))
            block_ref[m] = block_ref[m] - jnp.where(below, change[:, :size], 0.0)
            inverse_ref[m] = inverse_ref[m] - jnp.where(below, change[:, size:], 0.0)
        return 0

    lax.fori_loop(0, size // PANEL, panel, 0)


def add_gram(gram, pieces, held):
    mats, rank, _ = gram.shape

    def one(m, _):
        for j in range(0, rank, WIDE):
            total = None if held is None else held[m, j:, j : j + WIDE]
            for ref in pieces:
                part = dot_f32(ref[m, :, j:], ref[m, :, j : j + WIDE], ((0,), (0,)))
                total = part if total is None else total + part
            gram[m, j:, j : j + WIDE] = total
        return 0

    lax.fori_loop(0, mats, one, 0)


def gram_kernel(*refs, pieces):
    held = refs[pieces] if len(refs) > pieces + 1 else None
    add_gram(refs[-1], refs[:pieces], held)


def gram_of(pieces, held=None):
    mats, _, rank = pieces[0].shape
    args = list(pieces) + ([] if held is None else [held])
    depth = sum(p.shape[1] for p in pieces)
    vmem = pl.BlockSpec(memory_space=pltpu.VMEM)
    return pl.pallas_call(
        functools.partial(gram_kernel, pieces=len(pieces)),
        out_shape=jax.ShapeDtypeStruct((mats, rank, rank), F32),
        in_specs=[vmem] * len(args),
        out_specs=vmem,
        cost_estimate=pl.CostEstimate(
            flops=12 * mats * depth * rank * rank,
            bytes_accessed=4 * mats * rank * (rank + depth),
            transcendentals=0,
        ),
        name="gram",
    )(*args)


def factor(gram, inv, low, block, binv, scale, size):
    mats = block.shape[0]
    n = size // BLOCK

    def sl(i):
        return slice(i * BLOCK, (i + 1) * BLOCK)

    for b in range(n):
        below = (b + 1) * BLOCK
        for m in range(mats):
            block[m] = gram[m, sl(b), sl(b)]
        eliminate_block(block, binv, scale, mats, BLOCK)
        for m in range(mats):
            d_inv = binv[m] * jnp.sqrt(scale[m])
            inv[m, sl(b), sl(b)] = d_inv
            if b > 0:
                acc = dot_packed(
                    low[m, sl(b), : b * BLOCK], inv[m, : b * BLOCK, : b * BLOCK], ((1,), (0,))
                )
                inv[m, sl(b), : b * BLOCK] = -dot_packed(d_inv, acc, ((1,), (0,)))
            if b + 1 < n:
                low[m, below:size, sl(b)] = dot_packed(gram[m, below:size, sl(b)], d_inv, ((1,), (1,)))
                inv[m, sl(b), below:size] = jnp.zeros((BLOCK, size - below), F32)
                for j in range(b + 1, n):
                    gram[m, j * BLOCK : size, sl(j)] = gram[m, j * BLOCK : size, sl(j)] - dot_packed(
                        low[m, j * BLOCK : size, sl(b)], low[m, sl(j), sl(b)], ((1,), (1,))
                    )


def first_half_kernel(*refs, pieces):
    held, inv_out, low_out, rest_out, gram, low, block, binv, scale = refs[pieces:]
    mats, rank, _ = gram.shape
    half = rank // 2
    add_gram(gram, refs[:pieces], held)
    factor(gram, inv_out, low, block, binv, scale, half)
    for m in range(mats):
        side = dot_f32(gram[m, half:, :half], inv_out[m], ((1,), (1,)))
        low_out[m] = side
        rest_out[m] = gram[m, half:, half:] - dot_f32(side, side, ((1,), (1,)))


def second_half_kernel(offsets, *refs, pieces):
    own_ref = refs[0]
    piece_refs = refs[1 : 1 + pieces]
    inv_ref, side_ref, rest_ref, basis_ref = refs[1 + pieces : 5 + pieces]
    raw, gram, inv, low, block, binv, scale = refs[5 + pieces :]
    mats, _, rank = raw.shape
    half = rank // 2
    for i, ref in enumerate((own_ref, *piece_refs)):
        at = pl.multiple_of(offsets[i], 8)
        raw[:, pl.ds(at, ref.shape[1]), :] = ref[...]
    gram[...] = rest_ref[...]
    factor(gram, inv, low, block, binv, scale, half)

    def bases(m, _):
        acc = dot_f32(side_ref[m], inv_ref[m], ((1,), (0,)))
        left = -dot_f32(inv[m], acc, ((1,), (0,)))
        basis_ref[m, :, :half] = dot_split(raw[m, :, :half], inv_ref[m], ((1,), (1,))).astype(BF16)
        both = jnp.concatenate([left, inv[m]], axis=1)
        basis_ref[m, :, half:] = dot_split(raw[m], both, ((1,), (1,))).astype(BF16)
        return 0

    lax.fori_loop(0, mats, bases, 0)


def first_half(fresh, held):
    mats, rank, _ = held.shape
    half = rank // 2
    vmem = pl.BlockSpec(memory_space=pltpu.VMEM)
    state = jax.ShapeDtypeStruct((mats, half, half), F32)
    return pl.pallas_call(
        functools.partial(first_half_kernel, pieces=len(fresh)),
        out_shape=(state,) * 3,
        in_specs=[vmem] * (len(fresh) + 1),
        out_specs=(vmem,) * 3,
        scratch_shapes=[
            pltpu.VMEM((mats, rank, rank), F32),
            pltpu.VMEM((mats, half, half), F32),
        ]
        + [pltpu.VMEM((mats, BLOCK, BLOCK), F32)] * 3,
        cost_estimate=pl.CostEstimate(
            flops=20_000_000_000, bytes_accessed=4 * mats * rank * rank, transcendentals=0
        ),
        name="first_half",
    )(*fresh, held)


def second_half(own, pieces, offsets, state, feats):
    mats, _, rank = own.shape
    half = rank // 2
    vmem = pl.BlockSpec(memory_space=pltpu.VMEM)
    smem = pl.BlockSpec(memory_space=pltpu.SMEM)
    return pl.pallas_call(
        functools.partial(second_half_kernel, pieces=len(pieces)),
        out_shape=jax.ShapeDtypeStruct((mats, feats, rank), BF16),
        in_specs=[smem] + [vmem] * (4 + len(pieces)),
        out_specs=vmem,
        scratch_shapes=[pltpu.VMEM((mats, feats, rank), F32)]
        + [pltpu.VMEM((mats, half, half), F32)] * 3
        + [pltpu.VMEM((mats, BLOCK, BLOCK), F32)] * 3,
        cost_estimate=pl.CostEstimate(
            flops=20_000_000_000, bytes_accessed=6 * mats * feats * rank, transcendentals=0
        ),
        name="second_half",
    )(offsets, own, *pieces, *state)


def collect_kernel(places, counts, *refs):
    m = pl.program_id(0)
    owner_refs, group_refs = refs[:QUAD], refs[QUAD:]
    bucket_rows, unit_rows = owner_refs[0].shape[2], group_refs[0].shape[1]
    for ref in group_refs:
        ref[...] = jnp.zeros(ref.shape, BF16)
    for i, owner_ref in enumerate(owner_refs):

        def pick(s, _):
            place = places[i, m, s]

            @pl.when(place >= 0)
            def _():
                group = place // unit_rows
                at = pl.multiple_of(place - group * unit_rows, bucket_rows)
                for k, ref in enumerate(group_refs):

                    @pl.when(group == k)
                    def _():
                        ref[0, pl.ds(at, bucket_rows), :] = owner_ref[0, s]

            return 0

        lax.fori_loop(0, counts[i, m], pick, 0)


def collect_moments(owners, places, counts, depth, unit_rows):
    mats, capacity, bucket_rows, rank = owners[0].shape
    slots = pl.BlockSpec((1, capacity, bucket_rows, rank), lambda m, *_: (m, 0, 0, 0))
    group = pl.BlockSpec((1, unit_rows, rank), lambda m, *_: (m, 0, 0))
    return pl.pallas_call(
        collect_kernel,
        out_shape=(jax.ShapeDtypeStruct((mats, unit_rows, rank), BF16),) * depth,
        grid_spec=pltpu.PrefetchScalarGridSpec(
            num_scalar_prefetch=2,
            grid=(mats,),
            in_specs=[slots] * QUAD,
            out_specs=(group,) * depth,
        ),
        cost_estimate=pl.CostEstimate(
            flops=0, bytes_accessed=4 * QUAD * owners[0].size, transcendentals=0
        ),
        name="collect",
    )(places, counts, *owners)


def project_kernel(quads, where, grads_ref, own_basis, core_basis, other_ref, own_ref, result):
    unit_rows = other_ref.shape[2]
    for g, basis_ref in enumerate((own_basis, core_basis)):

        @pl.when(pl.program_id(0) == g)
        def _():
            result[...] = dot_bf16(grads_ref[0, 0], basis_ref[0], ((1,), (0,))).astype(BF16)

    for i, ref in ((0, other_ref), (1, other_ref), (2, own_ref), (3, own_ref)):
        at = pl.multiple_of(quads[i] * unit_rows, unit_rows)
        ref[i % 2, 0] = result[pl.ds(at, unit_rows), :]


def project(grads, bases, quads, where, unit_rows):
    _, mats, _, feats = grads.shape
    rank = bases[0].shape[2]
    rows = QUAD * unit_rows
    out = jax.ShapeDtypeStruct((2, mats, unit_rows, rank), BF16)
    out_spec = pl.BlockSpec((2, 1, unit_rows, rank), lambda g, q, w: (0, g ^ w[1], 0, 0))
    basis_spec = pl.BlockSpec((1, feats, rank), lambda g, q, w: (0, 0, 0))
    return pl.pallas_call(
        project_kernel,
        out_shape=(out, out),
        grid_spec=pltpu.PrefetchScalarGridSpec(
            num_scalar_prefetch=2,
            grid=(mats,),
            in_specs=[
                pl.BlockSpec((1, 1, rows, feats), lambda g, q, w: (0, g ^ w[1], w[0], 0)),
                basis_spec,
                basis_spec,
            ],
            out_specs=(out_spec, out_spec),
            scratch_shapes=[pltpu.VMEM((rows, rank), BF16)],
        ),
        cost_estimate=pl.CostEstimate(
            flops=2 * mats * rows * feats * rank,
            bytes_accessed=2 * mats * rows * (feats + rank),
            transcendentals=0,
        ),
        name="project",
    )(quads, where, grads, *bases)


def expand_kernel(quads, where, *refs, parts):
    out_ref, joined = refs[-2:]
    m = pl.program_id(0) ^ where[1]
    unit_rows = refs[0].shape[1]
    used = 0
    for i in range(QUAD):
        at = pl.multiple_of(quads[i] * unit_rows, unit_rows)
        if parts == QUAD or i % 2 == 0:
            joined[pl.ds(at, unit_rows), :] = refs[used][0]
            used += 1
        else:
            low, high = refs[used], refs[used + 1]
            used += 2
            joined[pl.ds(at, unit_rows), :] = jnp.where(m < pl.num_programs(0) // 2, low[0], high[0])
    for g, basis_ref in enumerate(refs[parts : parts + 2]):

        @pl.when(pl.program_id(0) == g)
        def _():
            out_ref[0] = dot_bf16(joined[...], basis_ref[0], ((1,), (1,))).astype(BF16)


def expand(parts, bases, quads, where, target, mats, local_rows):
    _, feats, rank = bases[0].shape
    unit_rows = parts[0][0].shape[1]
    rows = QUAD * unit_rows
    block = (1, unit_rows, rank)
    half = mats // 2
    in_specs, args = [], [quads, where]
    for part in parts:
        if len(part) == 1:
            in_specs.append(pl.BlockSpec(block, lambda g, q, w: (g ^ w[1], 0, 0)))
        else:
            in_specs.append(pl.BlockSpec(block, lambda g, q, w: (jnp.minimum(g ^ w[1], half - 1), 0, 0)))
            in_specs.append(pl.BlockSpec(block, lambda g, q, w: (jnp.maximum((g ^ w[1]) - half, 0), 0, 0)))
        args += part
    pieces = len(in_specs)
    in_specs += [pl.BlockSpec((1, feats, rank), lambda g, q, w: (0, 0, 0))] * 2
    args += bases
    aliases = {}
    if target is not None:
        in_specs.append(pl.BlockSpec(memory_space=pl.ANY))
        aliases = {len(args): 0}
        args.append(target)
    return pl.pallas_call(
        functools.partial(expand_kernel, parts=pieces),
        out_shape=jax.ShapeDtypeStruct((mats, local_rows, feats), BF16),
        grid_spec=pltpu.PrefetchScalarGridSpec(
            num_scalar_prefetch=2,
            grid=(mats,),
            in_specs=in_specs,
            out_specs=pl.BlockSpec((1, rows, feats), lambda g, q, w: (g ^ w[1], w[0], 0)),
            scratch_shapes=[pltpu.VMEM((rows, rank), BF16)],
        ),
        input_output_aliases=aliases,
        cost_estimate=pl.CostEstimate(
            flops=2 * mats * rows * feats * rank,
            bytes_accessed=2 * mats * rows * (feats + rank),
            transcendentals=0,
        ),
        name="expand",
    )(*args)


def new_moments(first, second, grad_rows):
    new_first = 0.9 * first + 0.1 * grad_rows
    new_second = 0.999 * second + 0.001 * grad_rows * grad_rows
    return new_first, new_second


def settle_kernel(piece_of, row_of, held, *refs, pieces):
    count = sum(pieces)
    first_ref, second_ref, first_out, second_out, rows, sem = refs[count:]
    m = pl.program_id(0)
    half = pl.num_programs(0) // 2
    sources = []
    for i, parts in enumerate(pieces):
        at = sum(pieces[:i])
        if parts == 1:
            sources.append((i, refs[at], None, 0))
        else:
            sources += [(i, refs[at], m < half, 0), (i, refs[at + 1], m >= half, half)]
    capacity, bucket_rows = rows.shape[0], rows.shape[1]

    def fetch(s, _):
        piece = piece_of[m, s]
        at = pl.multiple_of(row_of[m, s], bucket_rows)
        for i, ref, mine, base in sources:

            @pl.when(piece == i if mine is None else jnp.logical_and(piece == i, mine))
            def _():
                source = ref.at[m - base, pl.ds(at, bucket_rows), :]
                pltpu.make_async_copy(source, rows.at[s], sem).start()

        return 0

    lax.fori_loop(0, capacity, fetch, 0)
    pltpu.make_async_copy(rows, rows, sem).wait()

    def settle(s, _):
        first, second = first_ref[0, 0, s], second_ref[0, 0, s]
        new_first, new_second = new_moments(first, second, rows[s].astype(F32))
        keep = held[m, s] > 0
        first_out[0, 0, s] = jnp.where(keep, new_first, first)
        second_out[0, 0, s] = jnp.where(keep, new_second, second)
        return 0

    lax.fori_loop(0, capacity, settle, 0)


def settle_moments(first, second, pieces, piece_of, row_of, held):
    mats, _, capacity, bucket_rows, rank = first.shape
    spec = pl.BlockSpec((1, 1, capacity, bucket_rows, rank), lambda m, *_: (m, 0, 0, 0, 0))
    return pl.pallas_call(
        functools.partial(settle_kernel, pieces=tuple(len(p) for p in pieces)),
        out_shape=(
            jax.ShapeDtypeStruct(first.shape, F32),
            jax.ShapeDtypeStruct(second.shape, F32),
        ),
        grid_spec=pltpu.PrefetchScalarGridSpec(
            num_scalar_prefetch=3,
            grid=(mats,),
            in_specs=[pl.BlockSpec(memory_space=pl.ANY)] * sum(len(p) for p in pieces) + [spec, spec],
            out_specs=(spec, spec),
            scratch_shapes=[
                pltpu.VMEM((capacity, bucket_rows, rank), BF16),
                pltpu.SemaphoreType.DMA,
            ],
        ),
        cost_estimate=pl.CostEstimate(
            flops=8 * first.size, bytes_accessed=18 * first.size, transcendentals=0
        ),
        name="settle",
    )(piece_of, row_of, held, *(v for p in pieces for v in p), first, second)


def adam_update(first, second, grad_rows):
    new_first, new_second = new_moments(first, second, grad_rows)
    scaled = (
        6.0 * (new_first / (1.0 - 0.9**10)) / (jnp.sqrt(new_second / (1.0 - 0.999**10)) + 1e-08)
    )
    return scaled.astype(BF16)


def shards(grads, raw_proj, bucket_owner, first_moment, second_moment):
    mats, local_rows = grads.shape[1], grads.shape[2]
    local_feats, rank = raw_proj.shape[1], raw_proj.shape[2]
    buckets = bucket_owner.shape[1]
    capacity = first_moment.shape[2]
    bucket_rows = local_rows // buckets
    replicas = lax.axis_size("dp")
    splits = lax.axis_size("fsdp")
    depth = replicas // QUAD
    unit_rows = local_rows // replicas
    unit_buckets = buckets // replicas
    me = lax.axis_index("dp")
    my_z, my_quad = me // QUAD, me % QUAD

    def permute(v, target):
        return lax.ppermute(v, "dp", [(i, target(i)) for i in range(replicas)])

    def to_core(v):
        return permute(v, lambda i: i ^ 1)

    def to_x(v):
        return permute(v, lambda i: i ^ 2)

    def to_z(v, layers=1):
        return permute(v, lambda i: (i + layers * QUAD) % replicas)

    my_core = me % 2
    half = local_feats // 2
    own = lax.dynamic_slice_in_dim(raw_proj, my_core, 1, 0)
    parts = (
        lax.dynamic_slice(raw_proj, (my_core, 0, 0), (1, half, rank)),
        lax.optimization_barrier(own)[:, half:],
    )
    my_f = lax.axis_index("fsdp")
    gram = gram_of([own])
    pieces, offsets, early, fresh = [], [my_f * local_feats], [], []
    for shift in range(1, splits):
        base = ((my_f + splits - shift) % splits) * local_feats
        for i, indices in ((0, early), (1, fresh)):
            fetched = lax.ppermute(
                parts[i], "fsdp", [(j, (j + shift) % splits) for j in range(splits)]
            )
            indices.append(len(pieces))
            pieces.append(fetched)
            offsets.append(base + i * half)
    offsets = jnp.stack(offsets).astype(jnp.int32)
    gram = gram_of([pieces[i] for i in early], gram)

    same = bucket_owner[:, :, None] == bucket_owner[:, None, :]
    order = jnp.arange(buckets, dtype=jnp.int32)
    earlier = order[None, :] < order[:, None]
    ranks = jnp.sum(jnp.logical_and(same, earlier).astype(jnp.int32), axis=-1)
    owner_ids = jnp.stack([me ^ flip for flip in (0, 2, 1, 3)])
    local_slot = jnp.where(bucket_owner[None] == owner_ids[:, None, None], ranks[None], -1)
    slot_ids = jnp.arange(capacity, dtype=jnp.int32)
    matches = local_slot[:, :, None, :] == slot_ids[None, None, :, None]
    quad_occupied = jnp.any(matches, axis=3)
    quad_buckets = jnp.sum(jnp.where(matches, order[None, None, None, :], 0), axis=3)
    quad_counts = jnp.sum(quad_occupied.astype(jnp.int32), axis=2)
    occupied, bucket_of = quad_occupied[0], quad_buckets[0]
    quad_units = quad_buckets // unit_buckets
    steps = (quad_units // QUAD + depth - my_z) % depth
    places = steps * unit_rows + (quad_buckets % unit_buckets) * bucket_rows
    wanted = jnp.logical_and(quad_occupied, quad_units % QUAD == my_quad)
    places = jnp.where(wanted, places, -1).astype(jnp.int32)

    def unit_moments(moment):
        slots = moment[:, 0].astype(BF16)
        across = to_x(slots)
        owners = (slots, across, to_core(slots), to_core(across))
        groups = collect_moments(owners, places, quad_counts, depth, unit_rows)
        held = groups[depth - 1]
        for k in range(1, depth):
            held = to_z(held) + groups[depth - 1 - k]
        return held

    first_unit, second_unit = unit_moments(first_moment), unit_moments(second_moment)
    first_unit, second_unit = lax.optimization_barrier((first_unit, second_unit))

    state = first_half([pieces[i] for i in fresh], gram)
    basis = second_half(own, pieces, offsets, state, splits * local_feats)
    bases = (basis, to_core(basis))

    send_quads = jnp.stack([my_quad ^ flip for flip in (3, 1, 2, 0)]).astype(jnp.int32)
    held = None
    for k in range(1, depth + 1):
        where = jnp.stack([(my_z + depth - k) % depth, my_core]).astype(jnp.int32)
        other, own = project(grads, bases, send_quads, where, unit_rows)
        arrived = to_core(other)
        send = (own[0].astype(F32) + arrived[0].astype(F32)).astype(BF16)
        crossed = to_x(send)
        total = own[1].astype(F32) + arrived[1].astype(F32) + crossed.astype(F32)
        if held is not None:
            total = total + to_z(held).astype(F32)
        held = total.astype(BF16)
    held, grad_rows = lax.optimization_barrier((held, total))

    def ring(unit):
        groups = []
        across = (None,)
        half = mats // 2
        for k in range(depth):
            if 0 < k == depth - 1:
                over_z = to_z(across[0][half:])
                across = (to_x(unit[:half]), over_z)
            else:
                across = (to_x(unit),)
            core = to_core(unit)
            both = tuple(to_core(v) for v in across)
            groups.append(((unit,), across, (core,), both))
            if k + 1 < depth:
                unit = to_z(unit)
        return groups

    grad_groups = ring(held)
    update = adam_update(first_unit.astype(F32), second_unit.astype(F32), grad_rows)
    update_groups = ring(update)

    part_quads = jnp.stack([my_quad ^ flip for flip in (0, 2, 1, 3)]).astype(jnp.int32)
    weight_delta = None
    for k, parts in enumerate(update_groups):
        where = jnp.stack([(my_z + depth - k) % depth, my_core]).astype(jnp.int32)
        weight_delta = expand(
            parts, bases, part_quads, where, weight_delta, mats, local_rows
        )

    unit = bucket_of // unit_buckets
    back = (my_z + depth - unit // QUAD) % depth
    flip = (unit % QUAD) ^ my_quad
    piece_of = back * QUAD + (flip % 2) * 2 + flip // 2
    row_of = (bucket_of % unit_buckets) * bucket_rows
    first_out, second_out = settle_moments(
        first_moment,
        second_moment,
        [p for parts in grad_groups for p in parts],
        piece_of.astype(jnp.int32),
        row_of.astype(jnp.int32),
        occupied.astype(jnp.int32),
    )
    return weight_delta, first_out, second_out


def solution(mesh):
    return jax.shard_map(
        shards,
        mesh=mesh,
        in_specs=(
            P("dp", None, "fsdp", None),
            P(None, "fsdp", None),
            P(None, "fsdp"),
            P(None, "fsdp", "dp", None, None),
            P(None, "fsdp", "dp", None, None),
        ),
        out_specs=(
            P(None, "fsdp", None),
            P(None, "fsdp", "dp", None, None),
            P(None, "fsdp", "dp", None, None),
        ),
        check_vma=False,
    )
```

```python
import functools

import jax
import jax.numpy as jnp
from jax import lax
from jax.experimental import pallas as pl
from jax.experimental.pallas import tpu as pltpu
from jax.sharding import PartitionSpec as P


PANEL = 8
BLOCK = 128
WIDE = 256
QUAD = 4
F32 = jnp.float32
BF16 = jnp.bfloat16


def dot_f32(a, b, dims):
    return lax.dot_general(
        a, b, (dims, ((), ())), precision=lax.Precision.HIGHEST, preferred_element_type=F32
    )


def dot_bf16(a, b, dims):
    return lax.dot_general(a, b, (dims, ((), ())), preferred_element_type=F32)


def halves(x):
    high = x.astype(BF16)
    return high, (x - high.astype(F32)).astype(BF16)


def dot_split(a, b, dims):
    (a_high, a_low), (b_high, b_low) = halves(a), halves(b)
    return (
        dot_bf16(a_low, b_high, dims)
        + dot_bf16(a_high, b_low, dims)
        + dot_bf16(a_high, b_high, dims)
    )


def thirds(x):
    first = x.astype(BF16).astype(F32)
    rest = x - first
    second = rest.astype(BF16).astype(F32)
    return first, second, rest - second


def dot_packed(a, b, dims):
    a1, a2, a3 = thirds(a)
    b1, b2, b3 = thirds(b)
    (a_dim,), (b_dim,) = dims
    left = jnp.concatenate([a1, a2, a1, a3, a2, a1], axis=a_dim).astype(BF16)
    right = jnp.concatenate([b3, b2, b2, b1, b1, b1], axis=b_dim).astype(BF16)
    return dot_bf16(left, right, dims)


def eliminate_panel(block_ref, inverse_ref, scale_ref, m, start):
    rows = block_ref[m, pl.ds(start, PANEL), :]
    inv_rows = inverse_ref[m, pl.ds(start, PANEL), :]
    sub = lax.broadcasted_iota(jnp.int32, rows.shape, 0)
    cols = [
        jnp.take_along_axis(
            rows, jnp.full(rows.shape, start + j, jnp.int32), axis=1, mode="promise_in_bounds"
        )
        for j in range(PANEL)
    ]
    recip = jnp.zeros_like(rows)
    for j in range(PANEL):
        r = 1.0 / jnp.broadcast_to(cols[j][j : j + 1, :], rows.shape)
        recip = jnp.where(sub == j, r, recip)
        if j + 1 < PANEL:
            mult = jnp.where(sub > j, cols[j] * r, 0.0)
            for k in range(j + 1, PANEL):
                cols[k] = cols[k] - mult * jnp.broadcast_to(cols[k][j : j + 1, :], rows.shape)
            rows = rows - mult * jnp.broadcast_to(rows[j : j + 1, :], rows.shape)
            inv_rows = inv_rows - mult * jnp.broadcast_to(inv_rows[j : j + 1, :], rows.shape)
    inverse_ref[m, pl.ds(start, PANEL), :] = inv_rows
    scale_ref[m, pl.ds(start, PANEL), :] = recip
    return rows, inv_rows, recip


def eliminate_block(block_ref, inverse_ref, scale_ref, mats, size):
    row_id = lax.broadcasted_iota(jnp.int32, (size, size), 0)
    lane_id = lax.broadcasted_iota(jnp.int32, (size, size), 1)
    for m in range(mats):
        inverse_ref[m] = jnp.where(row_id == lane_id, 1.0, 0.0)

    def panel(p, _):
        start = pl.multiple_of(p * PANEL, PANEL)
        done = [eliminate_panel(block_ref, inverse_ref, scale_ref, m, start) for m in range(mats)]
        below = row_id >= start + PANEL
        for m in range(mats):
            rows, inv_rows, recip = done[m]
            both = jnp.concatenate([rows, inv_rows], axis=1)
            change = dot_packed(rows * recip, both, ((0,), (0,)))
            block_ref[m] = block_ref[m] - jnp.where(below, change[:, :size], 0.0)
            inverse_ref[m] = inverse_ref[m] - jnp.where(below, change[:, size:], 0.0)
        return 0

    lax.fori_loop(0, size // PANEL, panel, 0)


def add_gram(gram, pieces, held):
    mats, rank, _ = gram.shape

    def one(m, _):
        for j in range(0, rank, WIDE):
            total = None if held is None else held[m, j:, j : j + WIDE]
            for ref in pieces:
                part = dot_f32(ref[m, :, j:], ref[m, :, j : j + WIDE], ((0,), (0,)))
                total = part if total is None else total + part
            gram[m, j:, j : j + WIDE] = total
        return 0

    lax.fori_loop(0, mats, one, 0)


def gram_kernel(*refs, pieces):
    held = refs[pieces] if len(refs) > pieces + 1 else None
    add_gram(refs[-1], refs[:pieces], held)


def gram_of(pieces, held=None):
    mats, _, rank = pieces[0].shape
    args = list(pieces) + ([] if held is None else [held])
    depth = sum(p.shape[1] for p in pieces)
    vmem = pl.BlockSpec(memory_space=pltpu.VMEM)
    return pl.pallas_call(
        functools.partial(gram_kernel, pieces=len(pieces)),
        out_shape=jax.ShapeDtypeStruct((mats, rank, rank), F32),
        in_specs=[vmem] * len(args),
        out_specs=vmem,
        cost_estimate=pl.CostEstimate(
            flops=12 * mats * depth * rank * rank,
            bytes_accessed=4 * mats * rank * (rank + depth),
            transcendentals=0,
        ),
        name="gram",
    )(*args)


def factor(gram, inv, low, block, binv, scale, size):
    mats = block.shape[0]
    n = size // BLOCK

    def sl(i):
        return slice(i * BLOCK, (i + 1) * BLOCK)

    for b in range(n):
        below = (b + 1) * BLOCK
        for m in range(mats):
            block[m] = gram[m, sl(b), sl(b)]
        eliminate_block(block, binv, scale, mats, BLOCK)
        for m in range(mats):
            d_inv = binv[m] * jnp.sqrt(scale[m])
            inv[m, sl(b), sl(b)] = d_inv
            if b > 0:
                acc = dot_packed(
                    low[m, sl(b), : b * BLOCK], inv[m, : b * BLOCK, : b * BLOCK], ((1,), (0,))
                )
                inv[m, sl(b), : b * BLOCK] = -dot_packed(d_inv, acc, ((1,), (0,)))
            if b + 1 < n:
                low[m, below:size, sl(b)] = dot_packed(gram[m, below:size, sl(b)], d_inv, ((1,), (1,)))
                inv[m, sl(b), below:size] = jnp.zeros((BLOCK, size - below), F32)
                for j in range(b + 1, n):
                    gram[m, j * BLOCK : size, sl(j)] = gram[m, j * BLOCK : size, sl(j)] - dot_packed(
                        low[m, j * BLOCK : size, sl(b)], low[m, sl(j), sl(b)], ((1,), (1,))
                    )


def first_half_kernel(*refs, pieces):
    held, inv_out, low_out, rest_out, gram, low, block, binv, scale = refs[pieces:]
    mats, rank, _ = gram.shape
    half = rank // 2
    add_gram(gram, refs[:pieces], held)
    factor(gram, inv_out, low, block, binv, scale, half)
    for m in range(mats):
        side = dot_f32(gram[m, half:, :half], inv_out[m], ((1,), (1,)))
        low_out[m] = side
        rest_out[m] = gram[m, half:, half:] - dot_f32(side, side, ((1,), (1,)))


def second_half_kernel(offsets, *refs, pieces):
    own_ref = refs[0]
    piece_refs = refs[1 : 1 + pieces]
    inv_ref, side_ref, rest_ref, basis_ref = refs[1 + pieces : 5 + pieces]
    raw, gram, inv, low, block, binv, scale = refs[5 + pieces :]
    mats, _, rank = raw.shape
    half = rank // 2
    for i, ref in enumerate((own_ref, *piece_refs)):
        at = pl.multiple_of(offsets[i], 8)
        raw[:, pl.ds(at, ref.shape[1]), :] = ref[...]
    gram[...] = rest_ref[...]
    factor(gram, inv, low, block, binv, scale, half)

    def bases(m, _):
        acc = dot_f32(side_ref[m], inv_ref[m], ((1,), (0,)))
        left = -dot_f32(inv[m], acc, ((1,), (0,)))
        basis_ref[m, :, :half] = dot_split(raw[m, :, :half], inv_ref[m], ((1,), (1,))).astype(BF16)
        both = jnp.concatenate([left, inv[m]], axis=1)
        basis_ref[m, :, half:] = dot_split(raw[m], both, ((1,), (1,))).astype(BF16)
        return 0

    lax.fori_loop(0, mats, bases, 0)


def first_half(fresh, held):
    mats, rank, _ = held.shape
    half = rank // 2
    vmem = pl.BlockSpec(memory_space=pltpu.VMEM)
    state = jax.ShapeDtypeStruct((mats, half, half), F32)
    return pl.pallas_call(
        functools.partial(first_half_kernel, pieces=len(fresh)),
        out_shape=(state,) * 3,
        in_specs=[vmem] * (len(fresh) + 1),
        out_specs=(vmem,) * 3,
        scratch_shapes=[
            pltpu.VMEM((mats, rank, rank), F32),
            pltpu.VMEM((mats, half, half), F32),
        ]
        + [pltpu.VMEM((mats, BLOCK, BLOCK), F32)] * 3,
        cost_estimate=pl.CostEstimate(
            flops=20_000_000_000, bytes_accessed=4 * mats * rank * rank, transcendentals=0
        ),
        name="first_half",
    )(*fresh, held)


def second_half(own, pieces, offsets, state, feats):
    mats, _, rank = own.shape
    half = rank // 2
    vmem = pl.BlockSpec(memory_space=pltpu.VMEM)
    smem = pl.BlockSpec(memory_space=pltpu.SMEM)
    return pl.pallas_call(
        functools.partial(second_half_kernel, pieces=len(pieces)),
        out_shape=jax.ShapeDtypeStruct((mats, feats, rank), BF16),
        in_specs=[smem] + [vmem] * (4 + len(pieces)),
        out_specs=vmem,
        scratch_shapes=[pltpu.VMEM((mats, feats, rank), F32)]
        + [pltpu.VMEM((mats, half, half), F32)] * 3
        + [pltpu.VMEM((mats, BLOCK, BLOCK), F32)] * 3,
        cost_estimate=pl.CostEstimate(
            flops=20_000_000_000, bytes_accessed=6 * mats * feats * rank, transcendentals=0
        ),
        name="second_half",
    )(offsets, own, *pieces, *state)


def collect_kernel(places, counts, *refs):
    m = pl.program_id(0)
    owner_refs, group_refs = refs[:QUAD], refs[QUAD:]
    bucket_rows, unit_rows = owner_refs[0].shape[2], group_refs[0].shape[1]
    for ref in group_refs:
        ref[...] = jnp.zeros(ref.shape, BF16)
    for i, owner_ref in enumerate(owner_refs):

        def pick(s, _):
            place = places[i, m, s]

            @pl.when(place >= 0)
            def _():
                group = place // unit_rows
                at = pl.multiple_of(place - group * unit_rows, bucket_rows)
                for k, ref in enumerate(group_refs):

                    @pl.when(group == k)
                    def _():
                        ref[0, pl.ds(at, bucket_rows), :] = owner_ref[0, s]

            return 0

        lax.fori_loop(0, counts[i, m], pick, 0)


def collect_moments(owners, places, counts, depth, unit_rows):
    mats, capacity, bucket_rows, rank = owners[0].shape
    slots = pl.BlockSpec((1, capacity, bucket_rows, rank), lambda m, *_: (m, 0, 0, 0))
    group = pl.BlockSpec((1, unit_rows, rank), lambda m, *_: (m, 0, 0))
    return pl.pallas_call(
        collect_kernel,
        out_shape=(jax.ShapeDtypeStruct((mats, unit_rows, rank), BF16),) * depth,
        grid_spec=pltpu.PrefetchScalarGridSpec(
            num_scalar_prefetch=2,
            grid=(mats,),
            in_specs=[slots] * QUAD,
            out_specs=(group,) * depth,
        ),
        cost_estimate=pl.CostEstimate(
            flops=0, bytes_accessed=4 * QUAD * owners[0].size, transcendentals=0
        ),
        name="collect",
    )(places, counts, *owners)


def project_kernel(quads, where, grads_ref, own_basis, core_basis, other_ref, own_ref, result):
    unit_rows = other_ref.shape[2]
    for g, basis_ref in enumerate((own_basis, core_basis)):

        @pl.when(pl.program_id(0) == g)
        def _():
            result[...] = dot_bf16(grads_ref[0, 0], basis_ref[0], ((1,), (0,))).astype(BF16)

    for i, ref in ((0, other_ref), (1, other_ref), (2, own_ref), (3, own_ref)):
        at = pl.multiple_of(quads[i] * unit_rows, unit_rows)
        ref[i % 2, 0] = result[pl.ds(at, unit_rows), :]


def project(grads, bases, quads, where, unit_rows):
    _, mats, _, feats = grads.shape
    rank = bases[0].shape[2]
    rows = QUAD * unit_rows
    out = jax.ShapeDtypeStruct((2, mats, unit_rows, rank), BF16)
    out_spec = pl.BlockSpec((2, 1, unit_rows, rank), lambda g, q, w: (0, g ^ w[1], 0, 0))
    basis_spec = pl.BlockSpec((1, feats, rank), lambda g, q, w: (0, 0, 0))
    return pl.pallas_call(
        project_kernel,
        out_shape=(out, out),
        grid_spec=pltpu.PrefetchScalarGridSpec(
            num_scalar_prefetch=2,
            grid=(mats,),
            in_specs=[
                pl.BlockSpec((1, 1, rows, feats), lambda g, q, w: (0, g ^ w[1], w[0], 0)),
                basis_spec,
                basis_spec,
            ],
            out_specs=(out_spec, out_spec),
            scratch_shapes=[pltpu.VMEM((rows, rank), BF16)],
        ),
        cost_estimate=pl.CostEstimate(
            flops=2 * mats * rows * feats * rank,
            bytes_accessed=2 * mats * rows * (feats + rank),
            transcendentals=0,
        ),
        name="project",
    )(quads, where, grads, *bases)


def expand_kernel(quads, where, *refs, parts):
    out_ref, joined = refs[-2:]
    m = pl.program_id(0) ^ where[1]
    unit_rows = refs[0].shape[1]
    used = 0
    for i in range(QUAD):
        at = pl.multiple_of(quads[i] * unit_rows, unit_rows)
        if parts == QUAD or i % 2 == 0:
            joined[pl.ds(at, unit_rows), :] = refs[used][0]
            used += 1
        else:
            low, high = refs[used], refs[used + 1]
            used += 2
            joined[pl.ds(at, unit_rows), :] = jnp.where(m < pl.num_programs(0) // 2, low[0], high[0])
    for g, basis_ref in enumerate(refs[parts : parts + 2]):

        @pl.when(pl.program_id(0) == g)
        def _():
            out_ref[0] = dot_bf16(joined[...], basis_ref[0], ((1,), (1,))).astype(BF16)


def expand(parts, bases, quads, where, target, mats, local_rows):
    _, feats, rank = bases[0].shape
    unit_rows = parts[0][0].shape[1]
    rows = QUAD * unit_rows
    block = (1, unit_rows, rank)
    half = mats // 2
    in_specs, args = [], [quads, where]
    for part in parts:
        if len(part) == 1:
            in_specs.append(pl.BlockSpec(block, lambda g, q, w: (g ^ w[1], 0, 0)))
        else:
            in_specs.append(pl.BlockSpec(block, lambda g, q, w: (jnp.minimum(g ^ w[1], half - 1), 0, 0)))
            in_specs.append(pl.BlockSpec(block, lambda g, q, w: (jnp.maximum((g ^ w[1]) - half, 0), 0, 0)))
        args += part
    pieces = len(in_specs)
    in_specs += [pl.BlockSpec((1, feats, rank), lambda g, q, w: (0, 0, 0))] * 2
    args += bases
    aliases = {}
    if target is not None:
        in_specs.append(pl.BlockSpec(memory_space=pl.ANY))
        aliases = {len(args): 0}
        args.append(target)
    return pl.pallas_call(
        functools.partial(expand_kernel, parts=pieces),
        out_shape=jax.ShapeDtypeStruct((mats, local_rows, feats), BF16),
        grid_spec=pltpu.PrefetchScalarGridSpec(
            num_scalar_prefetch=2,
            grid=(mats,),
            in_specs=in_specs,
            out_specs=pl.BlockSpec((1, rows, feats), lambda g, q, w: (g ^ w[1], w[0], 0)),
            scratch_shapes=[pltpu.VMEM((rows, rank), BF16)],
        ),
        input_output_aliases=aliases,
        cost_estimate=pl.CostEstimate(
            flops=2 * mats * rows * feats * rank,
            bytes_accessed=2 * mats * rows * (feats + rank),
            transcendentals=0,
        ),
        name="expand",
    )(*args)


def new_moments(first, second, grad_rows):
    new_first = 0.9 * first + 0.1 * grad_rows
    new_second = 0.999 * second + 0.001 * grad_rows * grad_rows
    return new_first, new_second


def settle_kernel(piece_of, row_of, held, *refs, pieces):
    count = sum(pieces)
    first_ref, second_ref, first_out, second_out, rows, sem = refs[count:]
    m = pl.program_id(0)
    half = pl.num_programs(0) // 2
    sources = []
    for i, parts in enumerate(pieces):
        at = sum(pieces[:i])
        if parts == 1:
            sources.append((i, refs[at], None, 0))
        else:
            sources += [(i, refs[at], m < half, 0), (i, refs[at + 1], m >= half, half)]
    capacity, bucket_rows = rows.shape[0], rows.shape[1]

    def fetch(s, _):
        piece = piece_of[m, s]
        at = pl.multiple_of(row_of[m, s], bucket_rows)
        for i, ref, mine, base in sources:

            @pl.when(piece == i if mine is None else jnp.logical_and(piece == i, mine))
            def _():
                source = ref.at[m - base, pl.ds(at, bucket_rows), :]
                pltpu.make_async_copy(source, rows.at[s], sem).start()

        return 0

    lax.fori_loop(0, capacity, fetch, 0)
    pltpu.make_async_copy(rows, rows, sem).wait()

    def settle(s, _):
        first, second = first_ref[0, 0, s], second_ref[0, 0, s]
        new_first, new_second = new_moments(first, second, rows[s].astype(F32))
        keep = held[m, s] > 0
        first_out[0, 0, s] = jnp.where(keep, new_first, first)
        second_out[0, 0, s] = jnp.where(keep, new_second, second)
        return 0

    lax.fori_loop(0, capacity, settle, 0)


def settle_moments(first, second, pieces, piece_of, row_of, held):
    mats, _, capacity, bucket_rows, rank = first.shape
    spec = pl.BlockSpec((1, 1, capacity, bucket_rows, rank), lambda m, *_: (m, 0, 0, 0, 0))
    return pl.pallas_call(
        functools.partial(settle_kernel, pieces=tuple(len(p) for p in pieces)),
        out_shape=(
            jax.ShapeDtypeStruct(first.shape, F32),
            jax.ShapeDtypeStruct(second.shape, F32),
        ),
        grid_spec=pltpu.PrefetchScalarGridSpec(
            num_scalar_prefetch=3,
            grid=(mats,),
            in_specs=[pl.BlockSpec(memory_space=pl.ANY)] * sum(len(p) for p in pieces) + [spec, spec],
            out_specs=(spec, spec),
            scratch_shapes=[
                pltpu.VMEM((capacity, bucket_rows, rank), BF16),
                pltpu.SemaphoreType.DMA,
            ],
        ),
        cost_estimate=pl.CostEstimate(
            flops=8 * first.size, bytes_accessed=18 * first.size, transcendentals=0
        ),
        name="settle",
    )(piece_of, row_of, held, *(v for p in pieces for v in p), first, second)


def adam_update(first, second, grad_rows):
    new_first, new_second = new_moments(first, second, grad_rows)
    scaled = (
        6.0 * (new_first / (1.0 - 0.9**10)) / (jnp.sqrt(new_second / (1.0 - 0.999**10)) + 1e-08)
    )
    return scaled.astype(BF16)


def shards(grads, raw_proj, bucket_owner, first_moment, second_moment):
    mats, local_rows = grads.shape[1], grads.shape[2]
    local_feats, rank = raw_proj.shape[1], raw_proj.shape[2]
    buckets = bucket_owner.shape[1]
    capacity = first_moment.shape[2]
    bucket_rows = local_rows // buckets
    replicas = lax.axis_size("dp")
    splits = lax.axis_size("fsdp")
    depth = replicas // QUAD
    unit_rows = local_rows // replicas
    unit_buckets = buckets // replicas
    me = lax.axis_index("dp")
    my_z, my_quad = me // QUAD, me % QUAD

    def permute(v, target):
        return lax.ppermute(v, "dp", [(i, target(i)) for i in range(replicas)])

    def to_core(v):
        return permute(v, lambda i: i ^ 1)

    def to_x(v):
        return permute(v, lambda i: i ^ 2)

    def to_z(v, layers=1):
        return permute(v, lambda i: (i + layers * QUAD) % replicas)

    my_core = me % 2
    half = local_feats // 2
    own = lax.dynamic_slice_in_dim(raw_proj, my_core, 1, 0)
    parts = (
        lax.dynamic_slice(raw_proj, (my_core, 0, 0), (1, half, rank)),
        lax.optimization_barrier(own)[:, half:],
    )
    my_f = lax.axis_index("fsdp")
    gram = gram_of([own])
    pieces, offsets, early, fresh = [], [my_f * local_feats], [], []
    for shift in range(1, splits):
        base = ((my_f + splits - shift) % splits) * local_feats
        for i, indices in ((0, early), (1, fresh)):
            fetched = lax.ppermute(
                parts[i], "fsdp", [(j, (j + shift) % splits) for j in range(splits)]
            )
            indices.append(len(pieces))
            pieces.append(fetched)
            offsets.append(base + i * half)
    offsets = jnp.stack(offsets).astype(jnp.int32)
    gram = gram_of([pieces[i] for i in early], gram)

    same = bucket_owner[:, :, None] == bucket_owner[:, None, :]
    order = jnp.arange(buckets, dtype=jnp.int32)
    earlier = order[None, :] < order[:, None]
    ranks = jnp.sum(jnp.logical_and(same, earlier).astype(jnp.int32), axis=-1)
    owner_ids = jnp.stack([me ^ flip for flip in (0, 2, 1, 3)])
    local_slot = jnp.where(bucket_owner[None] == owner_ids[:, None, None], ranks[None], -1)
    slot_ids = jnp.arange(capacity, dtype=jnp.int32)
    matches = local_slot[:, :, None, :] == slot_ids[None, None, :, None]
    quad_occupied = jnp.any(matches, axis=3)
    quad_buckets = jnp.sum(jnp.where(matches, order[None, None, None, :], 0), axis=3)
    quad_counts = jnp.sum(quad_occupied.astype(jnp.int32), axis=2)
    occupied, bucket_of = quad_occupied[0], quad_buckets[0]
    quad_units = quad_buckets // unit_buckets
    steps = (quad_units // QUAD + depth - my_z) % depth
    places = steps * unit_rows + (quad_buckets % unit_buckets) * bucket_rows
    wanted = jnp.logical_and(quad_occupied, quad_units % QUAD == my_quad)
    places = jnp.where(wanted, places, -1).astype(jnp.int32)

    def unit_moments(moment):
        slots = moment[:, 0].astype(BF16)
        across = to_x(slots)
        owners = (slots, across, to_core(slots), to_core(across))
        groups = collect_moments(owners, places, quad_counts, depth, unit_rows)
        total = groups[0]
        for k in range(1, depth):
            total = total + to_z(groups[k], k)
        return total

    first_unit, second_unit = unit_moments(first_moment), unit_moments(second_moment)
    first_unit, second_unit = lax.optimization_barrier((first_unit, second_unit))

    state = first_half([pieces[i] for i in fresh], gram)
    basis = second_half(own, pieces, offsets, state, splits * local_feats)
    bases = (basis, to_core(basis))

    send_quads = jnp.stack([my_quad ^ flip for flip in (3, 1, 2, 0)]).astype(jnp.int32)
    held = None
    for k in range(1, depth + 1):
        where = jnp.stack([(my_z + depth - k) % depth, my_core]).astype(jnp.int32)
        other, own = project(grads, bases, send_quads, where, unit_rows)
        arrived = to_core(other)
        send = (own[0].astype(F32) + arrived[0].astype(F32)).astype(BF16)
        crossed = to_x(send)
        total = own[1].astype(F32) + arrived[1].astype(F32) + crossed.astype(F32)
        if held is not None:
            total = total + to_z(held).astype(F32)
        held = total.astype(BF16)
    held, grad_rows = lax.optimization_barrier((held, total))

    def ring(unit):
        groups = []
        across = (None,)
        half = mats // 2
        for k in range(depth):
            if 0 < k == depth - 1:
                over_z = to_z(across[0][half:])
                across = (to_x(unit[:half]), over_z)
            else:
                across = (to_x(unit),)
            core = to_core(unit)
            both = tuple(to_core(v) for v in across)
            groups.append(((unit,), across, (core,), both))
            if k + 1 < depth:
                unit = to_z(unit)
        return groups

    grad_groups = ring(held)
    update = adam_update(first_unit.astype(F32), second_unit.astype(F32), grad_rows)
    update_groups = ring(update)

    part_quads = jnp.stack([my_quad ^ flip for flip in (0, 2, 1, 3)]).astype(jnp.int32)
    weight_delta = None
    for k, parts in enumerate(update_groups):
        where = jnp.stack([(my_z + depth - k) % depth, my_core]).astype(jnp.int32)
        weight_delta = expand(
            parts, bases, part_quads, where, weight_delta, mats, local_rows
        )

    unit = bucket_of // unit_buckets
    back = (my_z + depth - unit // QUAD) % depth
    flip = (unit % QUAD) ^ my_quad
    piece_of = back * QUAD + (flip % 2) * 2 + flip // 2
    row_of = (bucket_of % unit_buckets) * bucket_rows
    first_out, second_out = settle_moments(
        first_moment,
        second_moment,
        [p for parts in grad_groups for p in parts],
        piece_of.astype(jnp.int32),
        row_of.astype(jnp.int32),
        occupied.astype(jnp.int32),
    )
    return weight_delta, first_out, second_out


def solution(mesh):
    return jax.shard_map(
        shards,
        mesh=mesh,
        in_specs=(
            P("dp", None, "fsdp", None),
            P(None, "fsdp", None),
            P(None, "fsdp"),
            P(None, "fsdp", "dp", None, None),
            P(None, "fsdp", "dp", None, None),
        ),
        out_specs=(
            P(None, "fsdp", None),
            P(None, "fsdp", "dp", None, None),
            P(None, "fsdp", "dp", None, None),
        ),
        check_vma=False,
    )
```
